512 devices in a mesh: req: 128 (over y, z, core), mdl: 4 (over x).
Axes of the slice: x: 4, y: 4, z: 16, core: 2. Of those that a mesh axis runs over, the one named last changes fastest.
Arguments:
- lengths: int32 [512], P('req'), may hold values from 16 to 768, as said below
- assignment: int32 [512], replicated, may hold values from 0 to 511, each once
- query: bfloat16 [512, 4096], P('req', 'mdl'), may hold values from -6 to 6
- key_value_fresh: bfloat16 [2, 512, 1024], P(None, 'req', 'mdl'), may hold values from -4.5 to 4.5
- kv_cache: bfloat16 [2, 131072, 1024], P(None, 'req', 'mdl'), may hold values from -6 to 6, as said below
- hidden_in: bfloat16 [512, 5120], P(None, ('req', 'mdl')), may hold values from -60 to 60
- out_weight: bfloat16 [4096, 5120], P('mdl', 'req'), may hold values from -0.09375 to 0.09375
- norm_gain: float32 [5120], replicated, may hold values from 0.5 to 1.5
- gate_up_weight: bfloat16 [2, 128, 4, 10, 32768], P(None, None, 'mdl', None, 'req'), may hold values from -0.078125 to 0.078125
- down_weight: bfloat16 [32768, 128, 4, 10], P('req', None, 'mdl'), may hold values from -0.125 to 0.125
Outputs:
- layer_out: bfloat16 [512, 5120], P(None, ('req', 'mdl'))
- kv_out: bfloat16 [2, 131072, 1024], P(None, 'req', 'mdl')
The draws below stay inside these ranges and needn't reach their ends.
Inputs may be any that keep to these rules, and one draw needn't show every extreme that they name: `lengths`: each value is from 16 to 48, except in exactly 6 slots, which lie in 6 different blocks of 4 slots and hold exactly 768. `assignment`: each request appears once. `kv_cache`: the cache of block r lies in rows r * 1024 on: its slots in order, slot s taking lengths[s] + 1 rows, of which the first lengths[s] hold its cached tokens and the last is free for the new one; the rows after them belong to no slot.
All inputs are finite; a program needn't handle non-finite values.
Results may differ from the reference program's by a relative error of at most 0.017.
Values may be sent and summed in bfloat16 or wider, within the bound.
No kernel may reach another device: no remote copies, remote signals or barrier semaphores. Data moves between devices by JAX's collectives and lax.ppermute only.
A program may use at most 64 MiB of HBM per device.

```python
import math
import jax
import jax.numpy as jnp
from jax import lax

D = 5120
QUERY_HEADS = 32
KEY_VALUE_HEADS = 8
HEAD_SIZE = 128
FF = 32768
REQUEST_SLOTS = 4
LONG = 768
LONGS = 6
SHORT_MIN = 16
SHORT_MAX = 48
BLOCKS = 128
SUBS = 4
DSUB = 10
REQUEST_COUNT = 512
CACHE_ROWS_EACH = 1024
CACHE_ROWS_ALL = 131072


def length_layout(key):
    short_draw = jax.random.randint(jax.random.fold_in(key, 13), (REQUEST_COUNT,), SHORT_MIN, SHORT_MAX + 1)
    chosen = jax.random.permutation(jax.random.fold_in(key, 11), BLOCKS)[:LONGS]
    slot_pick = jax.random.randint(jax.random.fold_in(key, 12), (LONGS,), 0, REQUEST_SLOTS)
    marks = jnp.zeros((REQUEST_COUNT,), jnp.int32).at[chosen * REQUEST_SLOTS + slot_pick].set(1)
    return jnp.where(marks == 1, LONG, short_draw).astype(jnp.int32)


def draw_lengths(key, part):
    return length_layout(key)


def draw_query(key, part):
    starting_sample = jnp.clip(jax.random.normal(jax.random.fold_in(key, 31), (REQUEST_COUNT, KEY_VALUE_HEADS, QUERY_HEADS // KEY_VALUE_HEADS, HEAD_SIZE), jnp.float32), -4.5, 4.5)
    return starting_sample.reshape(REQUEST_COUNT, QUERY_HEADS * HEAD_SIZE).astype(jnp.bfloat16)


def draw_kv_cache(key, part):
    starting_sample = jnp.clip(jax.random.normal(jax.random.fold_in(key, 41), (2, CACHE_ROWS_ALL, KEY_VALUE_HEADS, HEAD_SIZE), jnp.float32), -4.5, 4.5)
    return starting_sample.reshape(2, CACHE_ROWS_ALL, KEY_VALUE_HEADS * HEAD_SIZE).astype(jnp.bfloat16)


def draw_hidden_in(key, part):
    columns = jnp.arange(D, dtype=jnp.int32)
    sub_position = (columns // DSUB % SUBS).astype(jnp.float32)
    rising = 3.0 ** (sub_position / (SUBS - 1))
    spread = jnp.exp(jax.random.uniform(jax.random.fold_in(key, 51), (D,), jnp.float32, 0.0, math.log(3.3)))
    column_scale = rising * spread / 3.0
    noise = jnp.clip(jax.random.normal(jax.random.fold_in(key, 52), (REQUEST_COUNT, D), jnp.float32), -4.0, 4.0)
    return (noise * column_scale).astype(jnp.bfloat16)


def strengthened(result, own_key, source, target, blocks, factor):
    owner, partner = [(jnp.arange(result.shape[position]) // (result.shape[position] // blocks)).reshape([-1 if axis == position else 1 for axis in range(result.ndim)]) for position in (source, target)]
    chosen = jax.random.permutation(own_key, blocks)[partner]
    strong = (owner == chosen) | (owner == (partner + blocks // 2) % blocks)
    return jnp.where(strong, factor * result, result)


def levels(rng, extent, shards, low, largest):
    def one(dim, parts):
        heights = jax.random.uniform(jax.random.fold_in(jax.random.fold_in(rng, 6), dim), (parts,), jnp.float32, low / len(shards), largest / len(shards))
        return jnp.repeat(jnp.exp(heights), extent[dim] // parts).reshape((-1,) + (1,) * (len(extent) - dim - 1))

    gain = one(*shards[0])
    for cut in shards[1:]:
        gain = gain * one(*cut)
    return gain


def centred(own_key, shape, width, reach, cuts=(), kind=jnp.bfloat16):
    factor_of = levels(own_key, shape, cuts, -0.22, 0.18) if cuts else 1.0
    array = jax.random.normal(own_key, shape, jnp.float32) * width * factor_of
    return jnp.minimum(jnp.maximum(array, -reach), reach).astype(kind)


def bell_draw_with(rng, extent, width, limit, pieces, heavy, kind=jnp.bfloat16):
    array = width * jax.random.normal(rng, extent, jnp.float32)
    if pieces:
        array = array * levels(rng, extent, pieces, -0.22, 0.18)
    return jnp.clip(strengthened(array, jax.random.fold_in(rng, 3), *heavy), -limit, limit).astype(kind)


def setup_inputs(seed: int = 0) -> dict:
    key_of = jax.random.split(jax.random.key(seed), 11)
    return {
        "lengths": draw_lengths(jax.random.fold_in(key_of[10], 71), 0),
        "assignment": jax.random.permutation(key_of[1], REQUEST_COUNT).astype(jnp.int32),
        "query": draw_query(jax.random.fold_in(key_of[10], 71), 0),
        "key_value_fresh": centred(key_of[3], (2, REQUEST_COUNT, KEY_VALUE_HEADS * HEAD_SIZE), 1.0, 4.5, ((1, 128), (2, 4))),
        "kv_cache": draw_kv_cache(jax.random.fold_in(key_of[10], 71), 0),
        "hidden_in": draw_hidden_in(jax.random.fold_in(key_of[10], 71), 0),
        "out_weight": centred(key_of[6], (QUERY_HEADS * HEAD_SIZE, D), (QUERY_HEADS * HEAD_SIZE) ** -0.5, 0.09375, ((0, 4), (1, 128))),
        "norm_gain": jnp.clip(jax.random.uniform(key_of[7], (D,), jnp.float32, 0.5, 1.5), 0.5, 1.5),
        "gate_up_weight": centred(key_of[8], (2, BLOCKS, SUBS, DSUB, FF), D ** -0.5, 0.078125, ((2, 4), (4, 128))),
        "down_weight": bell_draw_with(key_of[9], (FF, BLOCKS, SUBS, DSUB), FF ** -0.5, 0.125, ((0, 128), (2, 4)), (0, 1, 128, 5.5)),
    }


def device_layer(packed):
    slot_lengths, query_per_slot, slot_new, key_value_store = packed
    span_sizes = (slot_lengths + 1).astype(jnp.int32)
    slot_starts = (jnp.cumsum(span_sizes) - span_sizes).astype(jnp.int32)
    for slot_index in range(REQUEST_SLOTS):
        target_row = (slot_starts[slot_index] + slot_lengths[slot_index]).astype(jnp.int32)
        key_value_store = lax.dynamic_update_slice(key_value_store, slot_new[:, slot_index:slot_index + 1, :], (jnp.int32(0), target_row, jnp.int32(0)))
    group_width = QUERY_HEADS // KEY_VALUE_HEADS
    key_row_block = key_value_store[0].reshape(CACHE_ROWS_EACH, KEY_VALUE_HEADS, HEAD_SIZE).astype(jnp.float32)
    value_row_block = key_value_store[1].reshape(CACHE_ROWS_EACH, KEY_VALUE_HEADS, HEAD_SIZE).astype(jnp.float32)
    query_rows = query_per_slot.reshape(REQUEST_SLOTS, KEY_VALUE_HEADS, group_width, HEAD_SIZE).astype(jnp.float32)
    scores = jnp.einsum('sngd,tnd->sngt', query_rows, key_row_block) * HEAD_SIZE ** (-0.5)
    row_ids = jnp.arange(CACHE_ROWS_EACH, dtype=jnp.int32)
    inside = (row_ids[None, :] >= slot_starts[:, None]) & (row_ids[None, :] <= (slot_starts + slot_lengths)[:, None])
    inside = inside[:, None, None, :]
    scores = jnp.where(inside, scores, -1e+30)
    row_max = lax.optimization_barrier(jnp.max(scores, axis=-1, keepdims=True))
    weights = jnp.where(inside, jnp.exp(scores - row_max), 0.0)
    denominator = lax.optimization_barrier(jnp.sum(weights, axis=-1))
    rounded = lax.optimization_barrier(weights.astype(jnp.bfloat16)).astype(jnp.float32)
    mixed = jnp.einsum('sngt,tnd->sngd', rounded, value_row_block)
    attended = (mixed / denominator[..., None]).astype(jnp.bfloat16).reshape(REQUEST_SLOTS, QUERY_HEADS * HEAD_SIZE)
    return (attended, key_value_store)

def reference(lengths, assignment, query, key_value_fresh, kv_cache, hidden_in, out_weight, norm_gain, gate_up_weight, down_weight):
    kv_width = kv_cache.shape[2]
    slot_lengths = lengths.reshape(BLOCKS, REQUEST_SLOTS).astype(jnp.int32)
    query_per_slot = query.reshape(BLOCKS, REQUEST_SLOTS, QUERY_HEADS * HEAD_SIZE)
    slot_new = jnp.transpose(key_value_fresh.reshape(2, BLOCKS, REQUEST_SLOTS, kv_width), (1, 0, 2, 3))
    pools = jnp.transpose(kv_cache.reshape(2, BLOCKS, CACHE_ROWS_EACH, kv_width), (1, 0, 2, 3))
    attended, pools = lax.map(device_layer, (slot_lengths, query_per_slot, slot_new, pools))
    kv_out = jnp.transpose(pools, (1, 0, 2, 3)).reshape(2, CACHE_ROWS_ALL, kv_width)
    attended = attended.reshape(REQUEST_COUNT, QUERY_HEADS * HEAD_SIZE)
    projected = jnp.dot(attended, out_weight, preferred_element_type=jnp.float32)
    placed = jnp.zeros((REQUEST_COUNT, D), jnp.float32).at[assignment].set(projected)
    residual = (hidden_in.astype(jnp.float32) + placed).astype(jnp.bfloat16)
    residual_wide = residual.astype(jnp.float32)
    square_mean = lax.optimization_barrier(jnp.mean(residual_wide * residual_wide, axis=-1, keepdims=True))
    normed = (residual_wide * lax.rsqrt(square_mean + 1e-05) * norm_gain).astype(jnp.bfloat16)
    gate_up = gate_up_weight.reshape(2, D, FF)
    gate = jnp.dot(normed, gate_up[0], preferred_element_type=jnp.float32)
    upward = jnp.dot(normed, gate_up[1], preferred_element_type=jnp.float32)
    hidden = (jax.nn.silu(gate) * upward).astype(jnp.bfloat16)
    lowered = jnp.dot(hidden, down_weight.reshape(FF, D), preferred_element_type=jnp.float32)
    layer_out = (residual_wide + lowered).astype(jnp.bfloat16)
    return (layer_out, kv_out)
```

```python
import jax
import jax.numpy as jnp
from jax import lax
from jax.sharding import Mesh, PartitionSpec as P

D = 5120
QUERY_HEADS = 32
KEY_VALUE_HEADS = 8
HEAD_SIZE = 128


NEGATIVE_FILL = -1e30
REQ = ("y", "z", "c")


def gather_rows(part):
    count = lax.axis_size(REQ)
    copies = jnp.broadcast_to(part[None], (count,) + part.shape)
    return lax.all_to_all(copies, REQ, 0, 0, tiled=True)


def scatter_sum(parts):
    wide = None
    for position, name in ((2, "c"), (1, "z"), (0, "y")):
        moved = lax.all_to_all(parts.astype(jnp.bfloat16), name, position, position, tiled=True)
        wide = moved.astype(jnp.float32).sum(position, keepdims=True)
        parts = wide
    return wide


def mdl_sum(value, wire):
    count = lax.axis_size("mdl")
    sent = value.astype(wire)
    total = value.astype(jnp.float32)
    for shift in range(1, count):
        pairs = [(i, (i + shift) % count) for i in range(count)]
        total = total + lax.ppermute(sent, "mdl", pairs).astype(jnp.float32)
    return total


def mdl_scatter_sum(value, wire):
    count = lax.axis_size("mdl")
    me = lax.axis_index("mdl")
    width = value.shape[-1] // count
    blocks = value.astype(wire).reshape(value.shape[:-1] + (count, width))
    total = lax.dynamic_index_in_dim(blocks, me, blocks.ndim - 2, keepdims=False).astype(jnp.float32)
    for shift in range(1, count):
        pairs = [(i, (i + shift) % count) for i in range(count)]
        outgoing = lax.dynamic_index_in_dim(blocks, (me + shift) % count, blocks.ndim - 2, keepdims=False)
        total = total + lax.ppermute(outgoing, "mdl", pairs).astype(jnp.float32)
    return total


def slot_bounds(lengths):
    span_sizes = lengths + 1
    first_rows = jnp.cumsum(span_sizes) - span_sizes
    return (first_rows, first_rows + span_sizes)


def attend_rows(query_rows, key_value_store, row_base, first_rows, end_rows):
    block_rows = 128
    slot_count, kv_heads, group_width, head_dim = query_rows.shape
    pool_rows = key_value_store.shape[1]
    key_table = key_value_store[0].reshape(pool_rows, kv_heads, head_dim)
    value_table = key_value_store[1].reshape(pool_rows, kv_heads, head_dim)
    needed = jnp.clip(jnp.max(end_rows) - row_base, 0, pool_rows)
    block_count = (needed + block_rows - 1) // block_rows
    score_scale = head_dim ** (-0.5)

    def advance(block_index, carried):
        running_max, denominator, accumulated = carried
        offset = block_index * block_rows
        key_block = lax.dynamic_slice_in_dim(key_table, offset, block_rows, 0)
        value_block = lax.dynamic_slice_in_dim(value_table, offset, block_rows, 0)
        scores = (
            jnp.einsum("sngd,tnd->sngt", query_rows, key_block, preferred_element_type=jnp.float32)
            * score_scale
        )
        row_ids = row_base + offset + jnp.arange(block_rows, dtype=jnp.int32)
        inside = (
            (row_ids[None, :] >= first_rows[:, None]) & (row_ids[None, :] < end_rows[:, None])
        )[:, None, None, :]
        scores = jnp.where(inside, scores, NEGATIVE_FILL)
        new_max = jnp.maximum(running_max, jnp.max(scores, axis=-1))
        weights = jnp.where(inside, jnp.exp(scores - new_max[..., None]), 0.0)
        factor = jnp.exp(running_max - new_max)
        denominator = denominator * factor + jnp.sum(weights, axis=-1)
        accumulated = accumulated * factor[..., None] + jnp.einsum(
            "sngt,tnd->sngd",
            weights.astype(jnp.bfloat16),
            value_block,
            preferred_element_type=jnp.float32,
        )
        return (new_max, denominator, accumulated)

    initial = (
        jnp.full((slot_count, kv_heads, group_width), NEGATIVE_FILL, jnp.float32),
        jnp.zeros((slot_count, kv_heads, group_width), jnp.float32),
        jnp.zeros((slot_count, kv_heads, group_width, head_dim), jnp.float32),
    )
    return lax.fori_loop(0, block_count, advance, initial)


def body(
    lengths,
    assignment,
    query,
    key_value_fresh,
    kv_cache,
    hidden_in,
    out_weight,
    norm_gain,
    gate_up_weight,
    down_weight,
):
    slot_count = lengths.shape[0]
    first_rows, end_rows = slot_bounds(lengths)
    key_value_store = kv_cache
    for slot_index in range(slot_count):
        key_value_store = lax.dynamic_update_slice(
            key_value_store,
            key_value_fresh[:, slot_index : slot_index + 1, :],
            (jnp.int32(0), end_rows[slot_index] - 1, jnp.int32(0)),
        )
    kv_heads = key_value_store.shape[2] // HEAD_SIZE
    group_width = QUERY_HEADS // KEY_VALUE_HEADS
    query_rows = query.reshape(slot_count, kv_heads, group_width, HEAD_SIZE)
    joint_max, denominator, accumulated = attend_rows(
        query_rows, key_value_store, 0, first_rows, end_rows
    )
    attended = (
        (accumulated / denominator[..., None])
        .astype(jnp.bfloat16)
        .reshape(slot_count, kv_heads * group_width * HEAD_SIZE)
    )
    all_attended = gather_rows(attended).reshape(-1, attended.shape[1])
    projected = jnp.dot(all_attended, out_weight, preferred_element_type=jnp.float32)
    head_share = mdl_scatter_sum(projected.astype(jnp.bfloat16), jnp.bfloat16)
    total_rows = assignment.shape[0]
    inverse = (
        jnp.zeros((total_rows,), jnp.int32)
        .at[assignment]
        .set(jnp.arange(total_rows, dtype=jnp.int32))
    )
    placed = jnp.take(head_share, inverse, axis=0)
    residual_wide = hidden_in.astype(jnp.float32) + placed
    residual = residual_wide.astype(jnp.bfloat16)
    local_wide = residual.astype(jnp.float32)
    col_groups = gate_up_weight.shape[1]
    sub_width = hidden_in.shape[1]
    gathered = jnp.transpose(gather_rows(residual), (1, 0, 2)).reshape(total_rows, col_groups * sub_width)
    widened = gathered.astype(jnp.float32)
    square_sum = mdl_sum(jnp.sum(widened * widened, axis=1), jnp.float32)
    gain_table = norm_gain.reshape(col_groups, lax.axis_size("mdl"), sub_width)
    gain_cols = lax.dynamic_index_in_dim(
        gain_table, lax.axis_index("mdl"), 1, keepdims=False
    ).reshape(col_groups * sub_width)
    normed = (widened * lax.rsqrt(square_sum / D + 1e-05)[:, None] * gain_cols).astype(jnp.bfloat16)
    gate_up = gate_up_weight.reshape(2, col_groups * sub_width, gate_up_weight.shape[4])
    partial_value = jnp.einsum("rk,gkf->grf", normed, gate_up, preferred_element_type=jnp.float32)
    gate_sums = mdl_sum(partial_value, jnp.bfloat16)
    hidden = (jax.nn.silu(gate_sums[0]) * gate_sums[1]).astype(jnp.bfloat16)
    columns = down_weight.reshape(down_weight.shape[0], col_groups * sub_width)
    lowered = lax.dot_general(
        columns, hidden, (((0,), (1,)), ((), ())), preferred_element_type=jnp.float32
    )
    mesh_shape = (lax.axis_size("y"), lax.axis_size("z"), lax.axis_size("c"))
    summed = scatter_sum(lowered.reshape(mesh_shape + (sub_width, total_rows))).reshape(sub_width, total_rows)
    layer_out = (local_wide + summed.T).astype(jnp.bfloat16)
    return (layer_out, key_value_store)


def solution(mesh):
    req_size, mdl_size = mesh.devices.shape
    chips_y = 4
    split = Mesh(
        mesh.devices.reshape(chips_y, req_size // (2 * chips_y), 2, mdl_size),
        REQ + ("mdl",),
    )
    return jax.shard_map(
        body,
        mesh=split,
        in_specs=(
            P(REQ),
            P(),
            P(REQ, "mdl"),
            P(None, REQ, "mdl"),
            P(None, REQ, "mdl"),
            P(None, (REQ + ("mdl",))),
            P("mdl", REQ),
            P(),
            P(None, None, "mdl", None, REQ),
            P(REQ, None, "mdl", None),
        ),
        out_specs=(P(None, REQ + ("mdl",)), P(None, REQ, "mdl")),
        check_vma=False,
    )
```

```python
import jax
import jax.numpy as jnp
from jax import lax
from jax.sharding import Mesh, PartitionSpec as P

D = 5120
QUERY_HEADS = 32
KEY_VALUE_HEADS = 8
HEAD_SIZE = 128


NEGATIVE_FILL = -1e30
REQ = ("y", "z", "c")


def gather_rows(part):
    count = lax.axis_size(REQ)
    flat = part.reshape(-1, 128)
    copies = jnp.broadcast_to(flat[None], (count,) + flat.shape)
    return lax.all_to_all(copies, REQ, 0, 0, tiled=True).reshape((count,) + part.shape)


def scatter_sum(parts):
    wide = None
    for position, name in ((2, "c"), (0, "y"), (1, "z")):
        moved = lax.all_to_all(parts.astype(jnp.bfloat16), name, position, position, tiled=True)
        wide = moved.astype(jnp.float32).sum(position, keepdims=True)
        parts = wide
    return wide


def mdl_sum(value, wire):
    count = lax.axis_size("mdl")
    sent = value.astype(wire)
    total = value.astype(jnp.float32)
    for shift in range(1, count):
        pairs = [(i, (i + shift) % count) for i in range(count)]
        total = total + lax.ppermute(sent, "mdl", pairs).astype(jnp.float32)
    return total


def mdl_scatter_sum(value, wire):
    count = lax.axis_size("mdl")
    me = lax.axis_index("mdl")
    height = value.shape[0] // count
    blocks = value.astype(wire).reshape((count, height * value.shape[1] // 128, 128))
    total = lax.dynamic_index_in_dim(blocks, me, 0, keepdims=False).astype(jnp.float32)
    for shift in range(1, count):
        pairs = [(i, (i + shift) % count) for i in range(count)]
        outgoing = lax.dynamic_index_in_dim(blocks, (me + shift) % count, 0, keepdims=False)
        total = total + lax.ppermute(outgoing, "mdl", pairs).astype(jnp.float32)
    return total.reshape(height, value.shape[1])


def slot_bounds(lengths):
    span_sizes = lengths + 1
    first_rows = jnp.cumsum(span_sizes) - span_sizes
    return (first_rows, first_rows + span_sizes)


def attend_rows(query_rows, key_value_store, row_base, first_rows, end_rows):
    block_rows = 128
    slot_count, kv_heads, group_width, head_dim = query_rows.shape
    pool_rows = key_value_store.shape[1]
    key_table = key_value_store[0].reshape(pool_rows, kv_heads, head_dim)
    value_table = key_value_store[1].reshape(pool_rows, kv_heads, head_dim)
    needed = jnp.clip(jnp.max(end_rows) - row_base, 0, pool_rows)
    block_count = (needed + block_rows - 1) // block_rows
    score_scale = head_dim ** (-0.5)

    def advance(block_index, carried):
        running_max, denominator, accumulated = carried
        offset = block_index * block_rows
        key_block = lax.dynamic_slice_in_dim(key_table, offset, block_rows, 0)
        value_block = lax.dynamic_slice_in_dim(value_table, offset, block_rows, 0)
        scores = (
            jnp.einsum("sngd,tnd->sngt", query_rows, key_block, preferred_element_type=jnp.float32)
            * score_scale
        )
        row_ids = row_base + offset + jnp.arange(block_rows, dtype=jnp.int32)
        inside = (
            (row_ids[None, :] >= first_rows[:, None]) & (row_ids[None, :] < end_rows[:, None])
        )[:, None, None, :]
        scores = jnp.where(inside, scores, NEGATIVE_FILL)
        new_max = jnp.maximum(running_max, jnp.max(scores, axis=-1))
        weights = jnp.where(inside, jnp.exp(scores - new_max[..., None]), 0.0)
        factor = jnp.exp(running_max - new_max)
        denominator = denominator * factor + jnp.sum(weights, axis=-1)
        accumulated = accumulated * factor[..., None] + jnp.einsum(
            "sngt,tnd->sngd",
            weights.astype(jnp.bfloat16),
            value_block,
            preferred_element_type=jnp.float32,
        )
        return (new_max, denominator, accumulated)

    initial = (
        jnp.full((slot_count, kv_heads, group_width), NEGATIVE_FILL, jnp.float32),
        jnp.zeros((slot_count, kv_heads, group_width), jnp.float32),
        jnp.zeros((slot_count, kv_heads, group_width, head_dim), jnp.float32),
    )
    return lax.fori_loop(0, block_count, advance, initial)


def body(
    lengths,
    assignment,
    query,
    key_value_fresh,
    kv_cache,
    hidden_in,
    out_weight,
    norm_gain,
    gate_up_weight,
    down_weight,
):
    slot_count = lengths.shape[0]
    first_rows, end_rows = slot_bounds(lengths)
    key_value_store = kv_cache
    for slot_index in range(slot_count):
        key_value_store = lax.dynamic_update_slice(
            key_value_store,
            key_value_fresh[:, slot_index : slot_index + 1, :],
            (jnp.int32(0), end_rows[slot_index] - 1, jnp.int32(0)),
        )
    kv_heads = key_value_store.shape[2] // HEAD_SIZE
    group_width = QUERY_HEADS // KEY_VALUE_HEADS
    query_rows = query.reshape(slot_count, kv_heads, group_width, HEAD_SIZE)
    joint_max, denominator, accumulated = attend_rows(
        query_rows, key_value_store, 0, first_rows, end_rows
    )
    attended = (
        (accumulated / denominator[..., None])
        .astype(jnp.bfloat16)
        .reshape(slot_count, kv_heads * group_width * HEAD_SIZE)
    )
    all_attended = gather_rows(attended).reshape(-1, attended.shape[1])
    projected = jnp.dot(all_attended, out_weight, preferred_element_type=jnp.float32)
    head_share = mdl_scatter_sum(projected.T, jnp.bfloat16).T
    total_rows = assignment.shape[0]
    inverse = (
        jnp.zeros((total_rows,), jnp.int32)
        .at[assignment]
        .set(jnp.arange(total_rows, dtype=jnp.int32))
    )
    placed = jnp.take(head_share, inverse, axis=0)
    residual_wide = hidden_in.astype(jnp.float32) + placed
    residual = residual_wide.astype(jnp.bfloat16)
    local_wide = residual.astype(jnp.float32)
    col_groups = gate_up_weight.shape[1]
    sub_width = hidden_in.shape[1]
    gathered = jnp.transpose(gather_rows(residual.T), (2, 0, 1)).reshape(total_rows, col_groups * sub_width)
    widened = gathered.astype(jnp.float32)
    square_sum = mdl_sum(jnp.sum(widened * widened, axis=1), jnp.float32)
    gain_table = norm_gain.reshape(col_groups, lax.axis_size("mdl"), sub_width)
    gain_cols = lax.dynamic_index_in_dim(
        gain_table, lax.axis_index("mdl"), 1, keepdims=False
    ).reshape(col_groups * sub_width)
    normed = (widened * lax.rsqrt(square_sum / D + 1e-05)[:, None] * gain_cols).astype(jnp.bfloat16)
    gate_up = gate_up_weight.reshape(2, col_groups * sub_width, gate_up_weight.shape[4])
    partial_value = jnp.einsum("rk,gkf->grf", normed, gate_up, preferred_element_type=jnp.float32)
    gate_sums = mdl_sum(partial_value, jnp.bfloat16)
    hidden = (jax.nn.silu(gate_sums[0]) * gate_sums[1]).astype(jnp.bfloat16)
    columns = down_weight.reshape(down_weight.shape[0], col_groups * sub_width)
    lowered = lax.dot_general(
        columns, hidden, (((0,), (1,)), ((), ())), preferred_element_type=jnp.float32
    )
    mesh_shape = (lax.axis_size("y"), lax.axis_size("z"), lax.axis_size("c"))
    summed = scatter_sum(lowered.reshape(mesh_shape + (sub_width * total_rows // 128, 128))).reshape(sub_width, total_rows)
    layer_out = (local_wide + summed.T).astype(jnp.bfloat16)
    return (layer_out, key_value_store)


def solution(mesh):
    req_size, mdl_size = mesh.devices.shape
    chips_y = 4
    split = Mesh(
        mesh.devices.reshape(chips_y, req_size // (2 * chips_y), 2, mdl_size),
        REQ + ("mdl",),
    )
    return jax.shard_map(
        body,
        mesh=split,
        in_specs=(
            P(REQ),
            P(),
            P(REQ, "mdl"),
            P(None, REQ, "mdl"),
            P(None, REQ, "mdl"),
            P(None, (REQ + ("mdl",))),
            P("mdl", REQ),
            P(),
            P(None, None, "mdl", None, REQ),
            P(REQ, None, "mdl", None),
        ),
        out_specs=(P(None, REQ + ("mdl",)), P(None, REQ, "mdl")),
        check_vma=False,
    )
```

```python
import jax
import jax.numpy as jnp
from jax import lax
from jax.sharding import Mesh, PartitionSpec as P

D = 5120
QUERY_HEADS = 32
KEY_VALUE_HEADS = 8
HEAD_SIZE = 128


NEGATIVE_FILL = -1e30
REQ = ("y", "z", "c")


def gather_rows(part):
    count = lax.axis_size(REQ)
    flat = part.reshape(-1, 128)
    flat = lax.all_gather(flat, "c", axis=0, tiled=True)
    flat = lax.all_gather(flat, "z", axis=0, tiled=True)
    copies = jnp.broadcast_to(flat[None], (lax.axis_size("y"),) + flat.shape)
    return lax.all_to_all(copies, "y", 0, 0, tiled=True).reshape((count,) + part.shape)


def scatter_sum(parts):
    wide = None
    for position, name in ((2, "c"), (0, "y"), (1, "z")):
        moved = lax.all_to_all(parts.astype(jnp.bfloat16), name, position, position, tiled=True)
        wide = moved.astype(jnp.float32).sum(position, keepdims=True)
        parts = wide
    return wide


def mdl_sum(values, wires):
    count = lax.axis_size("mdl")
    sent = tuple(v.astype(w) for v, w in zip(values, wires))
    totals = [v.astype(jnp.float32) for v in values]
    for shift in range(1, count):
        pairs = [(i, (i + shift) % count) for i in range(count)]
        arrived = lax.ppermute(sent, "mdl", pairs)
        totals = [t + a.astype(jnp.float32) for t, a in zip(totals, arrived)]
    return totals


def mdl_scatter_sum(value, wire):
    count = lax.axis_size("mdl")
    me = lax.axis_index("mdl")
    height = value.shape[0] // count
    blocks = value.astype(wire).reshape((count, height * value.shape[1] // 128, 128))
    total = lax.dynamic_index_in_dim(blocks, me, 0, keepdims=False).astype(jnp.float32)
    for shift in range(1, count):
        pairs = [(i, (i + shift) % count) for i in range(count)]
        outgoing = lax.dynamic_index_in_dim(blocks, (me + shift) % count, 0, keepdims=False)
        total = total + lax.ppermute(outgoing, "mdl", pairs).astype(jnp.float32)
    return total.reshape(height, value.shape[1])


def slot_bounds(lengths):
    span_sizes = lengths + 1
    first_rows = jnp.cumsum(span_sizes) - span_sizes
    return (first_rows, first_rows + span_sizes)


def attend_rows(query_rows, key_value_store, row_base, first_rows, end_rows):
    block_rows = 128
    slot_count, kv_heads, group_width, head_dim = query_rows.shape
    pool_rows = key_value_store.shape[1]
    key_table = key_value_store[0].reshape(pool_rows, kv_heads, head_dim)
    value_table = key_value_store[1].reshape(pool_rows, kv_heads, head_dim)
    needed = jnp.clip(jnp.max(end_rows) - row_base, 0, pool_rows)
    block_count = (needed + block_rows - 1) // block_rows
    score_scale = head_dim ** (-0.5)

    def advance(block_index, carried):
        running_max, denominator, accumulated = carried
        offset = block_index * block_rows
        key_block = lax.dynamic_slice_in_dim(key_table, offset, block_rows, 0)
        value_block = lax.dynamic_slice_in_dim(value_table, offset, block_rows, 0)
        scores = (
            jnp.einsum("sngd,tnd->sngt", query_rows, key_block, preferred_element_type=jnp.float32)
            * score_scale
        )
        row_ids = row_base + offset + jnp.arange(block_rows, dtype=jnp.int32)
        inside = (
            (row_ids[None, :] >= first_rows[:, None]) & (row_ids[None, :] < end_rows[:, None])
        )[:, None, None, :]
        scores = jnp.where(inside, scores, NEGATIVE_FILL)
        new_max = jnp.maximum(running_max, jnp.max(scores, axis=-1))
        weights = jnp.where(inside, jnp.exp(scores - new_max[..., None]), 0.0)
        factor = jnp.exp(running_max - new_max)
        denominator = denominator * factor + jnp.sum(weights, axis=-1)
        accumulated = accumulated * factor[..., None] + jnp.einsum(
            "sngt,tnd->sngd",
            weights.astype(jnp.bfloat16),
            value_block,
            preferred_element_type=jnp.float32,
        )
        return (new_max, denominator, accumulated)

    initial = (
        jnp.full((slot_count, kv_heads, group_width), NEGATIVE_FILL, jnp.float32),
        jnp.zeros((slot_count, kv_heads, group_width), jnp.float32),
        jnp.zeros((slot_count, kv_heads, group_width, head_dim), jnp.float32),
    )
    return lax.fori_loop(0, block_count, advance, initial)


def body(
    lengths,
    assignment,
    query,
    key_value_fresh,
    kv_cache,
    hidden_in,
    out_weight,
    norm_gain,
    gate_up_weight,
    down_weight,
):
    slot_count = lengths.shape[0]
    first_rows, end_rows = slot_bounds(lengths)
    key_value_store = kv_cache
    for slot_index in range(slot_count):
        key_value_store = lax.dynamic_update_slice(
            key_value_store,
            key_value_fresh[:, slot_index : slot_index + 1, :],
            (jnp.int32(0), end_rows[slot_index] - 1, jnp.int32(0)),
        )
    kv_heads = key_value_store.shape[2] // HEAD_SIZE
    group_width = QUERY_HEADS // KEY_VALUE_HEADS
    query_rows = query.reshape(slot_count, kv_heads, group_width, HEAD_SIZE)
    joint_max, denominator, accumulated = attend_rows(
        query_rows, key_value_store, 0, first_rows, end_rows
    )
    attended = (
        (accumulated / denominator[..., None])
        .astype(jnp.bfloat16)
        .reshape(slot_count, kv_heads * group_width * HEAD_SIZE)
    )
    all_attended = gather_rows(attended).reshape(-1, attended.shape[1])
    projected = jnp.dot(all_attended, out_weight, preferred_element_type=jnp.float32)
    head_share = mdl_scatter_sum(projected.T, jnp.bfloat16).T
    total_rows = assignment.shape[0]
    inverse = (
        jnp.zeros((total_rows,), jnp.int32)
        .at[assignment]
        .set(jnp.arange(total_rows, dtype=jnp.int32))
    )
    placed = jnp.take(head_share, inverse, axis=0)
    residual_wide = hidden_in.astype(jnp.float32) + placed
    residual = residual_wide.astype(jnp.bfloat16)
    local_wide = residual.astype(jnp.float32)
    col_groups = gate_up_weight.shape[1]
    sub_width = hidden_in.shape[1]
    gathered = jnp.transpose(gather_rows(residual.T), (2, 0, 1)).reshape(total_rows, col_groups * sub_width)
    widened = gathered.astype(jnp.float32)
    own_squares = jnp.sum(widened * widened, axis=1)
    gain_table = norm_gain.reshape(col_groups, lax.axis_size("mdl"), sub_width)
    gain_cols = lax.dynamic_index_in_dim(
        gain_table, lax.axis_index("mdl"), 1, keepdims=False
    ).reshape(col_groups * sub_width)
    unscaled = (widened * gain_cols).astype(jnp.bfloat16)
    gate_up = gate_up_weight.reshape(2, col_groups * sub_width, gate_up_weight.shape[4])
    partial_value = jnp.einsum("rk,gkf->gfr", unscaled, gate_up, preferred_element_type=jnp.float32)
    units = partial_value.shape[1]
    squares_high = own_squares.astype(jnp.bfloat16)
    squares_low = (own_squares - squares_high.astype(jnp.float32)).astype(jnp.bfloat16)
    payload = jnp.concatenate(
        [partial_value.reshape(2 * units, total_rows).astype(jnp.bfloat16), squares_high[None], squares_low[None]],
        axis=0,
    )
    (summed_payload,) = mdl_sum((payload,), (jnp.bfloat16,))
    square_sum = summed_payload[2 * units] + summed_payload[2 * units + 1]
    scale = lax.rsqrt(square_sum / D + 1e-05)
    gate_sums = summed_payload[: 2 * units].reshape(2, units, total_rows) * scale[None, None, :]
    hidden = (jax.nn.silu(gate_sums[0]) * gate_sums[1]).astype(jnp.bfloat16)
    columns = down_weight.reshape(down_weight.shape[0], col_groups * sub_width)
    lowered = lax.dot_general(
        columns, hidden, (((0,), (0,)), ((), ())), preferred_element_type=jnp.float32
    )
    mesh_shape = (lax.axis_size("y"), lax.axis_size("z"), lax.axis_size("c"))
    summed = scatter_sum(lowered.reshape(mesh_shape + (sub_width * total_rows // 128, 128))).reshape(sub_width, total_rows)
    layer_out = (local_wide + summed.T).astype(jnp.bfloat16)
    return (layer_out, key_value_store)


def solution(mesh):
    req_size, mdl_size = mesh.devices.shape
    chips_y = 4
    split = Mesh(
        mesh.devices.reshape(chips_y, req_size // (2 * chips_y), 2, mdl_size),
        REQ + ("mdl",),
    )
    return jax.shard_map(
        body,
        mesh=split,
        in_specs=(
            P(REQ),
            P(),
            P(REQ, "mdl"),
            P(None, REQ, "mdl"),
            P(None, REQ, "mdl"),
            P(None, (REQ + ("mdl",))),
            P("mdl", REQ),
            P(),
            P(None, None, "mdl", None, REQ),
            P(REQ, None, "mdl", None),
        ),
        out_specs=(P(None, REQ + ("mdl",)), P(None, REQ, "mdl")),
        check_vma=False,
    )
```

```python
import jax
import jax.numpy as jnp
from jax import lax
from jax.sharding import Mesh, PartitionSpec as P

D = 5120
QUERY_HEADS = 32
KEY_VALUE_HEADS = 8
HEAD_SIZE = 128


NEGATIVE_FILL = -1e30
REQ = ("y", "z", "c")


def gather_rows(part):
    count = lax.axis_size(REQ)
    flat = part.reshape(-1, 128)
    flat = lax.all_gather(flat, "c", axis=0, tiled=True)
    flat = lax.all_gather(flat, "z", axis=0, tiled=True)
    copies = jnp.broadcast_to(flat[None], (lax.axis_size("y"),) + flat.shape)
    return lax.all_to_all(copies, "y", 0, 0, tiled=True).reshape((count,) + part.shape)


def scatter_sum(parts):
    wide = None
    for position, name in ((2, "c"), (0, "y"), (1, "z")):
        moved = lax.all_to_all(parts.astype(jnp.bfloat16), name, position, position, tiled=True)
        wide = moved.astype(jnp.float32).sum(position, keepdims=True)
        parts = wide
    return wide


def mdl_sum(values, wires):
    count = lax.axis_size("mdl")
    sent = tuple(v.astype(w) for v, w in zip(values, wires))
    totals = [v.astype(jnp.float32) for v in values]
    for shift in range(1, count):
        pairs = [(i, (i + shift) % count) for i in range(count)]
        arrived = lax.ppermute(sent, "mdl", pairs)
        totals = [t + a.astype(jnp.float32) for t, a in zip(totals, arrived)]
    return totals


def mdl_scatter_sum(value, wire):
    count = lax.axis_size("mdl")
    height = value.shape[0] // count
    blocks = value.astype(wire).reshape((count, height * value.shape[1] // 128, 128))
    moved = lax.all_to_all(blocks, "mdl", 0, 0, tiled=True)
    return moved.astype(jnp.float32).sum(0).reshape(height, value.shape[1])


def slot_bounds(lengths):
    span_sizes = lengths + 1
    first_rows = jnp.cumsum(span_sizes) - span_sizes
    return (first_rows, first_rows + span_sizes)


def attend_rows(query_rows, key_value_store, row_base, first_rows, end_rows):
    block_rows = 128
    slot_count, kv_heads, group_width, head_dim = query_rows.shape
    pool_rows = key_value_store.shape[1]
    key_table = key_value_store[0].reshape(pool_rows, kv_heads, head_dim)
    value_table = key_value_store[1].reshape(pool_rows, kv_heads, head_dim)
    needed = jnp.clip(jnp.max(end_rows) - row_base, 0, pool_rows)
    block_count = (needed + block_rows - 1) // block_rows
    score_scale = head_dim ** (-0.5)

    def advance(block_index, carried):
        running_max, denominator, accumulated = carried
        offset = block_index * block_rows
        key_block = lax.dynamic_slice_in_dim(key_table, offset, block_rows, 0)
        value_block = lax.dynamic_slice_in_dim(value_table, offset, block_rows, 0)
        scores = (
            jnp.einsum("sngd,tnd->sngt", query_rows, key_block, preferred_element_type=jnp.float32)
            * score_scale
        )
        row_ids = row_base + offset + jnp.arange(block_rows, dtype=jnp.int32)
        inside = (
            (row_ids[None, :] >= first_rows[:, None]) & (row_ids[None, :] < end_rows[:, None])
        )[:, None, None, :]
        scores = jnp.where(inside, scores, NEGATIVE_FILL)
        new_max = jnp.maximum(running_max, jnp.max(scores, axis=-1))
        weights = jnp.where(inside, jnp.exp(scores - new_max[..., None]), 0.0)
        factor = jnp.exp(running_max - new_max)
        denominator = denominator * factor + jnp.sum(weights, axis=-1)
        accumulated = accumulated * factor[..., None] + jnp.einsum(
            "sngt,tnd->sngd",
            weights.astype(jnp.bfloat16),
            value_block,
            preferred_element_type=jnp.float32,
        )
        return (new_max, denominator, accumulated)

    initial = (
        jnp.full((slot_count, kv_heads, group_width), NEGATIVE_FILL, jnp.float32),
        jnp.zeros((slot_count, kv_heads, group_width), jnp.float32),
        jnp.zeros((slot_count, kv_heads, group_width, head_dim), jnp.float32),
    )
    return lax.fori_loop(0, block_count, advance, initial)


def body(
    lengths,
    assignment,
    query,
    key_value_fresh,
    kv_cache,
    hidden_in,
    out_weight,
    norm_gain,
    gate_up_weight,
    down_weight,
):
    slot_count = lengths.shape[0]
    first_rows, end_rows = slot_bounds(lengths)
    key_value_store = kv_cache
    for slot_index in range(slot_count):
        key_value_store = lax.dynamic_update_slice(
            key_value_store,
            key_value_fresh[:, slot_index : slot_index + 1, :],
            (jnp.int32(0), end_rows[slot_index] - 1, jnp.int32(0)),
        )
    kv_heads = key_value_store.shape[2] // HEAD_SIZE
    group_width = QUERY_HEADS // KEY_VALUE_HEADS
    query_rows = query.reshape(slot_count, kv_heads, group_width, HEAD_SIZE)
    joint_max, denominator, accumulated = attend_rows(
        query_rows, key_value_store, 0, first_rows, end_rows
    )
    attended = (
        (accumulated / denominator[..., None])
        .astype(jnp.bfloat16)
        .reshape(slot_count, kv_heads * group_width * HEAD_SIZE)
    )
    all_attended = gather_rows(attended).reshape(-1, attended.shape[1])
    projected = jnp.dot(all_attended, out_weight, preferred_element_type=jnp.float32)
    head_share = mdl_scatter_sum(projected.T, jnp.bfloat16).T
    total_rows = assignment.shape[0]
    inverse = (
        jnp.zeros((total_rows,), jnp.int32)
        .at[assignment]
        .set(jnp.arange(total_rows, dtype=jnp.int32))
    )
    placed = jnp.take(head_share, inverse, axis=0)
    residual_wide = hidden_in.astype(jnp.float32) + placed
    residual = residual_wide.astype(jnp.bfloat16)
    local_wide = residual.astype(jnp.float32)
    col_groups = gate_up_weight.shape[1]
    sub_width = hidden_in.shape[1]
    gathered = jnp.transpose(gather_rows(residual.T), (2, 0, 1)).reshape(total_rows, col_groups * sub_width)
    widened = gathered.astype(jnp.float32)
    own_squares = jnp.sum(widened * widened, axis=1)
    gain_table = norm_gain.reshape(col_groups, lax.axis_size("mdl"), sub_width)
    gain_cols = lax.dynamic_index_in_dim(
        gain_table, lax.axis_index("mdl"), 1, keepdims=False
    ).reshape(col_groups * sub_width)
    unscaled = (widened * gain_cols).astype(jnp.bfloat16)
    gate_up = gate_up_weight.reshape(2, col_groups * sub_width, gate_up_weight.shape[4])
    partial_value = jnp.einsum("rk,gkf->gfr", unscaled, gate_up, preferred_element_type=jnp.float32)
    units = partial_value.shape[1]
    mdl_count = lax.axis_size("mdl")
    quarter = units // mdl_count
    squares_high = own_squares.astype(jnp.bfloat16)
    squares_low = (own_squares - squares_high.astype(jnp.float32)).astype(jnp.bfloat16)
    squares_pair = jnp.broadcast_to(jnp.stack([squares_high, squares_low])[None], (mdl_count, 2, total_rows))
    blocks = jnp.transpose(
        partial_value.astype(jnp.bfloat16).reshape(2, mdl_count, quarter, total_rows), (1, 0, 2, 3)
    ).reshape(mdl_count, 2 * quarter, total_rows)
    payload = jnp.concatenate([blocks, squares_pair], axis=1)
    summed_payload = lax.all_to_all(payload, "mdl", 0, 0, tiled=True).astype(jnp.float32).sum(0)
    square_sum = summed_payload[2 * quarter] + summed_payload[2 * quarter + 1]
    scale = lax.rsqrt(square_sum / D + 1e-05)
    gate_part = summed_payload[:quarter] * scale[None, :]
    up_part = summed_payload[quarter : 2 * quarter] * scale[None, :]
    hidden_part = (jax.nn.silu(gate_part) * up_part).astype(jnp.bfloat16)
    hidden_copies = jnp.broadcast_to(hidden_part[None], (mdl_count,) + hidden_part.shape)
    hidden = lax.all_to_all(hidden_copies, "mdl", 0, 0, tiled=True).reshape(units, total_rows)
    columns = down_weight.reshape(down_weight.shape[0], col_groups * sub_width)
    lowered = lax.dot_general(
        columns, hidden, (((0,), (0,)), ((), ())), preferred_element_type=jnp.float32
    )
    mesh_shape = (lax.axis_size("y"), lax.axis_size("z"), lax.axis_size("c"))
    summed = scatter_sum(lowered.reshape(mesh_shape + (sub_width * total_rows // 128, 128))).reshape(sub_width, total_rows)
    layer_out = (local_wide + summed.T).astype(jnp.bfloat16)
    return (layer_out, key_value_store)


def solution(mesh):
    req_size, mdl_size = mesh.devices.shape
    chips_y = 4
    split = Mesh(
        mesh.devices.reshape(chips_y, req_size // (2 * chips_y), 2, mdl_size),
        REQ + ("mdl",),
    )
    return jax.shard_map(
        body,
        mesh=split,
        in_specs=(
            P(REQ),
            P(),
            P(REQ, "mdl"),
            P(None, REQ, "mdl"),
            P(None, REQ, "mdl"),
            P(None, (REQ + ("mdl",))),
            P("mdl", REQ),
            P(),
            P(None, None, "mdl", None, REQ),
            P(REQ, None, "mdl", None),
        ),
        out_specs=(P(None, REQ + ("mdl",)), P(None, REQ, "mdl")),
        check_vma=False,
    )
```

```python
import jax
import jax.numpy as jnp
from jax import lax
from jax.experimental import pallas as pl
from jax.experimental.pallas import tpu as pltpu
from jax.sharding import Mesh, PartitionSpec as P

D = 5120
QUERY_HEADS = 32
KEY_VALUE_HEADS = 8
HEAD_SIZE = 128


NEGATIVE_FILL = -1e30
REQ = ("y", "z", "c")


def gather_rows(part):
    count = lax.axis_size(REQ)
    flat = part.reshape(-1, 128)
    flat = lax.all_gather(flat, "c", axis=0, tiled=True)
    flat = lax.all_gather(flat, "z", axis=0, tiled=True)
    copies = jnp.broadcast_to(flat[None], (lax.axis_size("y"),) + flat.shape)
    return lax.all_to_all(copies, "y", 0, 0, tiled=True).reshape((count,) + part.shape)


def scatter_sum(parts):
    wide = None
    for position, name in ((2, "c"), (0, "y"), (1, "z")):
        moved = lax.all_to_all(parts.astype(jnp.bfloat16), name, position, position, tiled=True)
        wide = moved.astype(jnp.float32).sum(position, keepdims=True)
        parts = wide
    return wide


def mdl_sum(values, wires):
    count = lax.axis_size("mdl")
    sent = tuple(v.astype(w) for v, w in zip(values, wires))
    totals = [v.astype(jnp.float32) for v in values]
    for shift in range(1, count):
        pairs = [(i, (i + shift) % count) for i in range(count)]
        arrived = lax.ppermute(sent, "mdl", pairs)
        totals = [t + a.astype(jnp.float32) for t, a in zip(totals, arrived)]
    return totals


def mdl_scatter_sum(value, wire):
    count = lax.axis_size("mdl")
    height = value.shape[0] // count
    blocks = value.astype(wire).reshape((count, height * value.shape[1] // 128, 128))
    moved = lax.all_to_all(blocks, "mdl", 0, 0, tiled=True)
    return moved.astype(jnp.float32).sum(0).reshape(height, value.shape[1])


CHUNK_ROWS = 256


def attention_kernel(lengths_ref, query_ref, fresh_ref, cache_hbm, out_ref, keys, values, sems):
    rows = keys.shape[0]
    chunks = rows // CHUNK_ROWS
    copies = []
    for chunk in range(chunks):
        window = pl.ds(chunk * CHUNK_ROWS, CHUNK_ROWS)
        for which, target in ((0, keys), (1, values)):
            copy = pltpu.make_async_copy(cache_hbm.at[which, window], target.at[window], sems.at[which, chunk])
            copy.start()
            copies.append(copy)
    slot_count = lengths_ref.shape[0]
    kv_heads, row_count, head_dim = query_ref.shape
    group_width = row_count // slot_count
    row_slot = lax.broadcasted_iota(jnp.int32, (row_count, 1), 0) // group_width
    first = jnp.zeros((row_count, 1), jnp.int32)
    end = jnp.zeros((row_count, 1), jnp.int32)
    start = jnp.int32(0)
    for slot in range(slot_count):
        length = lengths_ref[slot]
        first = jnp.where(row_slot == slot, start, first)
        end = jnp.where(row_slot == slot, start + length, end)
        start = start + length + 1
    columns = lax.broadcasted_iota(jnp.int32, (row_count, rows), 1)
    inside = (columns >= first) & (columns < end)
    pick = (lax.broadcasted_iota(jnp.int32, (row_count, slot_count), 1) == row_slot)
    for copy in copies:
        copy.wait()
    score_scale = head_dim ** (-0.5)
    for head in range(kv_heads):
        lanes = pl.ds(head * head_dim, head_dim)
        query_rows = query_ref[head]
        scores = lax.dot_general(
            query_rows, keys[:, lanes], (((1,), (1,)), ((), ())), preferred_element_type=jnp.float32
        ) * score_scale
        fresh_scores = lax.dot_general(
            query_rows, fresh_ref[0, head], (((1,), (1,)), ((), ())), preferred_element_type=jnp.float32
        ) * score_scale
        new_score = jnp.sum(jnp.where(pick, fresh_scores, 0.0), axis=1, keepdims=True)
        scores = jnp.where(inside, scores, NEGATIVE_FILL)
        top = jnp.maximum(jnp.max(scores, axis=1, keepdims=True), new_score)
        weights = jnp.where(inside, jnp.exp(scores - top), 0.0)
        new_weight = jnp.exp(new_score - top)
        denominator = jnp.sum(weights, axis=1, keepdims=True) + new_weight
        mixed = jnp.dot(weights.astype(jnp.bfloat16), values[:, lanes], preferred_element_type=jnp.float32)
        fresh_values = jnp.dot(pick.astype(jnp.bfloat16), fresh_ref[1, head], preferred_element_type=jnp.float32)
        mixed = mixed + new_weight.astype(jnp.bfloat16).astype(jnp.float32) * fresh_values
        out_ref[head] = (mixed / denominator).astype(out_ref.dtype)


def attend_kernel(lengths, query, key_value_fresh, kv_cache):
    slot_count = lengths.shape[0]
    kv_width = kv_cache.shape[2]
    kv_heads = kv_width // HEAD_SIZE
    group_width = QUERY_HEADS // KEY_VALUE_HEADS
    rows = kv_cache.shape[1]
    query_rows = jnp.transpose(
        query.reshape(slot_count, kv_heads, group_width, HEAD_SIZE), (1, 0, 2, 3)
    ).reshape(kv_heads, slot_count * group_width, HEAD_SIZE)
    fresh = jnp.transpose(
        key_value_fresh.reshape(2, slot_count, kv_heads, HEAD_SIZE), (0, 2, 1, 3)
    )
    out = pl.pallas_call(
        attention_kernel,
        out_shape=jax.ShapeDtypeStruct(query_rows.shape, jnp.bfloat16),
        in_specs=[
            pl.BlockSpec(memory_space=pltpu.SMEM),
            pl.BlockSpec(memory_space=pltpu.VMEM),
            pl.BlockSpec(memory_space=pltpu.VMEM),
            pl.BlockSpec(memory_space=pl.ANY),
        ],
        out_specs=pl.BlockSpec(memory_space=pltpu.VMEM),
        scratch_shapes=[
            pltpu.VMEM((rows, kv_width), kv_cache.dtype),
            pltpu.VMEM((rows, kv_width), kv_cache.dtype),
            pltpu.SemaphoreType.DMA((2, rows // CHUNK_ROWS)),
        ],
        cost_estimate=pl.CostEstimate(
            flops=4 * kv_heads * slot_count * group_width * rows * HEAD_SIZE,
            transcendentals=kv_heads * slot_count * group_width * rows,
            bytes_accessed=2 * rows * kv_width * 2,
        ),
    )(lengths, query_rows, fresh, kv_cache)
    return jnp.transpose(
        out.reshape(kv_heads, slot_count, group_width, HEAD_SIZE), (1, 0, 2, 3)
    ).reshape(slot_count, kv_heads * group_width * HEAD_SIZE)


def slot_bounds(lengths):
    span_sizes = lengths + 1
    first_rows = jnp.cumsum(span_sizes) - span_sizes
    return (first_rows, first_rows + span_sizes)


def attend_rows(query_rows, key_value_store, row_base, first_rows, end_rows):
    block_rows = 128
    slot_count, kv_heads, group_width, head_dim = query_rows.shape
    pool_rows = key_value_store.shape[1]
    key_table = key_value_store[0].reshape(pool_rows, kv_heads, head_dim)
    value_table = key_value_store[1].reshape(pool_rows, kv_heads, head_dim)
    needed = jnp.clip(jnp.max(end_rows) - row_base, 0, pool_rows)
    block_count = (needed + block_rows - 1) // block_rows
    score_scale = head_dim ** (-0.5)

    def advance(block_index, carried):
        running_max, denominator, accumulated = carried
        offset = block_index * block_rows
        key_block = lax.dynamic_slice_in_dim(key_table, offset, block_rows, 0)
        value_block = lax.dynamic_slice_in_dim(value_table, offset, block_rows, 0)
        scores = (
            jnp.einsum("sngd,tnd->sngt", query_rows, key_block, preferred_element_type=jnp.float32)
            * score_scale
        )
        row_ids = row_base + offset + jnp.arange(block_rows, dtype=jnp.int32)
        inside = (
            (row_ids[None, :] >= first_rows[:, None]) & (row_ids[None, :] < end_rows[:, None])
        )[:, None, None, :]
        scores = jnp.where(inside, scores, NEGATIVE_FILL)
        new_max = jnp.maximum(running_max, jnp.max(scores, axis=-1))
        weights = jnp.where(inside, jnp.exp(scores - new_max[..., None]), 0.0)
        factor = jnp.exp(running_max - new_max)
        denominator = denominator * factor + jnp.sum(weights, axis=-1)
        accumulated = accumulated * factor[..., None] + jnp.einsum(
            "sngt,tnd->sngd",
            weights.astype(jnp.bfloat16),
            value_block,
            preferred_element_type=jnp.float32,
        )
        return (new_max, denominator, accumulated)

    initial = (
        jnp.full((slot_count, kv_heads, group_width), NEGATIVE_FILL, jnp.float32),
        jnp.zeros((slot_count, kv_heads, group_width), jnp.float32),
        jnp.zeros((slot_count, kv_heads, group_width, head_dim), jnp.float32),
    )
    return lax.fori_loop(0, block_count, advance, initial)


def body(
    lengths,
    assignment,
    query,
    key_value_fresh,
    kv_cache,
    hidden_in,
    out_weight,
    norm_gain,
    gate_up_weight,
    down_weight,
):
    slot_count = lengths.shape[0]
    first_rows, end_rows = slot_bounds(lengths)
    key_value_store = kv_cache
    for slot_index in range(slot_count):
        key_value_store = lax.dynamic_update_slice(
            key_value_store,
            key_value_fresh[:, slot_index : slot_index + 1, :],
            (jnp.int32(0), end_rows[slot_index] - 1, jnp.int32(0)),
        )
    kv_heads = key_value_store.shape[2] // HEAD_SIZE
    group_width = QUERY_HEADS // KEY_VALUE_HEADS
    attended = attend_kernel(lengths, query, key_value_fresh, kv_cache)
    all_attended = gather_rows(attended).reshape(-1, attended.shape[1])
    projected = jnp.dot(all_attended, out_weight, preferred_element_type=jnp.float32)
    head_share = mdl_scatter_sum(projected.T, jnp.bfloat16).T
    total_rows = assignment.shape[0]
    inverse = (
        jnp.zeros((total_rows,), jnp.int32)
        .at[assignment]
        .set(jnp.arange(total_rows, dtype=jnp.int32))
    )
    placed = jnp.take(head_share, inverse, axis=0)
    residual_wide = hidden_in.astype(jnp.float32) + placed
    residual = residual_wide.astype(jnp.bfloat16)
    local_wide = residual.astype(jnp.float32)
    col_groups = gate_up_weight.shape[1]
    sub_width = hidden_in.shape[1]
    gathered = jnp.transpose(gather_rows(residual.T), (2, 0, 1)).reshape(total_rows, col_groups * sub_width)
    widened = gathered.astype(jnp.float32)
    own_squares = jnp.sum(widened * widened, axis=1)
    gain_table = norm_gain.reshape(col_groups, lax.axis_size("mdl"), sub_width)
    gain_cols = lax.dynamic_index_in_dim(
        gain_table, lax.axis_index("mdl"), 1, keepdims=False
    ).reshape(col_groups * sub_width)
    unscaled = (widened * gain_cols).astype(jnp.bfloat16)
    gate_up = gate_up_weight.reshape(2, col_groups * sub_width, gate_up_weight.shape[4])
    partial_value = jnp.einsum("rk,gkf->gfr", unscaled, gate_up, preferred_element_type=jnp.float32)
    units = partial_value.shape[1]
    mdl_count = lax.axis_size("mdl")
    quarter = units // mdl_count
    squares_high = own_squares.astype(jnp.bfloat16)
    squares_low = (own_squares - squares_high.astype(jnp.float32)).astype(jnp.bfloat16)
    squares_pair = jnp.broadcast_to(jnp.stack([squares_high, squares_low])[None], (mdl_count, 2, total_rows))
    blocks = jnp.transpose(
        partial_value.astype(jnp.bfloat16).reshape(2, mdl_count, quarter, total_rows), (1, 0, 2, 3)
    ).reshape(mdl_count, 2 * quarter, total_rows)
    payload = jnp.concatenate([blocks, squares_pair], axis=1)
    summed_payload = lax.all_to_all(payload, "mdl", 0, 0, tiled=True).astype(jnp.float32).sum(0)
    square_sum = summed_payload[2 * quarter] + summed_payload[2 * quarter + 1]
    scale = lax.rsqrt(square_sum / D + 1e-05)
    gate_part = summed_payload[:quarter] * scale[None, :]
    up_part = summed_payload[quarter : 2 * quarter] * scale[None, :]
    hidden_part = (jax.nn.silu(gate_part) * up_part).astype(jnp.bfloat16)
    hidden_copies = jnp.broadcast_to(hidden_part[None], (mdl_count,) + hidden_part.shape)
    hidden = lax.all_to_all(hidden_copies, "mdl", 0, 0, tiled=True).reshape(units, total_rows)
    columns = down_weight.reshape(down_weight.shape[0], col_groups * sub_width)
    lowered = lax.dot_general(
        columns, hidden, (((0,), (0,)), ((), ())), preferred_element_type=jnp.float32
    )
    mesh_shape = (lax.axis_size("y"), lax.axis_size("z"), lax.axis_size("c"))
    summed = scatter_sum(lowered.reshape(mesh_shape + (sub_width * total_rows // 128, 128))).reshape(sub_width, total_rows)
    layer_out = (local_wide + summed.T).astype(jnp.bfloat16)
    return (layer_out, key_value_store)


def solution(mesh):
    req_size, mdl_size = mesh.devices.shape
    chips_y = 4
    split = Mesh(
        mesh.devices.reshape(chips_y, req_size // (2 * chips_y), 2, mdl_size),
        REQ + ("mdl",),
    )
    return jax.shard_map(
        body,
        mesh=split,
        in_specs=(
            P(REQ),
            P(),
            P(REQ, "mdl"),
            P(None, REQ, "mdl"),
            P(None, REQ, "mdl"),
            P(None, (REQ + ("mdl",))),
            P("mdl", REQ),
            P(),
            P(None, None, "mdl", None, REQ),
            P(REQ, None, "mdl", None),
        ),
        out_specs=(P(None, REQ + ("mdl",)), P(None, REQ, "mdl")),
        check_vma=False,
    )
```

```python
import jax
import jax.numpy as jnp
from jax import lax
from jax.experimental import pallas as pl
from jax.experimental.pallas import tpu as pltpu
from jax.sharding import Mesh, PartitionSpec as P

D = 5120
QUERY_HEADS = 32
KEY_VALUE_HEADS = 8
HEAD_SIZE = 128


NEGATIVE_FILL = -1e30
REQ = ("y", "z", "c")


def gather_rows(part):
    count = lax.axis_size(REQ)
    flat = part.reshape(-1, 128)
    flat = lax.all_gather(flat, "c", axis=0, tiled=True)
    flat = lax.all_gather(flat, "z", axis=0, tiled=True)
    copies = jnp.broadcast_to(flat[None], (lax.axis_size("y"),) + flat.shape)
    return lax.all_to_all(copies, "y", 0, 0, tiled=True).reshape((count,) + part.shape)


def scatter_sum(parts):
    wide = None
    for position, name in ((2, "c"), (0, "y"), (1, "z")):
        moved = lax.all_to_all(parts.astype(jnp.bfloat16), name, position, position, tiled=True)
        wide = moved.astype(jnp.float32).sum(position, keepdims=True)
        parts = wide
    return wide


def mdl_sum(values, wires):
    count = lax.axis_size("mdl")
    sent = tuple(v.astype(w) for v, w in zip(values, wires))
    totals = [v.astype(jnp.float32) for v in values]
    for shift in range(1, count):
        pairs = [(i, (i + shift) % count) for i in range(count)]
        arrived = lax.ppermute(sent, "mdl", pairs)
        totals = [t + a.astype(jnp.float32) for t, a in zip(totals, arrived)]
    return totals


def mdl_scatter_sum(value, wire):
    count = lax.axis_size("mdl")
    height = value.shape[0] // count
    blocks = value.astype(wire).reshape((count, height * value.shape[1] // 128, 128))
    moved = lax.all_to_all(blocks, "mdl", 0, 0, tiled=True)
    return moved.astype(jnp.float32).sum(0).reshape(height, value.shape[1])


CHUNK_ROWS = 256


def attention_kernel(lengths_ref, query_ref, fresh_ref, cache_hbm, out_ref, keys, values, sems):
    rows = keys.shape[0]
    chunks = rows // CHUNK_ROWS
    copies = []
    for chunk in range(chunks):
        window = pl.ds(chunk * CHUNK_ROWS, CHUNK_ROWS)
        for which, target in ((0, keys), (1, values)):
            copy = pltpu.make_async_copy(cache_hbm.at[which, window], target.at[window], sems.at[which, chunk])
            copy.start()
            copies.append(copy)
    slot_count = lengths_ref.shape[0]
    kv_heads, row_count, head_dim = query_ref.shape
    group_width = row_count // slot_count
    row_slot = lax.broadcasted_iota(jnp.int32, (row_count, 1), 0) // group_width
    first = jnp.zeros((row_count, 1), jnp.int32)
    end = jnp.zeros((row_count, 1), jnp.int32)
    start = jnp.int32(0)
    for slot in range(slot_count):
        length = lengths_ref[slot]
        first = jnp.where(row_slot == slot, start, first)
        end = jnp.where(row_slot == slot, start + length, end)
        start = start + length + 1
    columns = lax.broadcasted_iota(jnp.int32, (row_count, rows), 1)
    inside = (columns >= first) & (columns < end)
    pick = (lax.broadcasted_iota(jnp.int32, (row_count, slot_count), 1) == row_slot)
    for copy in copies:
        copy.wait()
    score_scale = head_dim ** (-0.5)
    for head in range(kv_heads):
        lanes = pl.ds(head * head_dim, head_dim)
        query_rows = query_ref[head]
        scores = lax.dot_general(
            query_rows, keys[:, lanes], (((1,), (1,)), ((), ())), preferred_element_type=jnp.float32
        ) * score_scale
        fresh_scores = lax.dot_general(
            query_rows, fresh_ref[0, head], (((1,), (1,)), ((), ())), preferred_element_type=jnp.float32
        ) * score_scale
        new_score = jnp.sum(jnp.where(pick, fresh_scores, 0.0), axis=1, keepdims=True)
        scores = jnp.where(inside, scores, NEGATIVE_FILL)
        top = jnp.maximum(jnp.max(scores, axis=1, keepdims=True), new_score)
        weights = jnp.where(inside, jnp.exp(scores - top), 0.0)
        new_weight = jnp.exp(new_score - top)
        denominator = jnp.sum(weights, axis=1, keepdims=True) + new_weight
        mixed = jnp.dot(weights.astype(jnp.bfloat16), values[:, lanes], preferred_element_type=jnp.float32)
        fresh_values = jnp.dot(pick.astype(jnp.bfloat16), fresh_ref[1, head], preferred_element_type=jnp.float32)
        mixed = mixed + new_weight.astype(jnp.bfloat16).astype(jnp.float32) * fresh_values
        out_ref[head] = (mixed / denominator).astype(out_ref.dtype)


def attend_kernel(lengths, query, key_value_fresh, kv_cache):
    slot_count = lengths.shape[0]
    kv_width = kv_cache.shape[2]
    kv_heads = kv_width // HEAD_SIZE
    group_width = QUERY_HEADS // KEY_VALUE_HEADS
    rows = kv_cache.shape[1]
    query_rows = jnp.transpose(
        query.reshape(slot_count, kv_heads, group_width, HEAD_SIZE), (1, 0, 2, 3)
    ).reshape(kv_heads, slot_count * group_width, HEAD_SIZE)
    fresh = jnp.transpose(
        key_value_fresh.reshape(2, slot_count, kv_heads, HEAD_SIZE), (0, 2, 1, 3)
    )
    out = pl.pallas_call(
        attention_kernel,
        out_shape=jax.ShapeDtypeStruct(query_rows.shape, jnp.bfloat16),
        in_specs=[
            pl.BlockSpec(memory_space=pltpu.SMEM),
            pl.BlockSpec(memory_space=pltpu.VMEM),
            pl.BlockSpec(memory_space=pltpu.VMEM),
            pl.BlockSpec(memory_space=pl.ANY),
        ],
        out_specs=pl.BlockSpec(memory_space=pltpu.VMEM),
        scratch_shapes=[
            pltpu.VMEM((rows, kv_width), kv_cache.dtype),
            pltpu.VMEM((rows, kv_width), kv_cache.dtype),
            pltpu.SemaphoreType.DMA((2, rows // CHUNK_ROWS)),
        ],
        cost_estimate=pl.CostEstimate(
            flops=4 * kv_heads * slot_count * group_width * rows * HEAD_SIZE,
            transcendentals=kv_heads * slot_count * group_width * rows,
            bytes_accessed=2 * rows * kv_width * 2,
        ),
    )(lengths, query_rows, fresh, kv_cache)
    return jnp.transpose(
        out.reshape(kv_heads, slot_count, group_width, HEAD_SIZE), (1, 0, 2, 3)
    ).reshape(slot_count, kv_heads * group_width * HEAD_SIZE)


def slot_bounds(lengths):
    span_sizes = lengths + 1
    first_rows = jnp.cumsum(span_sizes) - span_sizes
    return (first_rows, first_rows + span_sizes)


def attend_rows(query_rows, key_value_store, row_base, first_rows, end_rows):
    block_rows = 128
    slot_count, kv_heads, group_width, head_dim = query_rows.shape
    pool_rows = key_value_store.shape[1]
    key_table = key_value_store[0].reshape(pool_rows, kv_heads, head_dim)
    value_table = key_value_store[1].reshape(pool_rows, kv_heads, head_dim)
    needed = jnp.clip(jnp.max(end_rows) - row_base, 0, pool_rows)
    block_count = (needed + block_rows - 1) // block_rows
    score_scale = head_dim ** (-0.5)

    def advance(block_index, carried):
        running_max, denominator, accumulated = carried
        offset = block_index * block_rows
        key_block = lax.dynamic_slice_in_dim(key_table, offset, block_rows, 0)
        value_block = lax.dynamic_slice_in_dim(value_table, offset, block_rows, 0)
        scores = (
            jnp.einsum("sngd,tnd->sngt", query_rows, key_block, preferred_element_type=jnp.float32)
            * score_scale
        )
        row_ids = row_base + offset + jnp.arange(block_rows, dtype=jnp.int32)
        inside = (
            (row_ids[None, :] >= first_rows[:, None]) & (row_ids[None, :] < end_rows[:, None])
        )[:, None, None, :]
        scores = jnp.where(inside, scores, NEGATIVE_FILL)
        new_max = jnp.maximum(running_max, jnp.max(scores, axis=-1))
        weights = jnp.where(inside, jnp.exp(scores - new_max[..., None]), 0.0)
        factor = jnp.exp(running_max - new_max)
        denominator = denominator * factor + jnp.sum(weights, axis=-1)
        accumulated = accumulated * factor[..., None] + jnp.einsum(
            "sngt,tnd->sngd",
            weights.astype(jnp.bfloat16),
            value_block,
            preferred_element_type=jnp.float32,
        )
        return (new_max, denominator, accumulated)

    initial = (
        jnp.full((slot_count, kv_heads, group_width), NEGATIVE_FILL, jnp.float32),
        jnp.zeros((slot_count, kv_heads, group_width), jnp.float32),
        jnp.zeros((slot_count, kv_heads, group_width, head_dim), jnp.float32),
    )
    return lax.fori_loop(0, block_count, advance, initial)


def body(
    lengths,
    assignment,
    query,
    key_value_fresh,
    kv_cache,
    hidden_in,
    out_weight,
    norm_gain,
    gate_up_weight,
    down_weight,
):
    slot_count = lengths.shape[0]
    first_rows, end_rows = slot_bounds(lengths)
    key_value_store = kv_cache
    for slot_index in range(slot_count):
        key_value_store = lax.dynamic_update_slice(
            key_value_store,
            key_value_fresh[:, slot_index : slot_index + 1, :],
            (jnp.int32(0), end_rows[slot_index] - 1, jnp.int32(0)),
        )
    kv_heads = key_value_store.shape[2] // HEAD_SIZE
    group_width = QUERY_HEADS // KEY_VALUE_HEADS
    attended = attend_kernel(lengths, query, key_value_fresh, kv_cache)
    y_count, mdl_count = lax.axis_size("y"), lax.axis_size("mdl")
    weight_copies = jnp.broadcast_to(out_weight.T[None], (y_count,) + out_weight.T.shape)
    row_weight = lax.all_to_all(weight_copies, "y", 0, 0, tiled=True).reshape(-1, out_weight.shape[0])
    flat = attended.reshape(-1, 128)
    flat = lax.all_gather(flat, "c", axis=0, tiled=True)
    flat = lax.all_gather(flat, "z", axis=0, tiled=True)
    row_attended = flat.reshape(-1, attended.shape[1])
    row_slots = row_attended.shape[0]
    sub_width = hidden_in.shape[1]
    row_projected = lax.dot_general(
        row_weight, row_attended, (((1,), (1,)), ((), ())), preferred_element_type=jnp.float32
    )
    outgoing = row_projected.astype(jnp.bfloat16).reshape(y_count * mdl_count, sub_width, row_slots)
    arrived = lax.all_to_all(outgoing, ("y", "mdl"), 0, 0, tiled=True)
    head_sum = arrived.astype(jnp.float32).reshape(y_count, mdl_count, sub_width, row_slots).sum(1)
    head_share = jnp.transpose(head_sum, (1, 0, 2)).reshape(sub_width, y_count * row_slots).T
    total_rows = assignment.shape[0]
    inverse = (
        jnp.zeros((total_rows,), jnp.int32)
        .at[assignment]
        .set(jnp.arange(total_rows, dtype=jnp.int32))
    )
    placed = jnp.take(head_share, inverse, axis=0)
    residual_wide = hidden_in.astype(jnp.float32) + placed
    residual = residual_wide.astype(jnp.bfloat16)
    local_wide = residual.astype(jnp.float32)
    col_groups = gate_up_weight.shape[1]
    sub_width = hidden_in.shape[1]
    gathered = jnp.transpose(gather_rows(residual.T), (2, 0, 1)).reshape(total_rows, col_groups * sub_width)
    widened = gathered.astype(jnp.float32)
    own_squares = jnp.sum(widened * widened, axis=1)
    gain_table = norm_gain.reshape(col_groups, lax.axis_size("mdl"), sub_width)
    gain_cols = lax.dynamic_index_in_dim(
        gain_table, lax.axis_index("mdl"), 1, keepdims=False
    ).reshape(col_groups * sub_width)
    unscaled = (widened * gain_cols).astype(jnp.bfloat16)
    gate_up = gate_up_weight.reshape(2, col_groups * sub_width, gate_up_weight.shape[4])
    partial_value = jnp.einsum("rk,gkf->gfr", unscaled, gate_up, preferred_element_type=jnp.float32)
    units = partial_value.shape[1]
    mdl_count = lax.axis_size("mdl")
    quarter = units // mdl_count
    squares_high = own_squares.astype(jnp.bfloat16)
    squares_low = (own_squares - squares_high.astype(jnp.float32)).astype(jnp.bfloat16)
    squares_pair = jnp.broadcast_to(jnp.stack([squares_high, squares_low])[None], (mdl_count, 2, total_rows))
    blocks = jnp.transpose(
        partial_value.astype(jnp.bfloat16).reshape(2, mdl_count, quarter, total_rows), (1, 0, 2, 3)
    ).reshape(mdl_count, 2 * quarter, total_rows)
    payload = jnp.concatenate([blocks, squares_pair], axis=1)
    summed_payload = lax.all_to_all(payload, "mdl", 0, 0, tiled=True).astype(jnp.float32).sum(0)
    square_sum = summed_payload[2 * quarter] + summed_payload[2 * quarter + 1]
    scale = lax.rsqrt(square_sum / D + 1e-05)
    gate_part = summed_payload[:quarter] * scale[None, :]
    up_part = summed_payload[quarter : 2 * quarter] * scale[None, :]
    hidden_part = (jax.nn.silu(gate_part) * up_part).astype(jnp.bfloat16)
    hidden_copies = jnp.broadcast_to(hidden_part[None], (mdl_count,) + hidden_part.shape)
    hidden = lax.all_to_all(hidden_copies, "mdl", 0, 0, tiled=True).reshape(units, total_rows)
    columns = down_weight.reshape(down_weight.shape[0], col_groups * sub_width)
    lowered = lax.dot_general(
        columns, hidden, (((0,), (0,)), ((), ())), preferred_element_type=jnp.float32
    )
    mesh_shape = (lax.axis_size("y"), lax.axis_size("z"), lax.axis_size("c"))
    summed = scatter_sum(lowered.reshape(mesh_shape + (sub_width * total_rows // 128, 128))).reshape(sub_width, total_rows)
    layer_out = (local_wide + summed.T).astype(jnp.bfloat16)
    return (layer_out, key_value_store)


def solution(mesh):
    req_size, mdl_size = mesh.devices.shape
    chips_y = 4
    split = Mesh(
        mesh.devices.reshape(chips_y, req_size // (2 * chips_y), 2, mdl_size),
        REQ + ("mdl",),
    )
    return jax.shard_map(
        body,
        mesh=split,
        in_specs=(
            P(REQ),
            P(),
            P(REQ, "mdl"),
            P(None, REQ, "mdl"),
            P(None, REQ, "mdl"),
            P(None, (REQ + ("mdl",))),
            P("mdl", REQ),
            P(),
            P(None, None, "mdl", None, REQ),
            P(REQ, None, "mdl", None),
        ),
        out_specs=(P(None, REQ + ("mdl",)), P(None, REQ, "mdl")),
        check_vma=False,
    )
```

```python
import jax
import jax.numpy as jnp
from jax import lax
from jax.experimental import pallas as pl
from jax.experimental.pallas import tpu as pltpu
from jax.sharding import Mesh, PartitionSpec as P

D = 5120
QUERY_HEADS = 32
KEY_VALUE_HEADS = 8
HEAD_SIZE = 128


NEGATIVE_FILL = -1e30
REQ = ("y", "z", "c")


def gather_rows(part):
    count = lax.axis_size(REQ)
    flat = part.reshape(-1, 128)
    flat = lax.all_gather(flat, "c", axis=0, tiled=True)
    flat = lax.all_gather(flat, "z", axis=0, tiled=True)
    copies = jnp.broadcast_to(flat[None], (lax.axis_size("y"),) + flat.shape)
    return lax.all_to_all(copies, "y", 0, 0, tiled=True).reshape((count,) + part.shape)


def scatter_sum(parts):
    wide = None
    for position, name in ((2, "c"), (0, "y"), (1, "z")):
        moved = lax.all_to_all(parts.astype(jnp.bfloat16), name, position, position, tiled=True)
        wide = moved.astype(jnp.float32).sum(position, keepdims=True)
        parts = wide
    return wide


def mdl_sum(values, wires):
    count = lax.axis_size("mdl")
    sent = tuple(v.astype(w) for v, w in zip(values, wires))
    totals = [v.astype(jnp.float32) for v in values]
    for shift in range(1, count):
        pairs = [(i, (i + shift) % count) for i in range(count)]
        arrived = lax.ppermute(sent, "mdl", pairs)
        totals = [t + a.astype(jnp.float32) for t, a in zip(totals, arrived)]
    return totals


def mdl_scatter_sum(value, wire):
    count = lax.axis_size("mdl")
    height = value.shape[0] // count
    blocks = value.astype(wire).reshape((count, height * value.shape[1] // 128, 128))
    moved = lax.all_to_all(blocks, "mdl", 0, 0, tiled=True)
    return moved.astype(jnp.float32).sum(0).reshape(height, value.shape[1])


CHUNK_ROWS = 256


def attention_kernel(
    lengths_ref, query_ref, fresh_ref, cache_hbm, fresh_rows, out_ref, store_hbm, keys, values, sems, write_sems
):
    rows = keys.shape[0]
    chunks = rows // CHUNK_ROWS
    copies = []
    for chunk in range(chunks):
        window = pl.ds(chunk * CHUNK_ROWS, CHUNK_ROWS)
        for which, target in ((0, keys), (1, values)):
            copy = pltpu.make_async_copy(cache_hbm.at[which, window], target.at[window], sems.at[which, chunk])
            copy.start()
            copies.append(copy)
    slot_count = lengths_ref.shape[0]
    kv_heads, row_count, head_dim = query_ref.shape
    group_width = row_count // slot_count
    row_slot = lax.broadcasted_iota(jnp.int32, (row_count, 1), 0) // group_width
    first = jnp.zeros((row_count, 1), jnp.int32)
    end = jnp.zeros((row_count, 1), jnp.int32)
    start = jnp.int32(0)
    for slot in range(slot_count):
        length = lengths_ref[slot]
        first = jnp.where(row_slot == slot, start, first)
        end = jnp.where(row_slot == slot, start + length, end)
        start = start + length + 1
    columns = lax.broadcasted_iota(jnp.int32, (row_count, rows), 1)
    inside = (columns >= first) & (columns < end)
    pick = (lax.broadcasted_iota(jnp.int32, (row_count, slot_count), 1) == row_slot)
    for copy in copies:
        copy.wait()
    tile = 16
    within = lax.broadcasted_iota(jnp.int32, (tile, keys.shape[1]), 0)
    start = jnp.int32(0)
    for slot in range(slot_count):
        row = start + lengths_ref[slot]
        base = pl.multiple_of((row // tile) * tile, tile)
        for which, target in ((0, keys), (1, values)):
            block = target[pl.ds(base, tile), :]
            fresh_row = jnp.broadcast_to(fresh_rows[which, pl.ds(slot, 1), :], block.shape)
            target[pl.ds(base, tile), :] = jnp.where(within == row - base, fresh_row, block)
        start = row + 1
    writes = []
    for which, source in ((0, keys), (1, values)):
        write = pltpu.make_async_copy(source, store_hbm.at[which], write_sems.at[which])
        write.start()
        writes.append(write)
    score_scale = head_dim ** (-0.5)
    for head in range(kv_heads):
        lanes = pl.ds(head * head_dim, head_dim)
        query_rows = query_ref[head]
        scores = lax.dot_general(
            query_rows, keys[:, lanes], (((1,), (1,)), ((), ())), preferred_element_type=jnp.float32
        ) * score_scale
        fresh_scores = lax.dot_general(
            query_rows, fresh_ref[0, head], (((1,), (1,)), ((), ())), preferred_element_type=jnp.float32
        ) * score_scale
        new_score = jnp.sum(jnp.where(pick, fresh_scores, 0.0), axis=1, keepdims=True)
        scores = jnp.where(inside, scores, NEGATIVE_FILL)
        top = jnp.maximum(jnp.max(scores, axis=1, keepdims=True), new_score)
        weights = jnp.where(inside, jnp.exp(scores - top), 0.0)
        new_weight = jnp.exp(new_score - top)
        denominator = jnp.sum(weights, axis=1, keepdims=True) + new_weight
        mixed = jnp.dot(weights.astype(jnp.bfloat16), values[:, lanes], preferred_element_type=jnp.float32)
        fresh_values = jnp.dot(pick.astype(jnp.bfloat16), fresh_ref[1, head], preferred_element_type=jnp.float32)
        mixed = mixed + new_weight.astype(jnp.bfloat16).astype(jnp.float32) * fresh_values
        out_ref[head] = (mixed / denominator).astype(out_ref.dtype)
    for write in writes:
        write.wait()


def attend_kernel(lengths, query, key_value_fresh, kv_cache):
    slot_count = lengths.shape[0]
    kv_width = kv_cache.shape[2]
    kv_heads = kv_width // HEAD_SIZE
    group_width = QUERY_HEADS // KEY_VALUE_HEADS
    rows = kv_cache.shape[1]
    query_rows = jnp.transpose(
        query.reshape(slot_count, kv_heads, group_width, HEAD_SIZE), (1, 0, 2, 3)
    ).reshape(kv_heads, slot_count * group_width, HEAD_SIZE)
    fresh = jnp.transpose(
        key_value_fresh.reshape(2, slot_count, kv_heads, HEAD_SIZE), (0, 2, 1, 3)
    )
    out, store = pl.pallas_call(
        attention_kernel,
        out_shape=(
            jax.ShapeDtypeStruct(query_rows.shape, jnp.bfloat16),
            jax.ShapeDtypeStruct(kv_cache.shape, kv_cache.dtype),
        ),
        in_specs=[
            pl.BlockSpec(memory_space=pltpu.SMEM),
            pl.BlockSpec(memory_space=pltpu.VMEM),
            pl.BlockSpec(memory_space=pltpu.VMEM),
            pl.BlockSpec(memory_space=pl.ANY),
            pl.BlockSpec(memory_space=pltpu.VMEM),
        ],
        out_specs=(pl.BlockSpec(memory_space=pltpu.VMEM), pl.BlockSpec(memory_space=pl.ANY)),
        scratch_shapes=[
            pltpu.VMEM((rows, kv_width), kv_cache.dtype),
            pltpu.VMEM((rows, kv_width), kv_cache.dtype),
            pltpu.SemaphoreType.DMA((2, rows // CHUNK_ROWS)),
            pltpu.SemaphoreType.DMA((2,)),
        ],
        cost_estimate=pl.CostEstimate(
            flops=4 * kv_heads * slot_count * group_width * rows * HEAD_SIZE,
            transcendentals=kv_heads * slot_count * group_width * rows,
            bytes_accessed=2 * rows * kv_width * 2,
        ),
    )(lengths, query_rows, fresh, kv_cache, key_value_fresh)
    return store, jnp.transpose(
        out.reshape(kv_heads, slot_count, group_width, HEAD_SIZE), (1, 0, 2, 3)
    ).reshape(slot_count, kv_heads * group_width * HEAD_SIZE)


def slot_bounds(lengths):
    span_sizes = lengths + 1
    first_rows = jnp.cumsum(span_sizes) - span_sizes
    return (first_rows, first_rows + span_sizes)


def attend_rows(query_rows, key_value_store, row_base, first_rows, end_rows):
    block_rows = 128
    slot_count, kv_heads, group_width, head_dim = query_rows.shape
    pool_rows = key_value_store.shape[1]
    key_table = key_value_store[0].reshape(pool_rows, kv_heads, head_dim)
    value_table = key_value_store[1].reshape(pool_rows, kv_heads, head_dim)
    needed = jnp.clip(jnp.max(end_rows) - row_base, 0, pool_rows)
    block_count = (needed + block_rows - 1) // block_rows
    score_scale = head_dim ** (-0.5)

    def advance(block_index, carried):
        running_max, denominator, accumulated = carried
        offset = block_index * block_rows
        key_block = lax.dynamic_slice_in_dim(key_table, offset, block_rows, 0)
        value_block = lax.dynamic_slice_in_dim(value_table, offset, block_rows, 0)
        scores = (
            jnp.einsum("sngd,tnd->sngt", query_rows, key_block, preferred_element_type=jnp.float32)
            * score_scale
        )
        row_ids = row_base + offset + jnp.arange(block_rows, dtype=jnp.int32)
        inside = (
            (row_ids[None, :] >= first_rows[:, None]) & (row_ids[None, :] < end_rows[:, None])
        )[:, None, None, :]
        scores = jnp.where(inside, scores, NEGATIVE_FILL)
        new_max = jnp.maximum(running_max, jnp.max(scores, axis=-1))
        weights = jnp.where(inside, jnp.exp(scores - new_max[..., None]), 0.0)
        factor = jnp.exp(running_max - new_max)
        denominator = denominator * factor + jnp.sum(weights, axis=-1)
        accumulated = accumulated * factor[..., None] + jnp.einsum(
            "sngt,tnd->sngd",
            weights.astype(jnp.bfloat16),
            value_block,
            preferred_element_type=jnp.float32,
        )
        return (new_max, denominator, accumulated)

    initial = (
        jnp.full((slot_count, kv_heads, group_width), NEGATIVE_FILL, jnp.float32),
        jnp.zeros((slot_count, kv_heads, group_width), jnp.float32),
        jnp.zeros((slot_count, kv_heads, group_width, head_dim), jnp.float32),
    )
    return lax.fori_loop(0, block_count, advance, initial)


def body(
    lengths,
    assignment,
    query,
    key_value_fresh,
    kv_cache,
    hidden_in,
    out_weight,
    norm_gain,
    gate_up_weight,
    down_weight,
):
    slot_count = lengths.shape[0]
    first_rows, end_rows = slot_bounds(lengths)
    key_value_store, attended = attend_kernel(lengths, query, key_value_fresh, kv_cache)
    y_count, mdl_count = lax.axis_size("y"), lax.axis_size("mdl")
    weight_copies = jnp.broadcast_to(out_weight.T[None], (y_count,) + out_weight.T.shape)
    row_weight = lax.all_to_all(weight_copies, "y", 0, 0, tiled=True).reshape(-1, out_weight.shape[0])
    flat = attended.reshape(-1, 128)
    flat = lax.all_gather(flat, "c", axis=0, tiled=True)
    flat = lax.all_gather(flat, "z", axis=0, tiled=True)
    row_attended = flat.reshape(-1, attended.shape[1])
    row_slots = row_attended.shape[0]
    sub_width = hidden_in.shape[1]
    row_projected = lax.dot_general(
        row_weight, row_attended, (((1,), (1,)), ((), ())), preferred_element_type=jnp.float32
    )
    outgoing = row_projected.astype(jnp.bfloat16).reshape(y_count * mdl_count, sub_width, row_slots)
    arrived = lax.all_to_all(outgoing, ("y", "mdl"), 0, 0, tiled=True)
    head_sum = arrived.astype(jnp.float32).reshape(y_count, mdl_count, sub_width, row_slots).sum(1)
    head_share = jnp.transpose(head_sum, (1, 0, 2)).reshape(sub_width, y_count * row_slots).T
    total_rows = assignment.shape[0]
    inverse = (
        jnp.zeros((total_rows,), jnp.int32)
        .at[assignment]
        .set(jnp.arange(total_rows, dtype=jnp.int32))
    )
    placed = jnp.take(head_share, inverse, axis=0)
    residual_wide = hidden_in.astype(jnp.float32) + placed
    residual = residual_wide.astype(jnp.bfloat16)
    local_wide = residual.astype(jnp.float32)
    col_groups = gate_up_weight.shape[1]
    sub_width = hidden_in.shape[1]
    gathered = jnp.transpose(gather_rows(residual.T), (2, 0, 1)).reshape(total_rows, col_groups * sub_width)
    widened = gathered.astype(jnp.float32)
    own_squares = jnp.sum(widened * widened, axis=1)
    gain_table = norm_gain.reshape(col_groups, lax.axis_size("mdl"), sub_width)
    gain_cols = lax.dynamic_index_in_dim(
        gain_table, lax.axis_index("mdl"), 1, keepdims=False
    ).reshape(col_groups * sub_width)
    unscaled = (widened * gain_cols).astype(jnp.bfloat16)
    gate_up = gate_up_weight.reshape(2, col_groups * sub_width, gate_up_weight.shape[4])
    partial_value = jnp.einsum("rk,gkf->gfr", unscaled, gate_up, preferred_element_type=jnp.float32)
    units = partial_value.shape[1]
    mdl_count = lax.axis_size("mdl")
    quarter = units // mdl_count
    squares_high = own_squares.astype(jnp.bfloat16)
    squares_low = (own_squares - squares_high.astype(jnp.float32)).astype(jnp.bfloat16)
    squares_pair = jnp.broadcast_to(jnp.stack([squares_high, squares_low])[None], (mdl_count, 2, total_rows))
    blocks = jnp.transpose(
        partial_value.astype(jnp.bfloat16).reshape(2, mdl_count, quarter, total_rows), (1, 0, 2, 3)
    ).reshape(mdl_count, 2 * quarter, total_rows)
    payload = jnp.concatenate([blocks, squares_pair], axis=1)
    summed_payload = lax.all_to_all(payload, "mdl", 0, 0, tiled=True).astype(jnp.float32).sum(0)
    square_sum = summed_payload[2 * quarter] + summed_payload[2 * quarter + 1]
    scale = lax.rsqrt(square_sum / D + 1e-05)
    gate_part = summed_payload[:quarter] * scale[None, :]
    up_part = summed_payload[quarter : 2 * quarter] * scale[None, :]
    hidden_part = (jax.nn.silu(gate_part) * up_part).astype(jnp.bfloat16)
    hidden_copies = jnp.broadcast_to(hidden_part[None], (mdl_count,) + hidden_part.shape)
    hidden = lax.all_to_all(hidden_copies, "mdl", 0, 0, tiled=True).reshape(units, total_rows)
    columns = down_weight.reshape(down_weight.shape[0], col_groups * sub_width)
    lowered = lax.dot_general(
        columns, hidden, (((0,), (0,)), ((), ())), preferred_element_type=jnp.float32
    )
    mesh_shape = (lax.axis_size("y"), lax.axis_size("z"), lax.axis_size("c"))
    summed = scatter_sum(lowered.reshape(mesh_shape + (sub_width * total_rows // 128, 128))).reshape(sub_width, total_rows)
    layer_out = (local_wide + summed.T).astype(jnp.bfloat16)
    return (layer_out, key_value_store)


def solution(mesh):
    req_size, mdl_size = mesh.devices.shape
    chips_y = 4
    split = Mesh(
        mesh.devices.reshape(chips_y, req_size // (2 * chips_y), 2, mdl_size),
        REQ + ("mdl",),
    )
    return jax.shard_map(
        body,
        mesh=split,
        in_specs=(
            P(REQ),
            P(),
            P(REQ, "mdl"),
            P(None, REQ, "mdl"),
            P(None, REQ, "mdl"),
            P(None, (REQ + ("mdl",))),
            P("mdl", REQ),
            P(),
            P(None, None, "mdl", None, REQ),
            P(REQ, None, "mdl", None),
        ),
        out_specs=(P(None, REQ + ("mdl",)), P(None, REQ, "mdl")),
        check_vma=False,
    )
```

```python
import jax
import jax.numpy as jnp
from jax import lax
from jax.experimental import pallas as pl
from jax.experimental.pallas import tpu as pltpu
from jax.sharding import Mesh, PartitionSpec as P

D = 5120
QUERY_HEADS = 32
KEY_VALUE_HEADS = 8
HEAD_SIZE = 128


NEGATIVE_FILL = -1e30
REQ = ("y", "z", "c")


def gather_rows(part):
    count = lax.axis_size(REQ)
    flat = part.reshape(-1, 128)
    flat = lax.all_gather(flat, "c", axis=0, tiled=True)
    flat = lax.all_gather(flat, "z", axis=0, tiled=True)
    copies = jnp.broadcast_to(flat[None], (lax.axis_size("y"),) + flat.shape)
    return lax.all_to_all(copies, "y", 0, 0, tiled=True).reshape((count,) + part.shape)


def scatter_sum(parts):
    wide = None
    for position, name in ((2, "c"), (0, "y"), (1, "z")):
        moved = lax.all_to_all(parts.astype(jnp.bfloat16), name, position, position, tiled=True)
        wide = moved.astype(jnp.float32).sum(position, keepdims=True)
        parts = wide
    return wide


def mdl_sum(values, wires):
    count = lax.axis_size("mdl")
    sent = tuple(v.astype(w) for v, w in zip(values, wires))
    totals = [v.astype(jnp.float32) for v in values]
    for shift in range(1, count):
        pairs = [(i, (i + shift) % count) for i in range(count)]
        arrived = lax.ppermute(sent, "mdl", pairs)
        totals = [t + a.astype(jnp.float32) for t, a in zip(totals, arrived)]
    return totals


def mdl_scatter_sum(value, wire):
    count = lax.axis_size("mdl")
    height = value.shape[0] // count
    blocks = value.astype(wire).reshape((count, height * value.shape[1] // 128, 128))
    moved = lax.all_to_all(blocks, "mdl", 0, 0, tiled=True)
    return moved.astype(jnp.float32).sum(0).reshape(height, value.shape[1])


CHUNK_ROWS = 256


def attention_kernel(
    lengths_ref, query_ref, fresh_ref, cache_hbm, fresh_rows, out_ref, store_hbm, keys, values, sems, write_sems
):
    rows = keys.shape[0]
    chunks = rows // CHUNK_ROWS
    copies = []
    for chunk in range(chunks):
        window = pl.ds(chunk * CHUNK_ROWS, CHUNK_ROWS)
        for which, target in ((0, keys), (1, values)):
            copy = pltpu.make_async_copy(cache_hbm.at[which, window], target.at[window], sems.at[which, chunk])
            copy.start()
            copies.append(copy)
    slot_count = lengths_ref.shape[0]
    kv_heads, row_count, head_dim = query_ref.shape
    group_width = row_count // slot_count
    row_slot = lax.broadcasted_iota(jnp.int32, (row_count, 1), 0) // group_width
    first = jnp.zeros((row_count, 1), jnp.int32)
    end = jnp.zeros((row_count, 1), jnp.int32)
    start = jnp.int32(0)
    for slot in range(slot_count):
        length = lengths_ref[slot]
        first = jnp.where(row_slot == slot, start, first)
        end = jnp.where(row_slot == slot, start + length, end)
        start = start + length + 1
    columns = lax.broadcasted_iota(jnp.int32, (row_count, rows), 1)
    inside = (columns >= first) & (columns < end)
    pick = (lax.broadcasted_iota(jnp.int32, (row_count, slot_count), 1) == row_slot)
    for copy in copies:
        copy.wait()
    tile = 16
    within = lax.broadcasted_iota(jnp.int32, (tile, keys.shape[1]), 0)
    start = jnp.int32(0)
    for slot in range(slot_count):
        row = start + lengths_ref[slot]
        base = pl.multiple_of((row // tile) * tile, tile)
        for which, target in ((0, keys), (1, values)):
            block = target[pl.ds(base, tile), :]
            fresh_row = jnp.broadcast_to(fresh_rows[which, pl.ds(slot, 1), :], block.shape)
            target[pl.ds(base, tile), :] = jnp.where(within == row - base, fresh_row, block)
        start = row + 1
    writes = []
    for which, source in ((0, keys), (1, values)):
        write = pltpu.make_async_copy(source, store_hbm.at[which], write_sems.at[which])
        write.start()
        writes.append(write)
    score_scale = head_dim ** (-0.5)
    for head in range(kv_heads):
        lanes = pl.ds(head * head_dim, head_dim)
        query_rows = query_ref[head]
        scores = lax.dot_general(
            query_rows, keys[:, lanes], (((1,), (1,)), ((), ())), preferred_element_type=jnp.float32
        ) * score_scale
        fresh_scores = lax.dot_general(
            query_rows, fresh_ref[0, head], (((1,), (1,)), ((), ())), preferred_element_type=jnp.float32
        ) * score_scale
        new_score = jnp.sum(jnp.where(pick, fresh_scores, 0.0), axis=1, keepdims=True)
        scores = jnp.where(inside, scores, NEGATIVE_FILL)
        top = jnp.maximum(jnp.max(scores, axis=1, keepdims=True), new_score)
        weights = jnp.where(inside, jnp.exp(scores - top), 0.0)
        new_weight = jnp.exp(new_score - top)
        denominator = jnp.sum(weights, axis=1, keepdims=True) + new_weight
        mixed = jnp.dot(weights.astype(jnp.bfloat16), values[:, lanes], preferred_element_type=jnp.float32)
        fresh_values = jnp.dot(pick.astype(jnp.bfloat16), fresh_ref[1, head], preferred_element_type=jnp.float32)
        mixed = mixed + new_weight.astype(jnp.bfloat16).astype(jnp.float32) * fresh_values
        out_ref[head] = (mixed / denominator).astype(out_ref.dtype)
    for write in writes:
        write.wait()


def attend_kernel(lengths, query, key_value_fresh, kv_cache):
    slot_count = lengths.shape[0]
    kv_width = kv_cache.shape[2]
    kv_heads = kv_width // HEAD_SIZE
    group_width = QUERY_HEADS // KEY_VALUE_HEADS
    rows = kv_cache.shape[1]
    query_rows = jnp.transpose(
        query.reshape(slot_count, kv_heads, group_width, HEAD_SIZE), (1, 0, 2, 3)
    ).reshape(kv_heads, slot_count * group_width, HEAD_SIZE)
    fresh = jnp.transpose(
        key_value_fresh.reshape(2, slot_count, kv_heads, HEAD_SIZE), (0, 2, 1, 3)
    )
    out, store = pl.pallas_call(
        attention_kernel,
        out_shape=(
            jax.ShapeDtypeStruct(query_rows.shape, jnp.bfloat16),
            jax.ShapeDtypeStruct(kv_cache.shape, kv_cache.dtype),
        ),
        in_specs=[
            pl.BlockSpec(memory_space=pltpu.SMEM),
            pl.BlockSpec(memory_space=pltpu.VMEM),
            pl.BlockSpec(memory_space=pltpu.VMEM),
            pl.BlockSpec(memory_space=pl.ANY),
            pl.BlockSpec(memory_space=pltpu.VMEM),
        ],
        out_specs=(pl.BlockSpec(memory_space=pltpu.VMEM), pl.BlockSpec(memory_space=pl.ANY)),
        scratch_shapes=[
            pltpu.VMEM((rows, kv_width), kv_cache.dtype),
            pltpu.VMEM((rows, kv_width), kv_cache.dtype),
            pltpu.SemaphoreType.DMA((2, rows // CHUNK_ROWS)),
            pltpu.SemaphoreType.DMA((2,)),
        ],
        cost_estimate=pl.CostEstimate(
            flops=4 * kv_heads * slot_count * group_width * rows * HEAD_SIZE,
            transcendentals=kv_heads * slot_count * group_width * rows,
            bytes_accessed=2 * rows * kv_width * 2,
        ),
    )(lengths, query_rows, fresh, kv_cache, key_value_fresh)
    return store, jnp.transpose(
        out.reshape(kv_heads, slot_count, group_width, HEAD_SIZE), (1, 0, 2, 3)
    ).reshape(slot_count, kv_heads * group_width * HEAD_SIZE)


def slot_bounds(lengths):
    span_sizes = lengths + 1
    first_rows = jnp.cumsum(span_sizes) - span_sizes
    return (first_rows, first_rows + span_sizes)


def attend_rows(query_rows, key_value_store, row_base, first_rows, end_rows):
    block_rows = 128
    slot_count, kv_heads, group_width, head_dim = query_rows.shape
    pool_rows = key_value_store.shape[1]
    key_table = key_value_store[0].reshape(pool_rows, kv_heads, head_dim)
    value_table = key_value_store[1].reshape(pool_rows, kv_heads, head_dim)
    needed = jnp.clip(jnp.max(end_rows) - row_base, 0, pool_rows)
    block_count = (needed + block_rows - 1) // block_rows
    score_scale = head_dim ** (-0.5)

    def advance(block_index, carried):
        running_max, denominator, accumulated = carried
        offset = block_index * block_rows
        key_block = lax.dynamic_slice_in_dim(key_table, offset, block_rows, 0)
        value_block = lax.dynamic_slice_in_dim(value_table, offset, block_rows, 0)
        scores = (
            jnp.einsum("sngd,tnd->sngt", query_rows, key_block, preferred_element_type=jnp.float32)
            * score_scale
        )
        row_ids = row_base + offset + jnp.arange(block_rows, dtype=jnp.int32)
        inside = (
            (row_ids[None, :] >= first_rows[:, None]) & (row_ids[None, :] < end_rows[:, None])
        )[:, None, None, :]
        scores = jnp.where(inside, scores, NEGATIVE_FILL)
        new_max = jnp.maximum(running_max, jnp.max(scores, axis=-1))
        weights = jnp.where(inside, jnp.exp(scores - new_max[..., None]), 0.0)
        factor = jnp.exp(running_max - new_max)
        denominator = denominator * factor + jnp.sum(weights, axis=-1)
        accumulated = accumulated * factor[..., None] + jnp.einsum(
            "sngt,tnd->sngd",
            weights.astype(jnp.bfloat16),
            value_block,
            preferred_element_type=jnp.float32,
        )
        return (new_max, denominator, accumulated)

    initial = (
        jnp.full((slot_count, kv_heads, group_width), NEGATIVE_FILL, jnp.float32),
        jnp.zeros((slot_count, kv_heads, group_width), jnp.float32),
        jnp.zeros((slot_count, kv_heads, group_width, head_dim), jnp.float32),
    )
    return lax.fori_loop(0, block_count, advance, initial)


def body(
    lengths,
    assignment,
    query,
    key_value_fresh,
    kv_cache,
    hidden_in,
    out_weight,
    norm_gain,
    gate_up_weight,
    down_weight,
):
    slot_count = lengths.shape[0]
    first_rows, end_rows = slot_bounds(lengths)
    key_value_store, attended = attend_kernel(lengths, query, key_value_fresh, kv_cache)
    y_count, mdl_count = lax.axis_size("y"), lax.axis_size("mdl")
    weight_copies = jnp.broadcast_to(out_weight.T[None], (y_count,) + out_weight.T.shape)
    row_weight = lax.all_to_all(weight_copies, "y", 0, 0, tiled=True).reshape(-1, out_weight.shape[0])
    flat = attended.reshape(-1, 128)
    flat = lax.all_gather(flat, "c", axis=0, tiled=True)
    flat = lax.all_gather(flat, "z", axis=0, tiled=True)
    row_attended = flat.reshape(-1, attended.shape[1])
    row_slots = row_attended.shape[0]
    sub_width = hidden_in.shape[1]
    row_projected = lax.dot_general(
        row_weight, row_attended, (((1,), (1,)), ((), ())), preferred_element_type=jnp.float32
    )
    outgoing = row_projected.astype(jnp.bfloat16).reshape(y_count * mdl_count, sub_width, row_slots)
    arrived = lax.all_to_all(outgoing, ("y", "mdl"), 0, 0, tiled=True)
    head_sum = arrived.astype(jnp.float32).reshape(y_count, mdl_count, sub_width, row_slots).sum(1)
    head_share = jnp.transpose(head_sum, (1, 0, 2)).reshape(sub_width, y_count * row_slots).T
    total_rows = assignment.shape[0]
    selection = (
        assignment[:, None] == lax.broadcasted_iota(jnp.int32, (total_rows, total_rows), 1)
    ).astype(jnp.float32)
    placed = lax.dot_general(
        selection,
        head_share,
        (((0,), (0,)), ((), ())),
        precision=lax.Precision.HIGHEST,
        preferred_element_type=jnp.float32,
    )
    residual_wide = hidden_in.astype(jnp.float32) + placed
    residual = residual_wide.astype(jnp.bfloat16)
    local_wide = residual.astype(jnp.float32)
    col_groups = gate_up_weight.shape[1]
    sub_width = hidden_in.shape[1]
    gathered = jnp.transpose(gather_rows(residual.T), (2, 0, 1)).reshape(total_rows, col_groups * sub_width)
    widened = gathered.astype(jnp.float32)
    own_squares = jnp.sum(widened * widened, axis=1)
    gain_table = norm_gain.reshape(col_groups, lax.axis_size("mdl"), sub_width)
    gain_cols = lax.dynamic_index_in_dim(
        gain_table, lax.axis_index("mdl"), 1, keepdims=False
    ).reshape(col_groups * sub_width)
    unscaled = (widened * gain_cols).astype(jnp.bfloat16)
    gate_up = gate_up_weight.reshape(2, col_groups * sub_width, gate_up_weight.shape[4])
    partial_value = jnp.einsum("rk,gkf->gfr", unscaled, gate_up, preferred_element_type=jnp.float32)
    units = partial_value.shape[1]
    mdl_count = lax.axis_size("mdl")
    quarter = units // mdl_count
    squares_high = own_squares.astype(jnp.bfloat16)
    squares_low = (own_squares - squares_high.astype(jnp.float32)).astype(jnp.bfloat16)
    squares_pair = jnp.broadcast_to(jnp.stack([squares_high, squares_low])[None], (mdl_count, 2, total_rows))
    blocks = jnp.transpose(
        partial_value.astype(jnp.bfloat16).reshape(2, mdl_count, quarter, total_rows), (1, 0, 2, 3)
    ).reshape(mdl_count, 2 * quarter, total_rows)
    payload = jnp.concatenate([blocks, squares_pair], axis=1)
    summed_payload = lax.all_to_all(payload, "mdl", 0, 0, tiled=True).astype(jnp.float32).sum(0)
    square_sum = summed_payload[2 * quarter] + summed_payload[2 * quarter + 1]
    scale = lax.rsqrt(square_sum / D + 1e-05)
    gate_part = summed_payload[:quarter] * scale[None, :]
    up_part = summed_payload[quarter : 2 * quarter] * scale[None, :]
    hidden_part = (jax.nn.silu(gate_part) * up_part).astype(jnp.bfloat16)
    hidden_copies = jnp.broadcast_to(hidden_part[None], (mdl_count,) + hidden_part.shape)
    hidden = lax.all_to_all(hidden_copies, "mdl", 0, 0, tiled=True).reshape(units, total_rows)
    columns = down_weight.reshape(down_weight.shape[0], col_groups * sub_width)
    lowered = lax.dot_general(
        columns, hidden, (((0,), (0,)), ((), ())), preferred_element_type=jnp.float32
    )
    mesh_shape = (lax.axis_size("y"), lax.axis_size("z"), lax.axis_size("c"))
    summed = scatter_sum(lowered.reshape(mesh_shape + (sub_width * total_rows // 128, 128))).reshape(sub_width, total_rows)
    layer_out = (local_wide + summed.T).astype(jnp.bfloat16)
    return (layer_out, key_value_store)


def solution(mesh):
    req_size, mdl_size = mesh.devices.shape
    chips_y = 4
    split = Mesh(
        mesh.devices.reshape(chips_y, req_size // (2 * chips_y), 2, mdl_size),
        REQ + ("mdl",),
    )
    return jax.shard_map(
        body,
        mesh=split,
        in_specs=(
            P(REQ),
            P(),
            P(REQ, "mdl"),
            P(None, REQ, "mdl"),
            P(None, REQ, "mdl"),
            P(None, (REQ + ("mdl",))),
            P("mdl", REQ),
            P(),
            P(None, None, "mdl", None, REQ),
            P(REQ, None, "mdl", None),
        ),
        out_specs=(P(None, REQ + ("mdl",)), P(None, REQ, "mdl")),
        check_vma=False,
    )
```

```python
import jax
import jax.numpy as jnp
from jax import lax
from jax.experimental import pallas as pl
from jax.experimental.pallas import tpu as pltpu
from jax.sharding import Mesh, PartitionSpec as P

D = 5120
QUERY_HEADS = 32
KEY_VALUE_HEADS = 8
HEAD_SIZE = 128


NEGATIVE_FILL = -1e30
REQ = ("y", "z", "c")


def gather_rows(part):
    count = lax.axis_size(REQ)
    flat = part.reshape(-1, 128)
    flat = lax.all_gather(flat, "c", axis=0, tiled=True)
    flat = lax.all_gather(flat, "z", axis=0, tiled=True)
    copies = jnp.broadcast_to(flat[None], (lax.axis_size("y"),) + flat.shape)
    return lax.all_to_all(copies, "y", 0, 0, tiled=True).reshape((count,) + part.shape)


def scatter_sum(parts):
    wide = None
    for position, name in ((2, "c"), (0, "y"), (1, "z")):
        moved = lax.all_to_all(parts.astype(jnp.bfloat16), name, position, position, tiled=True)
        wide = moved.astype(jnp.float32).sum(position, keepdims=True)
        parts = wide
    return wide


def mdl_sum(values, wires):
    count = lax.axis_size("mdl")
    sent = tuple(v.astype(w) for v, w in zip(values, wires))
    totals = [v.astype(jnp.float32) for v in values]
    for shift in range(1, count):
        pairs = [(i, (i + shift) % count) for i in range(count)]
        arrived = lax.ppermute(sent, "mdl", pairs)
        totals = [t + a.astype(jnp.float32) for t, a in zip(totals, arrived)]
    return totals


def mdl_scatter_sum(value, wire):
    count = lax.axis_size("mdl")
    height = value.shape[0] // count
    blocks = value.astype(wire).reshape((count, height * value.shape[1] // 128, 128))
    moved = lax.all_to_all(blocks, "mdl", 0, 0, tiled=True)
    return moved.astype(jnp.float32).sum(0).reshape(height, value.shape[1])


CHUNK_ROWS = 256


def attention_kernel(
    lengths_ref, query_ref, fresh_ref, cache_hbm, fresh_rows, out_ref, store_hbm, keys, values, sems, write_sems
):
    rows = keys.shape[0]
    chunks = rows // CHUNK_ROWS
    copies = []
    for chunk in range(chunks):
        window = pl.ds(chunk * CHUNK_ROWS, CHUNK_ROWS)
        for which, target in ((0, keys), (1, values)):
            copy = pltpu.make_async_copy(cache_hbm.at[which, window], target.at[window], sems.at[which, chunk])
            copy.start()
            copies.append(copy)
    slot_count = lengths_ref.shape[0]
    kv_heads, row_count, head_dim = query_ref.shape
    group_width = row_count // slot_count
    row_slot = lax.broadcasted_iota(jnp.int32, (row_count, 1), 0) // group_width
    first = jnp.zeros((row_count, 1), jnp.int32)
    end = jnp.zeros((row_count, 1), jnp.int32)
    start = jnp.int32(0)
    for slot in range(slot_count):
        length = lengths_ref[slot]
        first = jnp.where(row_slot == slot, start, first)
        end = jnp.where(row_slot == slot, start + length, end)
        start = start + length + 1
    columns = lax.broadcasted_iota(jnp.int32, (row_count, rows), 1)
    inside = (columns >= first) & (columns < end)
    pick = (lax.broadcasted_iota(jnp.int32, (row_count, slot_count), 1) == row_slot)
    for copy in copies:
        copy.wait()
    tile = 16
    within = lax.broadcasted_iota(jnp.int32, (tile, keys.shape[1]), 0)
    start = jnp.int32(0)
    for slot in range(slot_count):
        row = start + lengths_ref[slot]
        base = pl.multiple_of((row // tile) * tile, tile)
        for which, target in ((0, keys), (1, values)):
            block = target[pl.ds(base, tile), :]
            fresh_row = jnp.broadcast_to(fresh_rows[which, pl.ds(slot, 1), :], block.shape)
            target[pl.ds(base, tile), :] = jnp.where(within == row - base, fresh_row, block)
        start = row + 1
    writes = []
    for which, source in ((0, keys), (1, values)):
        write = pltpu.make_async_copy(source, store_hbm.at[which], write_sems.at[which])
        write.start()
        writes.append(write)
    score_scale = head_dim ** (-0.5)
    for head in range(kv_heads):
        lanes = pl.ds(head * head_dim, head_dim)
        query_rows = query_ref[head]
        scores = lax.dot_general(
            query_rows, keys[:, lanes], (((1,), (1,)), ((), ())), preferred_element_type=jnp.float32
        ) * score_scale
        fresh_scores = lax.dot_general(
            query_rows, fresh_ref[0, head], (((1,), (1,)), ((), ())), preferred_element_type=jnp.float32
        ) * score_scale
        new_score = jnp.sum(jnp.where(pick, fresh_scores, 0.0), axis=1, keepdims=True)
        scores = jnp.where(inside, scores, NEGATIVE_FILL)
        top = jnp.maximum(jnp.max(scores, axis=1, keepdims=True), new_score)
        weights = jnp.where(inside, jnp.exp(scores - top), 0.0)
        new_weight = jnp.exp(new_score - top)
        denominator = jnp.sum(weights, axis=1, keepdims=True) + new_weight
        mixed = jnp.dot(weights.astype(jnp.bfloat16), values[:, lanes], preferred_element_type=jnp.float32)
        fresh_values = jnp.dot(pick.astype(jnp.bfloat16), fresh_ref[1, head], preferred_element_type=jnp.float32)
        mixed = mixed + new_weight.astype(jnp.bfloat16).astype(jnp.float32) * fresh_values
        out_ref[head] = (mixed / denominator).astype(out_ref.dtype)
    for write in writes:
        write.wait()


def attend_kernel(lengths, query, key_value_fresh, kv_cache):
    slot_count = lengths.shape[0]
    kv_width = kv_cache.shape[2]
    kv_heads = kv_width // HEAD_SIZE
    group_width = QUERY_HEADS // KEY_VALUE_HEADS
    rows = kv_cache.shape[1]
    query_rows = jnp.transpose(
        query.reshape(slot_count, kv_heads, group_width, HEAD_SIZE), (1, 0, 2, 3)
    ).reshape(kv_heads, slot_count * group_width, HEAD_SIZE)
    fresh = jnp.transpose(
        key_value_fresh.reshape(2, slot_count, kv_heads, HEAD_SIZE), (0, 2, 1, 3)
    )
    out, store = pl.pallas_call(
        attention_kernel,
        out_shape=(
            jax.ShapeDtypeStruct(query_rows.shape, jnp.bfloat16),
            jax.ShapeDtypeStruct(kv_cache.shape, kv_cache.dtype),
        ),
        in_specs=[
            pl.BlockSpec(memory_space=pltpu.SMEM),
            pl.BlockSpec(memory_space=pltpu.VMEM),
            pl.BlockSpec(memory_space=pltpu.VMEM),
            pl.BlockSpec(memory_space=pl.ANY),
            pl.BlockSpec(memory_space=pltpu.VMEM),
        ],
        out_specs=(pl.BlockSpec(memory_space=pltpu.VMEM), pl.BlockSpec(memory_space=pl.ANY)),
        scratch_shapes=[
            pltpu.VMEM((rows, kv_width), kv_cache.dtype),
            pltpu.VMEM((rows, kv_width), kv_cache.dtype),
            pltpu.SemaphoreType.DMA((2, rows // CHUNK_ROWS)),
            pltpu.SemaphoreType.DMA((2,)),
        ],
        cost_estimate=pl.CostEstimate(
            flops=4 * kv_heads * slot_count * group_width * rows * HEAD_SIZE,
            transcendentals=kv_heads * slot_count * group_width * rows,
            bytes_accessed=2 * rows * kv_width * 2,
        ),
    )(lengths, query_rows, fresh, kv_cache, key_value_fresh)
    return store, jnp.transpose(
        out.reshape(kv_heads, slot_count, group_width, HEAD_SIZE), (1, 0, 2, 3)
    ).reshape(slot_count, kv_heads * group_width * HEAD_SIZE)


def slot_bounds(lengths):
    span_sizes = lengths + 1
    first_rows = jnp.cumsum(span_sizes) - span_sizes
    return (first_rows, first_rows + span_sizes)


def attend_rows(query_rows, key_value_store, row_base, first_rows, end_rows):
    block_rows = 128
    slot_count, kv_heads, group_width, head_dim = query_rows.shape
    pool_rows = key_value_store.shape[1]
    key_table = key_value_store[0].reshape(pool_rows, kv_heads, head_dim)
    value_table = key_value_store[1].reshape(pool_rows, kv_heads, head_dim)
    needed = jnp.clip(jnp.max(end_rows) - row_base, 0, pool_rows)
    block_count = (needed + block_rows - 1) // block_rows
    score_scale = head_dim ** (-0.5)

    def advance(block_index, carried):
        running_max, denominator, accumulated = carried
        offset = block_index * block_rows
        key_block = lax.dynamic_slice_in_dim(key_table, offset, block_rows, 0)
        value_block = lax.dynamic_slice_in_dim(value_table, offset, block_rows, 0)
        scores = (
            jnp.einsum("sngd,tnd->sngt", query_rows, key_block, preferred_element_type=jnp.float32)
            * score_scale
        )
        row_ids = row_base + offset + jnp.arange(block_rows, dtype=jnp.int32)
        inside = (
            (row_ids[None, :] >= first_rows[:, None]) & (row_ids[None, :] < end_rows[:, None])
        )[:, None, None, :]
        scores = jnp.where(inside, scores, NEGATIVE_FILL)
        new_max = jnp.maximum(running_max, jnp.max(scores, axis=-1))
        weights = jnp.where(inside, jnp.exp(scores - new_max[..., None]), 0.0)
        factor = jnp.exp(running_max - new_max)
        denominator = denominator * factor + jnp.sum(weights, axis=-1)
        accumulated = accumulated * factor[..., None] + jnp.einsum(
            "sngt,tnd->sngd",
            weights.astype(jnp.bfloat16),
            value_block,
            preferred_element_type=jnp.float32,
        )
        return (new_max, denominator, accumulated)

    initial = (
        jnp.full((slot_count, kv_heads, group_width), NEGATIVE_FILL, jnp.float32),
        jnp.zeros((slot_count, kv_heads, group_width), jnp.float32),
        jnp.zeros((slot_count, kv_heads, group_width, head_dim), jnp.float32),
    )
    return lax.fori_loop(0, block_count, advance, initial)


def body(
    lengths,
    assignment,
    query,
    key_value_fresh,
    kv_cache,
    hidden_in,
    out_weight,
    norm_gain,
    gate_up_weight,
    down_weight,
):
    slot_count = lengths.shape[0]
    first_rows, end_rows = slot_bounds(lengths)
    key_value_store, attended = attend_kernel(lengths, query, key_value_fresh, kv_cache)
    y_count, mdl_count = lax.axis_size("y"), lax.axis_size("mdl")
    weight_copies = jnp.broadcast_to(out_weight.T[None], (y_count,) + out_weight.T.shape)
    row_weight = lax.all_to_all(weight_copies, "y", 0, 0, tiled=True).reshape(-1, out_weight.shape[0])
    flat = attended.reshape(-1, 128)
    flat = lax.all_gather(flat, "c", axis=0, tiled=True)
    flat = lax.all_gather(flat, "z", axis=0, tiled=True)
    row_attended = flat.reshape(-1, attended.shape[1])
    row_slots = row_attended.shape[0]
    sub_width = hidden_in.shape[1]
    row_projected = lax.dot_general(
        row_weight, row_attended, (((1,), (1,)), ((), ())), preferred_element_type=jnp.float32
    )
    outgoing = row_projected.astype(jnp.bfloat16).reshape(y_count * mdl_count, sub_width, row_slots)
    arrived = lax.all_to_all(outgoing, ("y", "mdl"), 0, 0, tiled=True)
    head_sum = arrived.astype(jnp.float32).reshape(y_count, mdl_count, sub_width, row_slots).sum(1)
    head_share = jnp.transpose(head_sum, (1, 0, 2)).reshape(sub_width, y_count * row_slots).T
    total_rows = assignment.shape[0]
    selection = (
        assignment[:, None] == lax.broadcasted_iota(jnp.int32, (total_rows, total_rows), 1)
    ).astype(jnp.float32)
    placed = lax.dot_general(
        selection,
        head_share,
        (((0,), (0,)), ((), ())),
        precision=lax.Precision.HIGHEST,
        preferred_element_type=jnp.float32,
    )
    residual_wide = hidden_in.astype(jnp.float32) + placed
    residual = residual_wide.astype(jnp.bfloat16)
    local_wide = residual.astype(jnp.float32)
    col_groups = gate_up_weight.shape[1]
    sub_width = hidden_in.shape[1]
    gathered = gather_rows(residual.T).reshape(col_groups * sub_width, total_rows)
    widened = gathered.astype(jnp.float32)
    own_squares = jnp.sum(widened * widened, axis=0)
    gain_table = norm_gain.reshape(col_groups, lax.axis_size("mdl"), sub_width)
    gain_cols = lax.dynamic_index_in_dim(
        gain_table, lax.axis_index("mdl"), 1, keepdims=False
    ).reshape(col_groups * sub_width)
    unscaled = (widened * gain_cols[:, None]).astype(jnp.bfloat16)
    gate_up = gate_up_weight.reshape(2, col_groups * sub_width, gate_up_weight.shape[4])
    partial_value = jnp.einsum("kr,gkf->gfr", unscaled, gate_up, preferred_element_type=jnp.float32)
    units = partial_value.shape[1]
    mdl_count = lax.axis_size("mdl")
    quarter = units // mdl_count
    squares_high = own_squares.astype(jnp.bfloat16)
    squares_low = (own_squares - squares_high.astype(jnp.float32)).astype(jnp.bfloat16)
    squares_pair = jnp.broadcast_to(jnp.stack([squares_high, squares_low])[None], (mdl_count, 2, total_rows))
    blocks = jnp.transpose(
        partial_value.astype(jnp.bfloat16).reshape(2, mdl_count, quarter, total_rows), (1, 0, 2, 3)
    ).reshape(mdl_count, 2 * quarter, total_rows)
    payload = jnp.concatenate([blocks, squares_pair], axis=1)
    summed_payload = lax.all_to_all(payload, "mdl", 0, 0, tiled=True).astype(jnp.float32).sum(0)
    square_sum = summed_payload[2 * quarter] + summed_payload[2 * quarter + 1]
    scale = lax.rsqrt(square_sum / D + 1e-05)
    gate_part = summed_payload[:quarter] * scale[None, :]
    up_part = summed_payload[quarter : 2 * quarter] * scale[None, :]
    hidden_part = (jax.nn.silu(gate_part) * up_part).astype(jnp.bfloat16)
    hidden_copies = jnp.broadcast_to(hidden_part[None], (mdl_count,) + hidden_part.shape)
    hidden = lax.all_to_all(hidden_copies, "mdl", 0, 0, tiled=True).reshape(units, total_rows)
    columns = down_weight.reshape(down_weight.shape[0], col_groups * sub_width)
    lowered = lax.dot_general(
        columns, hidden, (((0,), (0,)), ((), ())), preferred_element_type=jnp.float32
    )
    mesh_shape = (lax.axis_size("y"), lax.axis_size("z"), lax.axis_size("c"))
    summed = scatter_sum(lowered.reshape(mesh_shape + (sub_width * total_rows // 128, 128))).reshape(sub_width, total_rows)
    layer_out = (local_wide + summed.T).astype(jnp.bfloat16)
    return (layer_out, key_value_store)


def solution(mesh):
    req_size, mdl_size = mesh.devices.shape
    chips_y = 4
    split = Mesh(
        mesh.devices.reshape(chips_y, req_size // (2 * chips_y), 2, mdl_size),
        REQ + ("mdl",),
    )
    return jax.shard_map(
        body,
        mesh=split,
        in_specs=(
            P(REQ),
            P(),
            P(REQ, "mdl"),
            P(None, REQ, "mdl"),
            P(None, REQ, "mdl"),
            P(None, (REQ + ("mdl",))),
            P("mdl", REQ),
            P(),
            P(None, None, "mdl", None, REQ),
            P(REQ, None, "mdl", None),
        ),
        out_specs=(P(None, REQ + ("mdl",)), P(None, REQ, "mdl")),
        check_vma=False,
    )
```

```python
import jax
import jax.numpy as jnp
from jax import lax
from jax.experimental import pallas as pl
from jax.experimental.pallas import tpu as pltpu
from jax.sharding import Mesh, PartitionSpec as P

D = 5120
QUERY_HEADS = 32
KEY_VALUE_HEADS = 8
HEAD_SIZE = 128


NEGATIVE_FILL = -1e30
REQ = ("y", "z", "c")


def gather_rows(part):
    count = lax.axis_size(REQ)
    flat = part.reshape(-1, 128)
    flat = lax.all_gather(flat, "c", axis=0, tiled=True)
    flat = lax.all_gather(flat, "z", axis=0, tiled=True)
    copies = jnp.broadcast_to(flat[None], (lax.axis_size("y"),) + flat.shape)
    return lax.all_to_all(copies, "y", 0, 0, tiled=True).reshape((count,) + part.shape)


def scatter_sum(parts):
    wide = None
    for position, name in ((2, "c"), (1, "z"), (0, "y")):
        moved = lax.all_to_all(parts.astype(jnp.bfloat16), name, position, position, tiled=True)
        wide = moved.astype(jnp.float32).sum(position, keepdims=True)
        parts = wide
    return wide


def mdl_sum(values, wires):
    count = lax.axis_size("mdl")
    sent = tuple(v.astype(w) for v, w in zip(values, wires))
    totals = [v.astype(jnp.float32) for v in values]
    for shift in range(1, count):
        pairs = [(i, (i + shift) % count) for i in range(count)]
        arrived = lax.ppermute(sent, "mdl", pairs)
        totals = [t + a.astype(jnp.float32) for t, a in zip(totals, arrived)]
    return totals


def mdl_scatter_sum(value, wire):
    count = lax.axis_size("mdl")
    height = value.shape[0] // count
    blocks = value.astype(wire).reshape((count, height * value.shape[1] // 128, 128))
    moved = lax.all_to_all(blocks, "mdl", 0, 0, tiled=True)
    return moved.astype(jnp.float32).sum(0).reshape(height, value.shape[1])


CHUNK_ROWS = 256


def attention_kernel(
    lengths_ref, query_ref, fresh_ref, cache_hbm, fresh_rows, out_ref, store_hbm, keys, values, sems, write_sems
):
    rows = keys.shape[0]
    chunks = rows // CHUNK_ROWS
    copies = []
    for chunk in range(chunks):
        window = pl.ds(chunk * CHUNK_ROWS, CHUNK_ROWS)
        for which, target in ((0, keys), (1, values)):
            copy = pltpu.make_async_copy(cache_hbm.at[which, window], target.at[window], sems.at[which, chunk])
            copy.start()
            copies.append(copy)
    slot_count = lengths_ref.shape[0]
    kv_heads, row_count, head_dim = query_ref.shape
    group_width = row_count // slot_count
    row_slot = lax.broadcasted_iota(jnp.int32, (row_count, 1), 0) // group_width
    first = jnp.zeros((row_count, 1), jnp.int32)
    end = jnp.zeros((row_count, 1), jnp.int32)
    start = jnp.int32(0)
    for slot in range(slot_count):
        length = lengths_ref[slot]
        first = jnp.where(row_slot == slot, start, first)
        end = jnp.where(row_slot == slot, start + length, end)
        start = start + length + 1
    columns = lax.broadcasted_iota(jnp.int32, (row_count, rows), 1)
    inside = (columns >= first) & (columns < end)
    pick = (lax.broadcasted_iota(jnp.int32, (row_count, slot_count), 1) == row_slot)
    for copy in copies:
        copy.wait()
    tile = 16
    within = lax.broadcasted_iota(jnp.int32, (tile, keys.shape[1]), 0)
    start = jnp.int32(0)
    for slot in range(slot_count):
        row = start + lengths_ref[slot]
        base = pl.multiple_of((row // tile) * tile, tile)
        for which, target in ((0, keys), (1, values)):
            block = target[pl.ds(base, tile), :]
            fresh_row = jnp.broadcast_to(fresh_rows[which, pl.ds(slot, 1), :], block.shape)
            target[pl.ds(base, tile), :] = jnp.where(within == row - base, fresh_row, block)
        start = row + 1
    writes = []
    for which, source in ((0, keys), (1, values)):
        write = pltpu.make_async_copy(source, store_hbm.at[which], write_sems.at[which])
        write.start()
        writes.append(write)
    score_scale = head_dim ** (-0.5)
    for head in range(kv_heads):
        lanes = pl.ds(head * head_dim, head_dim)
        query_rows = query_ref[head]
        scores = lax.dot_general(
            query_rows, keys[:, lanes], (((1,), (1,)), ((), ())), preferred_element_type=jnp.float32
        ) * score_scale
        fresh_scores = lax.dot_general(
            query_rows, fresh_ref[0, head], (((1,), (1,)), ((), ())), preferred_element_type=jnp.float32
        ) * score_scale
        new_score = jnp.sum(jnp.where(pick, fresh_scores, 0.0), axis=1, keepdims=True)
        scores = jnp.where(inside, scores, NEGATIVE_FILL)
        top = jnp.maximum(jnp.max(scores, axis=1, keepdims=True), new_score)
        weights = jnp.where(inside, jnp.exp(scores - top), 0.0)
        new_weight = jnp.exp(new_score - top)
        denominator = jnp.sum(weights, axis=1, keepdims=True) + new_weight
        mixed = jnp.dot(weights.astype(jnp.bfloat16), values[:, lanes], preferred_element_type=jnp.float32)
        fresh_values = jnp.dot(pick.astype(jnp.bfloat16), fresh_ref[1, head], preferred_element_type=jnp.float32)
        mixed = mixed + new_weight.astype(jnp.bfloat16).astype(jnp.float32) * fresh_values
        out_ref[head] = (mixed / denominator).astype(out_ref.dtype)
    for write in writes:
        write.wait()


def attend_kernel(lengths, query, key_value_fresh, kv_cache):
    slot_count = lengths.shape[0]
    kv_width = kv_cache.shape[2]
    kv_heads = kv_width // HEAD_SIZE
    group_width = QUERY_HEADS // KEY_VALUE_HEADS
    rows = kv_cache.shape[1]
    query_rows = jnp.transpose(
        query.reshape(slot_count, kv_heads, group_width, HEAD_SIZE), (1, 0, 2, 3)
    ).reshape(kv_heads, slot_count * group_width, HEAD_SIZE)
    fresh = jnp.transpose(
        key_value_fresh.reshape(2, slot_count, kv_heads, HEAD_SIZE), (0, 2, 1, 3)
    )
    out, store = pl.pallas_call(
        attention_kernel,
        out_shape=(
            jax.ShapeDtypeStruct(query_rows.shape, jnp.bfloat16),
            jax.ShapeDtypeStruct(kv_cache.shape, kv_cache.dtype),
        ),
        in_specs=[
            pl.BlockSpec(memory_space=pltpu.SMEM),
            pl.BlockSpec(memory_space=pltpu.VMEM),
            pl.BlockSpec(memory_space=pltpu.VMEM),
            pl.BlockSpec(memory_space=pl.ANY),
            pl.BlockSpec(memory_space=pltpu.VMEM),
        ],
        out_specs=(pl.BlockSpec(memory_space=pltpu.VMEM), pl.BlockSpec(memory_space=pl.ANY)),
        scratch_shapes=[
            pltpu.VMEM((rows, kv_width), kv_cache.dtype),
            pltpu.VMEM((rows, kv_width), kv_cache.dtype),
            pltpu.SemaphoreType.DMA((2, rows // CHUNK_ROWS)),
            pltpu.SemaphoreType.DMA((2,)),
        ],
        cost_estimate=pl.CostEstimate(
            flops=4 * kv_heads * slot_count * group_width * rows * HEAD_SIZE,
            transcendentals=kv_heads * slot_count * group_width * rows,
            bytes_accessed=2 * rows * kv_width * 2,
        ),
    )(lengths, query_rows, fresh, kv_cache, key_value_fresh)
    return store, jnp.transpose(
        out.reshape(kv_heads, slot_count, group_width, HEAD_SIZE), (1, 0, 2, 3)
    ).reshape(slot_count, kv_heads * group_width * HEAD_SIZE)


def slot_bounds(lengths):
    span_sizes = lengths + 1
    first_rows = jnp.cumsum(span_sizes) - span_sizes
    return (first_rows, first_rows + span_sizes)


def attend_rows(query_rows, key_value_store, row_base, first_rows, end_rows):
    block_rows = 128
    slot_count, kv_heads, group_width, head_dim = query_rows.shape
    pool_rows = key_value_store.shape[1]
    key_table = key_value_store[0].reshape(pool_rows, kv_heads, head_dim)
    value_table = key_value_store[1].reshape(pool_rows, kv_heads, head_dim)
    needed = jnp.clip(jnp.max(end_rows) - row_base, 0, pool_rows)
    block_count = (needed + block_rows - 1) // block_rows
    score_scale = head_dim ** (-0.5)

    def advance(block_index, carried):
        running_max, denominator, accumulated = carried
        offset = block_index * block_rows
        key_block = lax.dynamic_slice_in_dim(key_table, offset, block_rows, 0)
        value_block = lax.dynamic_slice_in_dim(value_table, offset, block_rows, 0)
        scores = (
            jnp.einsum("sngd,tnd->sngt", query_rows, key_block, preferred_element_type=jnp.float32)
            * score_scale
        )
        row_ids = row_base + offset + jnp.arange(block_rows, dtype=jnp.int32)
        inside = (
            (row_ids[None, :] >= first_rows[:, None]) & (row_ids[None, :] < end_rows[:, None])
        )[:, None, None, :]
        scores = jnp.where(inside, scores, NEGATIVE_FILL)
        new_max = jnp.maximum(running_max, jnp.max(scores, axis=-1))
        weights = jnp.where(inside, jnp.exp(scores - new_max[..., None]), 0.0)
        factor = jnp.exp(running_max - new_max)
        denominator = denominator * factor + jnp.sum(weights, axis=-1)
        accumulated = accumulated * factor[..., None] + jnp.einsum(
            "sngt,tnd->sngd",
            weights.astype(jnp.bfloat16),
            value_block,
            preferred_element_type=jnp.float32,
        )
        return (new_max, denominator, accumulated)

    initial = (
        jnp.full((slot_count, kv_heads, group_width), NEGATIVE_FILL, jnp.float32),
        jnp.zeros((slot_count, kv_heads, group_width), jnp.float32),
        jnp.zeros((slot_count, kv_heads, group_width, head_dim), jnp.float32),
    )
    return lax.fori_loop(0, block_count, advance, initial)


def body(
    lengths,
    assignment,
    query,
    key_value_fresh,
    kv_cache,
    hidden_in,
    out_weight,
    norm_gain,
    gate_up_weight,
    down_weight,
):
    slot_count = lengths.shape[0]
    first_rows, end_rows = slot_bounds(lengths)
    key_value_store, attended = attend_kernel(lengths, query, key_value_fresh, kv_cache)
    y_count, mdl_count = lax.axis_size("y"), lax.axis_size("mdl")
    weight_copies = jnp.broadcast_to(out_weight.T[None], (y_count,) + out_weight.T.shape)
    row_weight = lax.all_to_all(weight_copies, "y", 0, 0, tiled=True).reshape(-1, out_weight.shape[0])
    flat = attended.reshape(-1, 128)
    flat = lax.all_gather(flat, "c", axis=0, tiled=True)
    flat = lax.all_gather(flat, "z", axis=0, tiled=True)
    row_attended = flat.reshape(-1, attended.shape[1])
    row_slots = row_attended.shape[0]
    sub_width = hidden_in.shape[1]
    row_projected = lax.dot_general(
        row_weight, row_attended, (((1,), (1,)), ((), ())), preferred_element_type=jnp.float32
    )
    outgoing = row_projected.astype(jnp.bfloat16).reshape(y_count * mdl_count, sub_width, row_slots)
    arrived = lax.all_to_all(outgoing, ("y", "mdl"), 0, 0, tiled=True)
    head_sum = arrived.astype(jnp.float32).reshape(y_count, mdl_count, sub_width, row_slots).sum(1)
    head_share = jnp.transpose(head_sum, (1, 0, 2)).reshape(sub_width, y_count * row_slots).T
    total_rows = assignment.shape[0]
    selection = (
        assignment[:, None] == lax.broadcasted_iota(jnp.int32, (total_rows, total_rows), 1)
    ).astype(jnp.float32)
    placed = lax.dot_general(
        selection,
        head_share,
        (((0,), (0,)), ((), ())),
        precision=lax.Precision.HIGHEST,
        preferred_element_type=jnp.float32,
    )
    residual_wide = hidden_in.astype(jnp.float32) + placed
    residual = residual_wide.astype(jnp.bfloat16)
    local_wide = residual.astype(jnp.float32)
    col_groups = gate_up_weight.shape[1]
    sub_width = hidden_in.shape[1]
    gathered = jnp.transpose(gather_rows(residual.T), (2, 0, 1)).reshape(total_rows, col_groups * sub_width)
    widened = gathered.astype(jnp.float32)
    own_squares = jnp.sum(widened * widened, axis=1)
    gain_table = norm_gain.reshape(col_groups, lax.axis_size("mdl"), sub_width)
    gain_cols = lax.dynamic_index_in_dim(
        gain_table, lax.axis_index("mdl"), 1, keepdims=False
    ).reshape(col_groups * sub_width)
    unscaled = (widened * gain_cols).astype(jnp.bfloat16)
    gate_up = gate_up_weight.reshape(2, col_groups * sub_width, gate_up_weight.shape[4])
    partial_value = jnp.einsum("rk,gkf->gfr", unscaled, gate_up, preferred_element_type=jnp.float32)
    units = partial_value.shape[1]
    mdl_count = lax.axis_size("mdl")
    quarter = units // mdl_count
    squares_high = own_squares.astype(jnp.bfloat16)
    squares_low = (own_squares - squares_high.astype(jnp.float32)).astype(jnp.bfloat16)
    squares_pair = jnp.broadcast_to(jnp.stack([squares_high, squares_low])[None], (mdl_count, 2, total_rows))
    blocks = jnp.transpose(
        partial_value.astype(jnp.bfloat16).reshape(2, mdl_count, quarter, total_rows), (1, 0, 2, 3)
    ).reshape(mdl_count, 2 * quarter, total_rows)
    payload = jnp.concatenate([blocks, squares_pair], axis=1)
    summed_payload = lax.all_to_all(payload, "mdl", 0, 0, tiled=True).astype(jnp.float32).sum(0)
    square_sum = summed_payload[2 * quarter] + summed_payload[2 * quarter + 1]
    scale = lax.rsqrt(square_sum / D + 1e-05)
    gate_part = summed_payload[:quarter] * scale[None, :]
    up_part = summed_payload[quarter : 2 * quarter] * scale[None, :]
    hidden_part = (jax.nn.silu(gate_part) * up_part).astype(jnp.bfloat16)
    hidden_copies = jnp.broadcast_to(hidden_part[None], (mdl_count,) + hidden_part.shape)
    hidden = lax.all_to_all(hidden_copies, "mdl", 0, 0, tiled=True).reshape(units, total_rows)
    columns = down_weight.reshape(down_weight.shape[0], col_groups * sub_width)
    lowered = lax.dot_general(
        columns, hidden, (((0,), (0,)), ((), ())), preferred_element_type=jnp.float32
    )
    mesh_shape = (lax.axis_size("y"), lax.axis_size("z"), lax.axis_size("c"))
    summed = scatter_sum(lowered.reshape(mesh_shape + (sub_width * total_rows // 128, 128))).reshape(sub_width, total_rows)
    layer_out = (local_wide + summed.T).astype(jnp.bfloat16)
    return (layer_out, key_value_store)


def solution(mesh):
    req_size, mdl_size = mesh.devices.shape
    chips_y = 4
    split = Mesh(
        mesh.devices.reshape(chips_y, req_size // (2 * chips_y), 2, mdl_size),
        REQ + ("mdl",),
    )
    return jax.shard_map(
        body,
        mesh=split,
        in_specs=(
            P(REQ),
            P(),
            P(REQ, "mdl"),
            P(None, REQ, "mdl"),
            P(None, REQ, "mdl"),
            P(None, (REQ + ("mdl",))),
            P("mdl", REQ),
            P(),
            P(None, None, "mdl", None, REQ),
            P(REQ, None, "mdl", None),
        ),
        out_specs=(P(None, REQ + ("mdl",)), P(None, REQ, "mdl")),
        check_vma=False,
    )
```

```python
import jax
import jax.numpy as jnp
from jax import lax
from jax.experimental import pallas as pl
from jax.experimental.pallas import tpu as pltpu
from jax.sharding import Mesh, PartitionSpec as P

D = 5120
QUERY_HEADS = 32
KEY_VALUE_HEADS = 8
HEAD_SIZE = 128


NEGATIVE_FILL = -1e30
REQ = ("y", "z", "c")


def gather_rows(part):
    count = lax.axis_size(REQ)
    flat = part.reshape(-1, 128)
    flat = lax.all_gather(flat, "c", axis=0, tiled=True)
    flat = lax.all_gather(flat, "z", axis=0, tiled=True)
    copies = jnp.broadcast_to(flat[None], (lax.axis_size("y"),) + flat.shape)
    return lax.all_to_all(copies, "y", 0, 0, tiled=True).reshape((count,) + part.shape)


def scatter_sum(parts):
    wide = None
    for position, name in ((2, "c"), (0, "y"), (1, "z")):
        moved = lax.all_to_all(parts.astype(jnp.bfloat16), name, position, position, tiled=True)
        wide = moved.astype(jnp.float32).sum(position, keepdims=True)
        parts = wide
    return wide


def mdl_sum(values, wires):
    count = lax.axis_size("mdl")
    sent = tuple(v.astype(w) for v, w in zip(values, wires))
    totals = [v.astype(jnp.float32) for v in values]
    for shift in range(1, count):
        pairs = [(i, (i + shift) % count) for i in range(count)]
        arrived = lax.ppermute(sent, "mdl", pairs)
        totals = [t + a.astype(jnp.float32) for t, a in zip(totals, arrived)]
    return totals


def mdl_scatter_sum(value, wire):
    count = lax.axis_size("mdl")
    height = value.shape[0] // count
    blocks = value.astype(wire).reshape((count, height * value.shape[1] // 128, 128))
    moved = lax.all_to_all(blocks, "mdl", 0, 0, tiled=True)
    return moved.astype(jnp.float32).sum(0).reshape(height, value.shape[1])


CHUNK_ROWS = 256


def attention_kernel(
    lengths_ref, query_ref, fresh_ref, cache_hbm, fresh_rows, out_ref, store_hbm, keys, values, sems, write_sems
):
    rows = keys.shape[0]
    chunks = rows // CHUNK_ROWS
    copies = []
    for chunk in range(chunks):
        window = pl.ds(chunk * CHUNK_ROWS, CHUNK_ROWS)
        for which, target in ((0, keys), (1, values)):
            copy = pltpu.make_async_copy(cache_hbm.at[which, window], target.at[window], sems.at[which, chunk])
            copy.start()
            copies.append(copy)
    slot_count = lengths_ref.shape[0]
    kv_heads, row_count, head_dim = query_ref.shape
    group_width = row_count // slot_count
    row_slot = lax.broadcasted_iota(jnp.int32, (row_count, 1), 0) // group_width
    first = jnp.zeros((row_count, 1), jnp.int32)
    end = jnp.zeros((row_count, 1), jnp.int32)
    start = jnp.int32(0)
    for slot in range(slot_count):
        length = lengths_ref[slot]
        first = jnp.where(row_slot == slot, start, first)
        end = jnp.where(row_slot == slot, start + length, end)
        start = start + length + 1
    columns = lax.broadcasted_iota(jnp.int32, (row_count, rows), 1)
    inside = (columns >= first) & (columns < end)
    pick = (lax.broadcasted_iota(jnp.int32, (row_count, slot_count), 1) == row_slot)
    for copy in copies:
        copy.wait()
    tile = 16
    within = lax.broadcasted_iota(jnp.int32, (tile, keys.shape[1]), 0)
    start = jnp.int32(0)
    for slot in range(slot_count):
        row = start + lengths_ref[slot]
        base = pl.multiple_of((row // tile) * tile, tile)
        for which, target in ((0, keys), (1, values)):
            block = target[pl.ds(base, tile), :]
            fresh_row = jnp.broadcast_to(fresh_rows[which, pl.ds(slot, 1), :], block.shape)
            target[pl.ds(base, tile), :] = jnp.where(within == row - base, fresh_row, block)
        start = row + 1
    writes = []
    for which, source in ((0, keys), (1, values)):
        write = pltpu.make_async_copy(source, store_hbm.at[which], write_sems.at[which])
        write.start()
        writes.append(write)
    score_scale = head_dim ** (-0.5)
    for head in range(kv_heads):
        lanes = pl.ds(head * head_dim, head_dim)
        query_rows = query_ref[head]
        scores = lax.dot_general(
            query_rows, keys[:, lanes], (((1,), (1,)), ((), ())), preferred_element_type=jnp.float32
        ) * score_scale
        fresh_scores = lax.dot_general(
            query_rows, fresh_ref[0, head], (((1,), (1,)), ((), ())), preferred_element_type=jnp.float32
        ) * score_scale
        new_score = jnp.sum(jnp.where(pick, fresh_scores, 0.0), axis=1, keepdims=True)
        scores = jnp.where(inside, scores, NEGATIVE_FILL)
        top = jnp.maximum(jnp.max(scores, axis=1, keepdims=True), new_score)
        weights = jnp.where(inside, jnp.exp(scores - top), 0.0)
        new_weight = jnp.exp(new_score - top)
        denominator = jnp.sum(weights, axis=1, keepdims=True) + new_weight
        mixed = jnp.dot(weights.astype(jnp.bfloat16), values[:, lanes], preferred_element_type=jnp.float32)
        fresh_values = jnp.dot(pick.astype(jnp.bfloat16), fresh_ref[1, head], preferred_element_type=jnp.float32)
        mixed = mixed + new_weight.astype(jnp.bfloat16).astype(jnp.float32) * fresh_values
        out_ref[head] = (mixed / denominator).astype(out_ref.dtype)
    for write in writes:
        write.wait()


def attend_kernel(lengths, query, key_value_fresh, kv_cache):
    slot_count = lengths.shape[0]
    kv_width = kv_cache.shape[2]
    kv_heads = kv_width // HEAD_SIZE
    group_width = QUERY_HEADS // KEY_VALUE_HEADS
    rows = kv_cache.shape[1]
    query_rows = jnp.transpose(
        query.reshape(slot_count, kv_heads, group_width, HEAD_SIZE), (1, 0, 2, 3)
    ).reshape(kv_heads, slot_count * group_width, HEAD_SIZE)
    fresh = jnp.transpose(
        key_value_fresh.reshape(2, slot_count, kv_heads, HEAD_SIZE), (0, 2, 1, 3)
    )
    out, store = pl.pallas_call(
        attention_kernel,
        out_shape=(
            jax.ShapeDtypeStruct(query_rows.shape, jnp.bfloat16),
            jax.ShapeDtypeStruct(kv_cache.shape, kv_cache.dtype),
        ),
        in_specs=[
            pl.BlockSpec(memory_space=pltpu.SMEM),
            pl.BlockSpec(memory_space=pltpu.VMEM),
            pl.BlockSpec(memory_space=pltpu.VMEM),
            pl.BlockSpec(memory_space=pl.ANY),
            pl.BlockSpec(memory_space=pltpu.VMEM),
        ],
        out_specs=(pl.BlockSpec(memory_space=pltpu.VMEM), pl.BlockSpec(memory_space=pl.ANY)),
        scratch_shapes=[
            pltpu.VMEM((rows, kv_width), kv_cache.dtype),
            pltpu.VMEM((rows, kv_width), kv_cache.dtype),
            pltpu.SemaphoreType.DMA((2, rows // CHUNK_ROWS)),
            pltpu.SemaphoreType.DMA((2,)),
        ],
        cost_estimate=pl.CostEstimate(
            flops=4 * kv_heads * slot_count * group_width * rows * HEAD_SIZE,
            transcendentals=kv_heads * slot_count * group_width * rows,
            bytes_accessed=2 * rows * kv_width * 2,
        ),
    )(lengths, query_rows, fresh, kv_cache, key_value_fresh)
    return store, jnp.transpose(
        out.reshape(kv_heads, slot_count, group_width, HEAD_SIZE), (1, 0, 2, 3)
    ).reshape(slot_count, kv_heads * group_width * HEAD_SIZE)


def slot_bounds(lengths):
    span_sizes = lengths + 1
    first_rows = jnp.cumsum(span_sizes) - span_sizes
    return (first_rows, first_rows + span_sizes)


def attend_rows(query_rows, key_value_store, row_base, first_rows, end_rows):
    block_rows = 128
    slot_count, kv_heads, group_width, head_dim = query_rows.shape
    pool_rows = key_value_store.shape[1]
    key_table = key_value_store[0].reshape(pool_rows, kv_heads, head_dim)
    value_table = key_value_store[1].reshape(pool_rows, kv_heads, head_dim)
    needed = jnp.clip(jnp.max(end_rows) - row_base, 0, pool_rows)
    block_count = (needed + block_rows - 1) // block_rows
    score_scale = head_dim ** (-0.5)

    def advance(block_index, carried):
        running_max, denominator, accumulated = carried
        offset = block_index * block_rows
        key_block = lax.dynamic_slice_in_dim(key_table, offset, block_rows, 0)
        value_block = lax.dynamic_slice_in_dim(value_table, offset, block_rows, 0)
        scores = (
            jnp.einsum("sngd,tnd->sngt", query_rows, key_block, preferred_element_type=jnp.float32)
            * score_scale
        )
        row_ids = row_base + offset + jnp.arange(block_rows, dtype=jnp.int32)
        inside = (
            (row_ids[None, :] >= first_rows[:, None]) & (row_ids[None, :] < end_rows[:, None])
        )[:, None, None, :]
        scores = jnp.where(inside, scores, NEGATIVE_FILL)
        new_max = jnp.maximum(running_max, jnp.max(scores, axis=-1))
        weights = jnp.where(inside, jnp.exp(scores - new_max[..., None]), 0.0)
        factor = jnp.exp(running_max - new_max)
        denominator = denominator * factor + jnp.sum(weights, axis=-1)
        accumulated = accumulated * factor[..., None] + jnp.einsum(
            "sngt,tnd->sngd",
            weights.astype(jnp.bfloat16),
            value_block,
            preferred_element_type=jnp.float32,
        )
        return (new_max, denominator, accumulated)

    initial = (
        jnp.full((slot_count, kv_heads, group_width), NEGATIVE_FILL, jnp.float32),
        jnp.zeros((slot_count, kv_heads, group_width), jnp.float32),
        jnp.zeros((slot_count, kv_heads, group_width, head_dim), jnp.float32),
    )
    return lax.fori_loop(0, block_count, advance, initial)


def body(
    lengths,
    assignment,
    query,
    key_value_fresh,
    kv_cache,
    hidden_in,
    out_weight,
    norm_gain,
    gate_up_weight,
    down_weight,
):
    slot_count = lengths.shape[0]
    first_rows, end_rows = slot_bounds(lengths)
    key_value_store, attended = attend_kernel(lengths, query, key_value_fresh, kv_cache)
    y_count, mdl_count = lax.axis_size("y"), lax.axis_size("mdl")
    weight_copies = jnp.broadcast_to(out_weight.T[None], (y_count,) + out_weight.T.shape)
    row_weight = lax.all_to_all(weight_copies, "y", 0, 0, tiled=True).reshape(-1, out_weight.shape[0])
    flat = attended.reshape(-1, 128)
    flat = lax.all_gather(flat, "c", axis=0, tiled=True)
    flat = lax.all_gather(flat, "z", axis=0, tiled=True)
    row_attended = flat.reshape(-1, attended.shape[1])
    row_slots = row_attended.shape[0]
    sub_width = hidden_in.shape[1]
    row_projected = lax.dot_general(
        row_weight, row_attended, (((1,), (1,)), ((), ())), preferred_element_type=jnp.float32
    )
    outgoing = row_projected.astype(jnp.bfloat16).reshape(y_count * mdl_count, sub_width, row_slots)
    arrived = lax.all_to_all(outgoing, ("y", "mdl"), 0, 0, tiled=True)
    head_sum = arrived.astype(jnp.float32).reshape(y_count, mdl_count, sub_width, row_slots).sum(1)
    head_share = jnp.transpose(head_sum, (1, 0, 2)).reshape(sub_width, y_count * row_slots).T
    total_rows = assignment.shape[0]
    selection = (
        assignment[:, None] == lax.broadcasted_iota(jnp.int32, (total_rows, total_rows), 1)
    ).astype(jnp.float32)
    placed = lax.dot_general(
        selection,
        head_share,
        (((0,), (0,)), ((), ())),
        precision=lax.Precision.HIGHEST,
        preferred_element_type=jnp.float32,
    )
    residual_wide = hidden_in.astype(jnp.float32) + placed
    residual = residual_wide.astype(jnp.bfloat16)
    local_wide = residual.astype(jnp.float32)
    col_groups = gate_up_weight.shape[1]
    sub_width = hidden_in.shape[1]
    local_squares = jnp.sum(local_wide * local_wide, axis=1)
    local_high = local_squares.astype(jnp.bfloat16)
    local_low = (local_squares - local_high.astype(jnp.float32)).astype(jnp.bfloat16)
    sent = jnp.concatenate([residual.T, local_high[None], local_low[None]], axis=0)
    arrived = gather_rows(sent)
    own_squares = jnp.sum(arrived[:, sub_width:].astype(jnp.float32), axis=(0, 1))
    gathered = jnp.transpose(arrived[:, :sub_width], (2, 0, 1)).reshape(total_rows, col_groups * sub_width)
    widened = gathered.astype(jnp.float32)
    gain_table = norm_gain.reshape(col_groups, lax.axis_size("mdl"), sub_width)
    gain_cols = lax.dynamic_index_in_dim(
        gain_table, lax.axis_index("mdl"), 1, keepdims=False
    ).reshape(col_groups * sub_width)
    unscaled = (widened * gain_cols).astype(jnp.bfloat16)
    gate_up = gate_up_weight.reshape(2, col_groups * sub_width, gate_up_weight.shape[4])
    partial_value = jnp.einsum("rk,gkf->gfr", unscaled, gate_up, preferred_element_type=jnp.float32)
    units = partial_value.shape[1]
    mdl_count = lax.axis_size("mdl")
    quarter = units // mdl_count
    squares_high = own_squares.astype(jnp.bfloat16)
    squares_low = (own_squares - squares_high.astype(jnp.float32)).astype(jnp.bfloat16)
    squares_pair = jnp.broadcast_to(jnp.stack([squares_high, squares_low])[None], (mdl_count, 2, total_rows))
    blocks = jnp.transpose(
        partial_value.astype(jnp.bfloat16).reshape(2, mdl_count, quarter, total_rows), (1, 0, 2, 3)
    ).reshape(mdl_count, 2 * quarter, total_rows)
    payload = jnp.concatenate([blocks, squares_pair], axis=1)
    summed_payload = lax.all_to_all(payload, "mdl", 0, 0, tiled=True).astype(jnp.float32).sum(0)
    square_sum = summed_payload[2 * quarter] + summed_payload[2 * quarter + 1]
    scale = lax.rsqrt(square_sum / D + 1e-05)
    gate_part = summed_payload[:quarter] * scale[None, :]
    up_part = summed_payload[quarter : 2 * quarter] * scale[None, :]
    hidden_part = (jax.nn.silu(gate_part) * up_part).astype(jnp.bfloat16)
    hidden_copies = jnp.broadcast_to(hidden_part[None], (mdl_count,) + hidden_part.shape)
    hidden = lax.all_to_all(hidden_copies, "mdl", 0, 0, tiled=True).reshape(units, total_rows)
    columns = down_weight.reshape(down_weight.shape[0], col_groups * sub_width)
    lowered = lax.dot_general(
        columns, hidden, (((0,), (0,)), ((), ())), preferred_element_type=jnp.float32
    )
    mesh_shape = (lax.axis_size("y"), lax.axis_size("z"), lax.axis_size("c"))
    summed = scatter_sum(lowered.reshape(mesh_shape + (sub_width * total_rows // 128, 128))).reshape(sub_width, total_rows)
    layer_out = (local_wide + summed.T).astype(jnp.bfloat16)
    return (layer_out, key_value_store)


def solution(mesh):
    req_size, mdl_size = mesh.devices.shape
    chips_y = 4
    split = Mesh(
        mesh.devices.reshape(chips_y, req_size // (2 * chips_y), 2, mdl_size),
        REQ + ("mdl",),
    )
    return jax.shard_map(
        body,
        mesh=split,
        in_specs=(
            P(REQ),
            P(),
            P(REQ, "mdl"),
            P(None, REQ, "mdl"),
            P(None, REQ, "mdl"),
            P(None, (REQ + ("mdl",))),
            P("mdl", REQ),
            P(),
            P(None, None, "mdl", None, REQ),
            P(REQ, None, "mdl", None),
        ),
        out_specs=(P(None, REQ + ("mdl",)), P(None, REQ, "mdl")),
        check_vma=False,
    )
```

```python
import jax
import jax.numpy as jnp
from jax import lax
from jax.experimental import pallas as pl
from jax.experimental.pallas import tpu as pltpu
from jax.sharding import Mesh, PartitionSpec as P

D = 5120
QUERY_HEADS = 32
KEY_VALUE_HEADS = 8
HEAD_SIZE = 128


NEGATIVE_FILL = -1e30
REQ = ("y", "z", "c")


def gather_rows(part):
    count = lax.axis_size(REQ)
    flat = part.reshape(-1, 128)
    flat = lax.all_gather(flat, "c", axis=0, tiled=True)
    flat = lax.all_gather(flat, "z", axis=0, tiled=True)
    copies = jnp.broadcast_to(flat[None], (lax.axis_size("y"),) + flat.shape)
    return lax.all_to_all(copies, "y", 0, 0, tiled=True).reshape((count,) + part.shape)


def scatter_sum(parts):
    wide = None
    for position, name in ((2, "c"), (0, "y"), (1, "z")):
        moved = lax.all_to_all(parts.astype(jnp.bfloat16), name, position, position, tiled=True)
        wide = moved.astype(jnp.float32).sum(position, keepdims=True)
        parts = wide
    return wide


def mdl_sum(values, wires):
    count = lax.axis_size("mdl")
    sent = tuple(v.astype(w) for v, w in zip(values, wires))
    totals = [v.astype(jnp.float32) for v in values]
    for shift in range(1, count):
        pairs = [(i, (i + shift) % count) for i in range(count)]
        arrived = lax.ppermute(sent, "mdl", pairs)
        totals = [t + a.astype(jnp.float32) for t, a in zip(totals, arrived)]
    return totals


def mdl_scatter_sum(value, wire):
    count = lax.axis_size("mdl")
    height = value.shape[0] // count
    blocks = value.astype(wire).reshape((count, height * value.shape[1] // 128, 128))
    moved = lax.all_to_all(blocks, "mdl", 0, 0, tiled=True)
    return moved.astype(jnp.float32).sum(0).reshape(height, value.shape[1])


CHUNK_ROWS = 256


def attention_kernel(
    lengths_ref, query_ref, fresh_ref, cache_hbm, fresh_rows, out_ref, store_hbm, keys, values, sems, write_sems
):
    rows = keys.shape[0]
    chunks = rows // CHUNK_ROWS
    copies = []
    for chunk in range(chunks):
        window = pl.ds(chunk * CHUNK_ROWS, CHUNK_ROWS)
        for which, target in ((0, keys), (1, values)):
            copy = pltpu.make_async_copy(cache_hbm.at[which, window], target.at[window], sems.at[which, chunk])
            copy.start()
            copies.append(copy)
    slot_count = lengths_ref.shape[0]
    kv_heads, row_count, head_dim = query_ref.shape
    group_width = row_count // slot_count
    row_slot = lax.broadcasted_iota(jnp.int32, (row_count, 1), 0) // group_width
    first = jnp.zeros((row_count, 1), jnp.int32)
    end = jnp.zeros((row_count, 1), jnp.int32)
    start = jnp.int32(0)
    for slot in range(slot_count):
        length = lengths_ref[slot]
        first = jnp.where(row_slot == slot, start, first)
        end = jnp.where(row_slot == slot, start + length, end)
        start = start + length + 1
    columns = lax.broadcasted_iota(jnp.int32, (row_count, rows), 1)
    inside = (columns >= first) & (columns < end)
    pick = (lax.broadcasted_iota(jnp.int32, (row_count, slot_count), 1) == row_slot)
    for copy in copies:
        copy.wait()
    tile = 16
    within = lax.broadcasted_iota(jnp.int32, (tile, keys.shape[1]), 0)
    start = jnp.int32(0)
    for slot in range(slot_count):
        row = start + lengths_ref[slot]
        base = pl.multiple_of((row // tile) * tile, tile)
        for which, target in ((0, keys), (1, values)):
            block = target[pl.ds(base, tile), :]
            fresh_row = jnp.broadcast_to(fresh_rows[which, pl.ds(slot, 1), :], block.shape)
            target[pl.ds(base, tile), :] = jnp.where(within == row - base, fresh_row, block)
        start = row + 1
    writes = []
    for which, source in ((0, keys), (1, values)):
        write = pltpu.make_async_copy(source, store_hbm.at[which], write_sems.at[which])
        write.start()
        writes.append(write)
    score_scale = head_dim ** (-0.5)
    results = []
    for head in range(kv_heads):
        lanes = pl.ds(head * head_dim, head_dim)
        query_rows = query_ref[head]
        scores = lax.dot_general(
            query_rows, keys[:, lanes], (((1,), (1,)), ((), ())), preferred_element_type=jnp.float32
        ) * score_scale
        fresh_scores = lax.dot_general(
            query_rows, fresh_ref[0, head], (((1,), (1,)), ((), ())), preferred_element_type=jnp.float32
        ) * score_scale
        new_score = jnp.sum(jnp.where(pick, fresh_scores, 0.0), axis=1, keepdims=True)
        scores = jnp.where(inside, scores, NEGATIVE_FILL)
        top = jnp.maximum(jnp.max(scores, axis=1, keepdims=True), new_score)
        weights = jnp.where(inside, jnp.exp(scores - top), 0.0)
        new_weight = jnp.exp(new_score - top)
        denominator = jnp.sum(weights, axis=1, keepdims=True) + new_weight
        mixed = jnp.dot(weights.astype(jnp.bfloat16), values[:, lanes], preferred_element_type=jnp.float32)
        fresh_values = jnp.dot(pick.astype(jnp.bfloat16), fresh_ref[1, head], preferred_element_type=jnp.float32)
        mixed = mixed + new_weight.astype(jnp.bfloat16).astype(jnp.float32) * fresh_values
        results.append(mixed / denominator)
    pieces = [
        results[head][slot * group_width : (slot + 1) * group_width]
        for slot in range(slot_count)
        for head in range(kv_heads)
    ]
    out_ref[...] = jnp.concatenate(pieces, axis=0).astype(out_ref.dtype)
    for write in writes:
        write.wait()


def attend_kernel(lengths, query, key_value_fresh, kv_cache):
    slot_count = lengths.shape[0]
    kv_width = kv_cache.shape[2]
    kv_heads = kv_width // HEAD_SIZE
    group_width = QUERY_HEADS // KEY_VALUE_HEADS
    rows = kv_cache.shape[1]
    query_rows = jnp.transpose(
        query.reshape(slot_count, kv_heads, group_width, HEAD_SIZE), (1, 0, 2, 3)
    ).reshape(kv_heads, slot_count * group_width, HEAD_SIZE)
    fresh = jnp.transpose(
        key_value_fresh.reshape(2, slot_count, kv_heads, HEAD_SIZE), (0, 2, 1, 3)
    )
    out, store = pl.pallas_call(
        attention_kernel,
        out_shape=(
            jax.ShapeDtypeStruct((slot_count * kv_heads * group_width, HEAD_SIZE), jnp.bfloat16),
            jax.ShapeDtypeStruct(kv_cache.shape, kv_cache.dtype),
        ),
        in_specs=[
            pl.BlockSpec(memory_space=pltpu.SMEM),
            pl.BlockSpec(memory_space=pltpu.VMEM),
            pl.BlockSpec(memory_space=pltpu.VMEM),
            pl.BlockSpec(memory_space=pl.ANY),
            pl.BlockSpec(memory_space=pltpu.VMEM),
        ],
        out_specs=(pl.BlockSpec(memory_space=pltpu.VMEM), pl.BlockSpec(memory_space=pl.ANY)),
        scratch_shapes=[
            pltpu.VMEM((rows, kv_width), kv_cache.dtype),
            pltpu.VMEM((rows, kv_width), kv_cache.dtype),
            pltpu.SemaphoreType.DMA((2, rows // CHUNK_ROWS)),
            pltpu.SemaphoreType.DMA((2,)),
        ],
        cost_estimate=pl.CostEstimate(
            flops=4 * kv_heads * slot_count * group_width * rows * HEAD_SIZE,
            transcendentals=kv_heads * slot_count * group_width * rows,
            bytes_accessed=2 * rows * kv_width * 2,
        ),
    )(lengths, query_rows, fresh, kv_cache, key_value_fresh)
    return store, out.reshape(slot_count, kv_heads * group_width * HEAD_SIZE)


def slot_bounds(lengths):
    span_sizes = lengths + 1
    first_rows = jnp.cumsum(span_sizes) - span_sizes
    return (first_rows, first_rows + span_sizes)


def attend_rows(query_rows, key_value_store, row_base, first_rows, end_rows):
    block_rows = 128
    slot_count, kv_heads, group_width, head_dim = query_rows.shape
    pool_rows = key_value_store.shape[1]
    key_table = key_value_store[0].reshape(pool_rows, kv_heads, head_dim)
    value_table = key_value_store[1].reshape(pool_rows, kv_heads, head_dim)
    needed = jnp.clip(jnp.max(end_rows) - row_base, 0, pool_rows)
    block_count = (needed + block_rows - 1) // block_rows
    score_scale = head_dim ** (-0.5)

    def advance(block_index, carried):
        running_max, denominator, accumulated = carried
        offset = block_index * block_rows
        key_block = lax.dynamic_slice_in_dim(key_table, offset, block_rows, 0)
        value_block = lax.dynamic_slice_in_dim(value_table, offset, block_rows, 0)
        scores = (
            jnp.einsum("sngd,tnd->sngt", query_rows, key_block, preferred_element_type=jnp.float32)
            * score_scale
        )
        row_ids = row_base + offset + jnp.arange(block_rows, dtype=jnp.int32)
        inside = (
            (row_ids[None, :] >= first_rows[:, None]) & (row_ids[None, :] < end_rows[:, None])
        )[:, None, None, :]
        scores = jnp.where(inside, scores, NEGATIVE_FILL)
        new_max = jnp.maximum(running_max, jnp.max(scores, axis=-1))
        weights = jnp.where(inside, jnp.exp(scores - new_max[..., None]), 0.0)
        factor = jnp.exp(running_max - new_max)
        denominator = denominator * factor + jnp.sum(weights, axis=-1)
        accumulated = accumulated * factor[..., None] + jnp.einsum(
            "sngt,tnd->sngd",
            weights.astype(jnp.bfloat16),
            value_block,
            preferred_element_type=jnp.float32,
        )
        return (new_max, denominator, accumulated)

    initial = (
        jnp.full((slot_count, kv_heads, group_width), NEGATIVE_FILL, jnp.float32),
        jnp.zeros((slot_count, kv_heads, group_width), jnp.float32),
        jnp.zeros((slot_count, kv_heads, group_width, head_dim), jnp.float32),
    )
    return lax.fori_loop(0, block_count, advance, initial)


def body(
    lengths,
    assignment,
    query,
    key_value_fresh,
    kv_cache,
    hidden_in,
    out_weight,
    norm_gain,
    gate_up_weight,
    down_weight,
):
    slot_count = lengths.shape[0]
    first_rows, end_rows = slot_bounds(lengths)
    key_value_store, attended = attend_kernel(lengths, query, key_value_fresh, kv_cache)
    y_count, mdl_count = lax.axis_size("y"), lax.axis_size("mdl")
    weight_copies = jnp.broadcast_to(out_weight.T[None], (y_count,) + out_weight.T.shape)
    row_weight = lax.all_to_all(weight_copies, "y", 0, 0, tiled=True).reshape(-1, out_weight.shape[0])
    flat = attended.reshape(-1, 128)
    flat = lax.all_gather(flat, "c", axis=0, tiled=True)
    flat = lax.all_gather(flat, "z", axis=0, tiled=True)
    row_attended = flat.reshape(-1, attended.shape[1])
    row_slots = row_attended.shape[0]
    sub_width = hidden_in.shape[1]
    row_projected = lax.dot_general(
        row_weight, row_attended, (((1,), (1,)), ((), ())), preferred_element_type=jnp.float32
    )
    outgoing = row_projected.astype(jnp.bfloat16).reshape(y_count * mdl_count, sub_width, row_slots)
    arrived = lax.all_to_all(outgoing, ("y", "mdl"), 0, 0, tiled=True)
    head_sum = arrived.astype(jnp.float32).reshape(y_count, mdl_count, sub_width, row_slots).sum(1)
    head_share = jnp.transpose(head_sum, (1, 0, 2)).reshape(sub_width, y_count * row_slots).T
    total_rows = assignment.shape[0]
    selection = (
        assignment[:, None] == lax.broadcasted_iota(jnp.int32, (total_rows, total_rows), 1)
    ).astype(jnp.float32)
    placed = lax.dot_general(
        selection,
        head_share,
        (((0,), (0,)), ((), ())),
        precision=lax.Precision.HIGHEST,
        preferred_element_type=jnp.float32,
    )
    residual_wide = hidden_in.astype(jnp.float32) + placed
    residual = residual_wide.astype(jnp.bfloat16)
    local_wide = residual.astype(jnp.float32)
    col_groups = gate_up_weight.shape[1]
    sub_width = hidden_in.shape[1]
    gathered = jnp.transpose(gather_rows(residual.T), (2, 0, 1)).reshape(total_rows, col_groups * sub_width)
    widened = gathered.astype(jnp.float32)
    own_squares = jnp.sum(widened * widened, axis=1)
    gain_table = norm_gain.reshape(col_groups, lax.axis_size("mdl"), sub_width)
    gain_cols = lax.dynamic_index_in_dim(
        gain_table, lax.axis_index("mdl"), 1, keepdims=False
    ).reshape(col_groups * sub_width)
    unscaled = (widened * gain_cols).astype(jnp.bfloat16)
    gate_up = gate_up_weight.reshape(2, col_groups * sub_width, gate_up_weight.shape[4])
    partial_value = jnp.einsum("rk,gkf->gfr", unscaled, gate_up, preferred_element_type=jnp.float32)
    units = partial_value.shape[1]
    mdl_count = lax.axis_size("mdl")
    quarter = units // mdl_count
    squares_high = own_squares.astype(jnp.bfloat16)
    squares_low = (own_squares - squares_high.astype(jnp.float32)).astype(jnp.bfloat16)
    squares_pair = jnp.broadcast_to(jnp.stack([squares_high, squares_low])[None], (mdl_count, 2, total_rows))
    blocks = jnp.transpose(
        partial_value.astype(jnp.bfloat16).reshape(2, mdl_count, quarter, total_rows), (1, 0, 2, 3)
    ).reshape(mdl_count, 2 * quarter, total_rows)
    payload = jnp.concatenate([blocks, squares_pair], axis=1)
    summed_payload = lax.all_to_all(payload, "mdl", 0, 0, tiled=True).astype(jnp.float32).sum(0)
    square_sum = summed_payload[2 * quarter] + summed_payload[2 * quarter + 1]
    scale = lax.rsqrt(square_sum / D + 1e-05)
    gate_part = summed_payload[:quarter] * scale[None, :]
    up_part = summed_payload[quarter : 2 * quarter] * scale[None, :]
    hidden_part = (jax.nn.silu(gate_part) * up_part).astype(jnp.bfloat16)
    hidden_copies = jnp.broadcast_to(hidden_part[None], (mdl_count,) + hidden_part.shape)
    hidden = lax.all_to_all(hidden_copies, "mdl", 0, 0, tiled=True).reshape(units, total_rows)
    columns = down_weight.reshape(down_weight.shape[0], col_groups * sub_width)
    lowered = lax.dot_general(
        columns, hidden, (((0,), (0,)), ((), ())), preferred_element_type=jnp.float32
    )
    mesh_shape = (lax.axis_size("y"), lax.axis_size("z"), lax.axis_size("c"))
    summed = scatter_sum(lowered.reshape(mesh_shape + (sub_width * total_rows // 128, 128))).reshape(sub_width, total_rows)
    layer_out = (local_wide + summed.T).astype(jnp.bfloat16)
    return (layer_out, key_value_store)


def solution(mesh):
    req_size, mdl_size = mesh.devices.shape
    chips_y = 4
    split = Mesh(
        mesh.devices.reshape(chips_y, req_size // (2 * chips_y), 2, mdl_size),
        REQ + ("mdl",),
    )
    return jax.shard_map(
        body,
        mesh=split,
        in_specs=(
            P(REQ),
            P(),
            P(REQ, "mdl"),
            P(None, REQ, "mdl"),
            P(None, REQ, "mdl"),
            P(None, (REQ + ("mdl",))),
            P("mdl", REQ),
            P(),
            P(None, None, "mdl", None, REQ),
            P(REQ, None, "mdl", None),
        ),
        out_specs=(P(None, REQ + ("mdl",)), P(None, REQ, "mdl")),
        check_vma=False,
    )
```

```python
import jax
import jax.numpy as jnp
from jax import lax
from jax.experimental import pallas as pl
from jax.experimental.pallas import tpu as pltpu
from jax.sharding import Mesh, PartitionSpec as P

D = 5120
QUERY_HEADS = 32
KEY_VALUE_HEADS = 8
HEAD_SIZE = 128


NEGATIVE_FILL = -1e30
REQ = ("y", "z", "c")


def gather_rows(part):
    count = lax.axis_size(REQ)
    flat = part.reshape(-1, 128)
    flat = lax.all_gather(flat, "c", axis=0, tiled=True)
    flat = lax.all_gather(flat, "z", axis=0, tiled=True)
    copies = jnp.broadcast_to(flat[None], (lax.axis_size("y"),) + flat.shape)
    return lax.all_to_all(copies, "y", 0, 0, tiled=True).reshape((count,) + part.shape)


def scatter_sum(parts):
    wide = None
    for position, name in ((2, "c"), (0, "y"), (1, "z")):
        moved = lax.all_to_all(parts.astype(jnp.bfloat16), name, position, position, tiled=True)
        wide = moved.astype(jnp.float32).sum(position, keepdims=True)
        parts = wide
    return wide


def mdl_sum(values, wires):
    count = lax.axis_size("mdl")
    sent = tuple(v.astype(w) for v, w in zip(values, wires))
    totals = [v.astype(jnp.float32) for v in values]
    for shift in range(1, count):
        pairs = [(i, (i + shift) % count) for i in range(count)]
        arrived = lax.ppermute(sent, "mdl", pairs)
        totals = [t + a.astype(jnp.float32) for t, a in zip(totals, arrived)]
    return totals


def mdl_scatter_sum(value, wire):
    count = lax.axis_size("mdl")
    height = value.shape[0] // count
    blocks = value.astype(wire).reshape((count, height * value.shape[1] // 128, 128))
    moved = lax.all_to_all(blocks, "mdl", 0, 0, tiled=True)
    return moved.astype(jnp.float32).sum(0).reshape(height, value.shape[1])


CHUNK_ROWS = 256


def attention_kernel(
    lengths_ref, query_ref, cache_hbm, fresh_rows, out_ref, store_hbm, keys, values, sems, write_sems
):
    rows = keys.shape[0]
    chunks = rows // CHUNK_ROWS
    copies = []
    for chunk in range(chunks):
        window = pl.ds(chunk * CHUNK_ROWS, CHUNK_ROWS)
        for which, target in ((0, keys), (1, values)):
            copy = pltpu.make_async_copy(cache_hbm.at[which, window], target.at[window], sems.at[which, chunk])
            copy.start()
            copies.append(copy)
    slot_count = lengths_ref.shape[0]
    kv_heads, row_count, head_dim = query_ref.shape
    group_width = row_count // slot_count
    row_slot = lax.broadcasted_iota(jnp.int32, (row_count, 1), 0) // group_width
    first = jnp.zeros((row_count, 1), jnp.int32)
    end = jnp.zeros((row_count, 1), jnp.int32)
    start = jnp.int32(0)
    for slot in range(slot_count):
        length = lengths_ref[slot]
        first = jnp.where(row_slot == slot, start, first)
        end = jnp.where(row_slot == slot, start + length, end)
        start = start + length + 1
    columns = lax.broadcasted_iota(jnp.int32, (row_count, rows), 1)
    inside = (columns >= first) & (columns < end)
    pick = (lax.broadcasted_iota(jnp.int32, (row_count, slot_count), 1) == row_slot)
    for copy in copies:
        copy.wait()
    tile = 16
    within = lax.broadcasted_iota(jnp.int32, (tile, keys.shape[1]), 0)
    start = jnp.int32(0)
    for slot in range(slot_count):
        row = start + lengths_ref[slot]
        base = pl.multiple_of((row // tile) * tile, tile)
        for which, target in ((0, keys), (1, values)):
            block = target[pl.ds(base, tile), :]
            fresh_row = jnp.broadcast_to(fresh_rows[which, pl.ds(slot, 1), :], block.shape)
            target[pl.ds(base, tile), :] = jnp.where(within == row - base, fresh_row, block)
        start = row + 1
    writes = []
    for which, source in ((0, keys), (1, values)):
        write = pltpu.make_async_copy(source, store_hbm.at[which], write_sems.at[which])
        write.start()
        writes.append(write)
    score_scale = head_dim ** (-0.5)
    results = []
    for head in range(kv_heads):
        lanes = pl.ds(head * head_dim, head_dim)
        query_rows = query_ref[head]
        scores = lax.dot_general(
            query_rows, keys[:, lanes], (((1,), (1,)), ((), ())), preferred_element_type=jnp.float32
        ) * score_scale
        fresh_scores = lax.dot_general(
            query_rows, fresh_rows[0, :, lanes], (((1,), (1,)), ((), ())), preferred_element_type=jnp.float32
        ) * score_scale
        new_score = jnp.sum(jnp.where(pick, fresh_scores, 0.0), axis=1, keepdims=True)
        scores = jnp.where(inside, scores, NEGATIVE_FILL)
        top = jnp.maximum(jnp.max(scores, axis=1, keepdims=True), new_score)
        weights = jnp.where(inside, jnp.exp(scores - top), 0.0)
        new_weight = jnp.exp(new_score - top)
        denominator = jnp.sum(weights, axis=1, keepdims=True) + new_weight
        mixed = jnp.dot(weights.astype(jnp.bfloat16), values[:, lanes], preferred_element_type=jnp.float32)
        fresh_values = jnp.dot(pick.astype(jnp.bfloat16), fresh_rows[1, :, lanes], preferred_element_type=jnp.float32)
        mixed = mixed + new_weight.astype(jnp.bfloat16).astype(jnp.float32) * fresh_values
        results.append(mixed / denominator)
    pieces = [
        results[head][slot * group_width : (slot + 1) * group_width]
        for slot in range(slot_count)
        for head in range(kv_heads)
    ]
    out_ref[...] = jnp.concatenate(pieces, axis=0).astype(out_ref.dtype)
    for write in writes:
        write.wait()


def attend_kernel(lengths, query, key_value_fresh, kv_cache):
    slot_count = lengths.shape[0]
    kv_width = kv_cache.shape[2]
    kv_heads = kv_width // HEAD_SIZE
    group_width = QUERY_HEADS // KEY_VALUE_HEADS
    rows = kv_cache.shape[1]
    query_rows = jnp.transpose(
        query.reshape(slot_count, kv_heads, group_width, HEAD_SIZE), (1, 0, 2, 3)
    ).reshape(kv_heads, slot_count * group_width, HEAD_SIZE)
    out, store = pl.pallas_call(
        attention_kernel,
        out_shape=(
            jax.ShapeDtypeStruct((slot_count * kv_heads * group_width, HEAD_SIZE), jnp.bfloat16),
            jax.ShapeDtypeStruct(kv_cache.shape, kv_cache.dtype),
        ),
        in_specs=[
            pl.BlockSpec(memory_space=pltpu.SMEM),
            pl.BlockSpec(memory_space=pltpu.VMEM),
            pl.BlockSpec(memory_space=pl.ANY),
            pl.BlockSpec(memory_space=pltpu.VMEM),
        ],
        out_specs=(pl.BlockSpec(memory_space=pltpu.VMEM), pl.BlockSpec(memory_space=pl.ANY)),
        scratch_shapes=[
            pltpu.VMEM((rows, kv_width), kv_cache.dtype),
            pltpu.VMEM((rows, kv_width), kv_cache.dtype),
            pltpu.SemaphoreType.DMA((2, rows // CHUNK_ROWS)),
            pltpu.SemaphoreType.DMA((2,)),
        ],
        cost_estimate=pl.CostEstimate(
            flops=4 * kv_heads * slot_count * group_width * rows * HEAD_SIZE,
            transcendentals=kv_heads * slot_count * group_width * rows,
            bytes_accessed=2 * rows * kv_width * 2,
        ),
    )(lengths, query_rows, kv_cache, key_value_fresh)
    return store, out.reshape(slot_count, kv_heads * group_width * HEAD_SIZE)


def slot_bounds(lengths):
    span_sizes = lengths + 1
    first_rows = jnp.cumsum(span_sizes) - span_sizes
    return (first_rows, first_rows + span_sizes)


def attend_rows(query_rows, key_value_store, row_base, first_rows, end_rows):
    block_rows = 128
    slot_count, kv_heads, group_width, head_dim = query_rows.shape
    pool_rows = key_value_store.shape[1]
    key_table = key_value_store[0].reshape(pool_rows, kv_heads, head_dim)
    value_table = key_value_store[1].reshape(pool_rows, kv_heads, head_dim)
    needed = jnp.clip(jnp.max(end_rows) - row_base, 0, pool_rows)
    block_count = (needed + block_rows - 1) // block_rows
    score_scale = head_dim ** (-0.5)

    def advance(block_index, carried):
        running_max, denominator, accumulated = carried
        offset = block_index * block_rows
        key_block = lax.dynamic_slice_in_dim(key_table, offset, block_rows, 0)
        value_block = lax.dynamic_slice_in_dim(value_table, offset, block_rows, 0)
        scores = (
            jnp.einsum("sngd,tnd->sngt", query_rows, key_block, preferred_element_type=jnp.float32)
            * score_scale
        )
        row_ids = row_base + offset + jnp.arange(block_rows, dtype=jnp.int32)
        inside = (
            (row_ids[None, :] >= first_rows[:, None]) & (row_ids[None, :] < end_rows[:, None])
        )[:, None, None, :]
        scores = jnp.where(inside, scores, NEGATIVE_FILL)
        new_max = jnp.maximum(running_max, jnp.max(scores, axis=-1))
        weights = jnp.where(inside, jnp.exp(scores - new_max[..., None]), 0.0)
        factor = jnp.exp(running_max - new_max)
        denominator = denominator * factor + jnp.sum(weights, axis=-1)
        accumulated = accumulated * factor[..., None] + jnp.einsum(
            "sngt,tnd->sngd",
            weights.astype(jnp.bfloat16),
            value_block,
            preferred_element_type=jnp.float32,
        )
        return (new_max, denominator, accumulated)

    initial = (
        jnp.full((slot_count, kv_heads, group_width), NEGATIVE_FILL, jnp.float32),
        jnp.zeros((slot_count, kv_heads, group_width), jnp.float32),
        jnp.zeros((slot_count, kv_heads, group_width, head_dim), jnp.float32),
    )
    return lax.fori_loop(0, block_count, advance, initial)


def body(
    lengths,
    assignment,
    query,
    key_value_fresh,
    kv_cache,
    hidden_in,
    out_weight,
    norm_gain,
    gate_up_weight,
    down_weight,
):
    slot_count = lengths.shape[0]
    first_rows, end_rows = slot_bounds(lengths)
    key_value_store, attended = attend_kernel(lengths, query, key_value_fresh, kv_cache)
    y_count, mdl_count = lax.axis_size("y"), lax.axis_size("mdl")
    weight_copies = jnp.broadcast_to(out_weight.T[None], (y_count,) + out_weight.T.shape)
    row_weight = lax.all_to_all(weight_copies, "y", 0, 0, tiled=True).reshape(-1, out_weight.shape[0])
    flat = attended.reshape(-1, 128)
    flat = lax.all_gather(flat, "c", axis=0, tiled=True)
    flat = lax.all_gather(flat, "z", axis=0, tiled=True)
    row_attended = flat.reshape(-1, attended.shape[1])
    row_slots = row_attended.shape[0]
    sub_width = hidden_in.shape[1]
    row_projected = lax.dot_general(
        row_weight, row_attended, (((1,), (1,)), ((), ())), preferred_element_type=jnp.float32
    )
    outgoing = row_projected.astype(jnp.bfloat16).reshape(y_count * mdl_count, sub_width, row_slots)
    arrived = lax.all_to_all(outgoing, ("y", "mdl"), 0, 0, tiled=True)
    head_sum = arrived.astype(jnp.float32).reshape(y_count, mdl_count, sub_width, row_slots).sum(1)
    head_share = jnp.transpose(head_sum, (1, 0, 2)).reshape(sub_width, y_count * row_slots).T
    total_rows = assignment.shape[0]
    selection = (
        assignment[:, None] == lax.broadcasted_iota(jnp.int32, (total_rows, total_rows), 1)
    ).astype(jnp.float32)
    placed = lax.dot_general(
        selection,
        head_share,
        (((0,), (0,)), ((), ())),
        precision=lax.Precision.HIGHEST,
        preferred_element_type=jnp.float32,
    )
    residual_wide = hidden_in.astype(jnp.float32) + placed
    residual = residual_wide.astype(jnp.bfloat16)
    local_wide = residual.astype(jnp.float32)
    col_groups = gate_up_weight.shape[1]
    sub_width = hidden_in.shape[1]
    gathered = jnp.transpose(gather_rows(residual.T), (2, 0, 1)).reshape(total_rows, col_groups * sub_width)
    widened = gathered.astype(jnp.float32)
    own_squares = jnp.sum(widened * widened, axis=1)
    gain_table = norm_gain.reshape(col_groups, lax.axis_size("mdl"), sub_width)
    gain_cols = lax.dynamic_index_in_dim(
        gain_table, lax.axis_index("mdl"), 1, keepdims=False
    ).reshape(col_groups * sub_width)
    unscaled = (widened * gain_cols).astype(jnp.bfloat16)
    gate_up = gate_up_weight.reshape(2, col_groups * sub_width, gate_up_weight.shape[4])
    partial_value = jnp.einsum("rk,gkf->gfr", unscaled, gate_up, preferred_element_type=jnp.float32)
    units = partial_value.shape[1]
    mdl_count = lax.axis_size("mdl")
    quarter = units // mdl_count
    squares_high = own_squares.astype(jnp.bfloat16)
    squares_low = (own_squares - squares_high.astype(jnp.float32)).astype(jnp.bfloat16)
    squares_pair = jnp.broadcast_to(jnp.stack([squares_high, squares_low])[None], (mdl_count, 2, total_rows))
    blocks = jnp.transpose(
        partial_value.astype(jnp.bfloat16).reshape(2, mdl_count, quarter, total_rows), (1, 0, 2, 3)
    ).reshape(mdl_count, 2 * quarter, total_rows)
    payload = jnp.concatenate([blocks, squares_pair], axis=1)
    summed_payload = lax.all_to_all(payload, "mdl", 0, 0, tiled=True).astype(jnp.float32).sum(0)
    square_sum = summed_payload[2 * quarter] + summed_payload[2 * quarter + 1]
    scale = lax.rsqrt(square_sum / D + 1e-05)
    gate_part = summed_payload[:quarter] * scale[None, :]
    up_part = summed_payload[quarter : 2 * quarter] * scale[None, :]
    hidden_part = (jax.nn.silu(gate_part) * up_part).astype(jnp.bfloat16)
    hidden_copies = jnp.broadcast_to(hidden_part[None], (mdl_count,) + hidden_part.shape)
    hidden = lax.all_to_all(hidden_copies, "mdl", 0, 0, tiled=True).reshape(units, total_rows)
    columns = down_weight.reshape(down_weight.shape[0], col_groups * sub_width)
    lowered = lax.dot_general(
        columns, hidden, (((0,), (0,)), ((), ())), preferred_element_type=jnp.float32
    )
    mesh_shape = (lax.axis_size("y"), lax.axis_size("z"), lax.axis_size("c"))
    summed = scatter_sum(lowered.reshape(mesh_shape + (sub_width * total_rows // 128, 128))).reshape(sub_width, total_rows)
    layer_out = (local_wide + summed.T).astype(jnp.bfloat16)
    return (layer_out, key_value_store)


def solution(mesh):
    req_size, mdl_size = mesh.devices.shape
    chips_y = 4
    split = Mesh(
        mesh.devices.reshape(chips_y, req_size // (2 * chips_y), 2, mdl_size),
        REQ + ("mdl",),
    )
    return jax.shard_map(
        body,
        mesh=split,
        in_specs=(
            P(REQ),
            P(),
            P(REQ, "mdl"),
            P(None, REQ, "mdl"),
            P(None, REQ, "mdl"),
            P(None, (REQ + ("mdl",))),
            P("mdl", REQ),
            P(),
            P(None, None, "mdl", None, REQ),
            P(REQ, None, "mdl", None),
        ),
        out_specs=(P(None, REQ + ("mdl",)), P(None, REQ, "mdl")),
        check_vma=False,
    )
```

```python
import jax
import jax.numpy as jnp
from jax import lax
from jax.experimental import pallas as pl
from jax.experimental.pallas import tpu as pltpu
from jax.sharding import Mesh, PartitionSpec as P

D = 5120
QUERY_HEADS = 32
KEY_VALUE_HEADS = 8
HEAD_SIZE = 128


NEGATIVE_FILL = -1e30
REQ = ("y", "z", "c")


def gather_rows(part):
    count = lax.axis_size(REQ)
    flat = part.reshape(-1, 128)
    flat = lax.all_gather(flat, "c", axis=0, tiled=True)
    flat = lax.all_gather(flat, "z", axis=0, tiled=True)
    copies = jnp.broadcast_to(flat[None], (lax.axis_size("y"),) + flat.shape)
    return lax.all_to_all(copies, "y", 0, 0, tiled=True).reshape((count,) + part.shape)


def scatter_sum(parts):
    wide = None
    for position, name in ((2, "c"), (0, "y"), (1, "z")):
        moved = lax.all_to_all(parts.astype(jnp.bfloat16), name, position, position, tiled=True)
        wide = moved.astype(jnp.float32).sum(position, keepdims=True)
        parts = wide
    return wide


def mdl_sum(values, wires):
    count = lax.axis_size("mdl")
    sent = tuple(v.astype(w) for v, w in zip(values, wires))
    totals = [v.astype(jnp.float32) for v in values]
    for shift in range(1, count):
        pairs = [(i, (i + shift) % count) for i in range(count)]
        arrived = lax.ppermute(sent, "mdl", pairs)
        totals = [t + a.astype(jnp.float32) for t, a in zip(totals, arrived)]
    return totals


def mdl_scatter_sum(value, wire):
    count = lax.axis_size("mdl")
    height = value.shape[0] // count
    blocks = value.astype(wire).reshape((count, height * value.shape[1] // 128, 128))
    moved = lax.all_to_all(blocks, "mdl", 0, 0, tiled=True)
    return moved.astype(jnp.float32).sum(0).reshape(height, value.shape[1])


CHUNK_ROWS = 256


def attention_kernel(
    lengths_ref, query_ref, cache_hbm, fresh_rows, out_ref, store_hbm, keys, values, sems, write_sems
):
    rows = keys.shape[0]
    chunks = rows // CHUNK_ROWS
    copies = []
    for chunk in range(chunks):
        window = pl.ds(chunk * CHUNK_ROWS, CHUNK_ROWS)
        for which, target in ((0, keys), (1, values)):
            copy = pltpu.make_async_copy(cache_hbm.at[which, window], target.at[window], sems.at[which, chunk])
            copy.start()
            copies.append(copy)
    slot_count = lengths_ref.shape[0]
    head_dim = HEAD_SIZE
    kv_heads = keys.shape[1] // head_dim
    row_count = query_ref.shape[1] // kv_heads // head_dim * slot_count
    group_width = row_count // slot_count
    row_slot = lax.broadcasted_iota(jnp.int32, (row_count, 1), 0) // group_width
    first = jnp.zeros((row_count, 1), jnp.int32)
    end = jnp.zeros((row_count, 1), jnp.int32)
    start = jnp.int32(0)
    for slot in range(slot_count):
        length = lengths_ref[slot]
        first = jnp.where(row_slot == slot, start, first)
        end = jnp.where(row_slot == slot, start + length, end)
        start = start + length + 1
    columns = lax.broadcasted_iota(jnp.int32, (row_count, rows), 1)
    inside = (columns >= first) & (columns < end)
    pick = (lax.broadcasted_iota(jnp.int32, (row_count, slot_count), 1) == row_slot)
    for copy in copies:
        copy.wait()
    tile = 16
    within = lax.broadcasted_iota(jnp.int32, (tile, keys.shape[1]), 0)
    start = jnp.int32(0)
    for slot in range(slot_count):
        row = start + lengths_ref[slot]
        base = pl.multiple_of((row // tile) * tile, tile)
        for which, target in ((0, keys), (1, values)):
            block = target[pl.ds(base, tile), :]
            fresh_row = jnp.broadcast_to(fresh_rows[which, pl.ds(slot, 1), :], block.shape)
            target[pl.ds(base, tile), :] = jnp.where(within == row - base, fresh_row, block)
        start = row + 1
    writes = []
    for which, source in ((0, keys), (1, values)):
        write = pltpu.make_async_copy(source, store_hbm.at[which], write_sems.at[which])
        write.start()
        writes.append(write)
    score_scale = head_dim ** (-0.5)
    results = []
    wide_query = query_ref[...].astype(jnp.float32)
    for head in range(kv_heads):
        lanes = pl.ds(head * head_dim, head_dim)
        query_rows = jnp.concatenate(
            [
                wide_query[slot : slot + 1, (head * group_width + g) * head_dim : (head * group_width + g + 1) * head_dim]
                for slot in range(slot_count)
                for g in range(group_width)
            ],
            axis=0,
        ).astype(query_ref.dtype)
        scores = lax.dot_general(
            query_rows, keys[:, lanes], (((1,), (1,)), ((), ())), preferred_element_type=jnp.float32
        ) * score_scale
        fresh_scores = lax.dot_general(
            query_rows, fresh_rows[0, :, lanes], (((1,), (1,)), ((), ())), preferred_element_type=jnp.float32
        ) * score_scale
        new_score = jnp.sum(jnp.where(pick, fresh_scores, 0.0), axis=1, keepdims=True)
        scores = jnp.where(inside, scores, NEGATIVE_FILL)
        top = jnp.maximum(jnp.max(scores, axis=1, keepdims=True), new_score)
        weights = jnp.where(inside, jnp.exp(scores - top), 0.0)
        new_weight = jnp.exp(new_score - top)
        denominator = jnp.sum(weights, axis=1, keepdims=True) + new_weight
        mixed = jnp.dot(weights.astype(jnp.bfloat16), values[:, lanes], preferred_element_type=jnp.float32)
        fresh_values = jnp.dot(pick.astype(jnp.bfloat16), fresh_rows[1, :, lanes], preferred_element_type=jnp.float32)
        mixed = mixed + new_weight.astype(jnp.bfloat16).astype(jnp.float32) * fresh_values
        results.append(mixed / denominator)
    pieces = [
        results[head][slot * group_width : (slot + 1) * group_width]
        for slot in range(slot_count)
        for head in range(kv_heads)
    ]
    out_ref[...] = jnp.concatenate(pieces, axis=0).astype(out_ref.dtype)
    for write in writes:
        write.wait()


def attend_kernel(lengths, query, key_value_fresh, kv_cache):
    slot_count = lengths.shape[0]
    kv_width = kv_cache.shape[2]
    kv_heads = kv_width // HEAD_SIZE
    group_width = QUERY_HEADS // KEY_VALUE_HEADS
    rows = kv_cache.shape[1]
    out, store = pl.pallas_call(
        attention_kernel,
        out_shape=(
            jax.ShapeDtypeStruct((slot_count * kv_heads * group_width, HEAD_SIZE), jnp.bfloat16),
            jax.ShapeDtypeStruct(kv_cache.shape, kv_cache.dtype),
        ),
        in_specs=[
            pl.BlockSpec(memory_space=pltpu.SMEM),
            pl.BlockSpec(memory_space=pltpu.VMEM),
            pl.BlockSpec(memory_space=pl.ANY),
            pl.BlockSpec(memory_space=pltpu.VMEM),
        ],
        out_specs=(pl.BlockSpec(memory_space=pltpu.VMEM), pl.BlockSpec(memory_space=pl.ANY)),
        scratch_shapes=[
            pltpu.VMEM((rows, kv_width), kv_cache.dtype),
            pltpu.VMEM((rows, kv_width), kv_cache.dtype),
            pltpu.SemaphoreType.DMA((2, rows // CHUNK_ROWS)),
            pltpu.SemaphoreType.DMA((2,)),
        ],
        cost_estimate=pl.CostEstimate(
            flops=4 * kv_heads * slot_count * group_width * rows * HEAD_SIZE,
            transcendentals=kv_heads * slot_count * group_width * rows,
            bytes_accessed=2 * rows * kv_width * 2,
        ),
    )(lengths, query, kv_cache, key_value_fresh)
    return store, out.reshape(slot_count, kv_heads * group_width * HEAD_SIZE)


def slot_bounds(lengths):
    span_sizes = lengths + 1
    first_rows = jnp.cumsum(span_sizes) - span_sizes
    return (first_rows, first_rows + span_sizes)


def attend_rows(query_rows, key_value_store, row_base, first_rows, end_rows):
    block_rows = 128
    slot_count, kv_heads, group_width, head_dim = query_rows.shape
    pool_rows = key_value_store.shape[1]
    key_table = key_value_store[0].reshape(pool_rows, kv_heads, head_dim)
    value_table = key_value_store[1].reshape(pool_rows, kv_heads, head_dim)
    needed = jnp.clip(jnp.max(end_rows) - row_base, 0, pool_rows)
    block_count = (needed + block_rows - 1) // block_rows
    score_scale = head_dim ** (-0.5)

    def advance(block_index, carried):
        running_max, denominator, accumulated = carried
        offset = block_index * block_rows
        key_block = lax.dynamic_slice_in_dim(key_table, offset, block_rows, 0)
        value_block = lax.dynamic_slice_in_dim(value_table, offset, block_rows, 0)
        scores = (
            jnp.einsum("sngd,tnd->sngt", query_rows, key_block, preferred_element_type=jnp.float32)
            * score_scale
        )
        row_ids = row_base + offset + jnp.arange(block_rows, dtype=jnp.int32)
        inside = (
            (row_ids[None, :] >= first_rows[:, None]) & (row_ids[None, :] < end_rows[:, None])
        )[:, None, None, :]
        scores = jnp.where(inside, scores, NEGATIVE_FILL)
        new_max = jnp.maximum(running_max, jnp.max(scores, axis=-1))
        weights = jnp.where(inside, jnp.exp(scores - new_max[..., None]), 0.0)
        factor = jnp.exp(running_max - new_max)
        denominator = denominator * factor + jnp.sum(weights, axis=-1)
        accumulated = accumulated * factor[..., None] + jnp.einsum(
            "sngt,tnd->sngd",
            weights.astype(jnp.bfloat16),
            value_block,
            preferred_element_type=jnp.float32,
        )
        return (new_max, denominator, accumulated)

    initial = (
        jnp.full((slot_count, kv_heads, group_width), NEGATIVE_FILL, jnp.float32),
        jnp.zeros((slot_count, kv_heads, group_width), jnp.float32),
        jnp.zeros((slot_count, kv_heads, group_width, head_dim), jnp.float32),
    )
    return lax.fori_loop(0, block_count, advance, initial)


def body(
    lengths,
    assignment,
    query,
    key_value_fresh,
    kv_cache,
    hidden_in,
    out_weight,
    norm_gain,
    gate_up_weight,
    down_weight,
):
    slot_count = lengths.shape[0]
    first_rows, end_rows = slot_bounds(lengths)
    key_value_store, attended = attend_kernel(lengths, query, key_value_fresh, kv_cache)
    y_count, mdl_count = lax.axis_size("y"), lax.axis_size("mdl")
    weight_copies = jnp.broadcast_to(out_weight.T[None], (y_count,) + out_weight.T.shape)
    row_weight = lax.all_to_all(weight_copies, "y", 0, 0, tiled=True).reshape(-1, out_weight.shape[0])
    flat = attended.reshape(-1, 128)
    flat = lax.all_gather(flat, "c", axis=0, tiled=True)
    flat = lax.all_gather(flat, "z", axis=0, tiled=True)
    row_attended = flat.reshape(-1, attended.shape[1])
    row_slots = row_attended.shape[0]
    sub_width = hidden_in.shape[1]
    row_projected = lax.dot_general(
        row_weight, row_attended, (((1,), (1,)), ((), ())), preferred_element_type=jnp.float32
    )
    outgoing = row_projected.astype(jnp.bfloat16).reshape(y_count * mdl_count, sub_width, row_slots)
    arrived = lax.all_to_all(outgoing, ("y", "mdl"), 0, 0, tiled=True)
    head_sum = arrived.astype(jnp.float32).reshape(y_count, mdl_count, sub_width, row_slots).sum(1)
    head_share = jnp.transpose(head_sum, (1, 0, 2)).reshape(sub_width, y_count * row_slots).T
    total_rows = assignment.shape[0]
    selection = (
        assignment[:, None] == lax.broadcasted_iota(jnp.int32, (total_rows, total_rows), 1)
    ).astype(jnp.float32)
    placed = lax.dot_general(
        selection,
        head_share,
        (((0,), (0,)), ((), ())),
        precision=lax.Precision.HIGHEST,
        preferred_element_type=jnp.float32,
    )
    residual_wide = hidden_in.astype(jnp.float32) + placed
    residual = residual_wide.astype(jnp.bfloat16)
    local_wide = residual.astype(jnp.float32)
    col_groups = gate_up_weight.shape[1]
    sub_width = hidden_in.shape[1]
    gathered = jnp.transpose(gather_rows(residual.T), (2, 0, 1)).reshape(total_rows, col_groups * sub_width)
    widened = gathered.astype(jnp.float32)
    own_squares = jnp.sum(widened * widened, axis=1)
    gain_table = norm_gain.reshape(col_groups, lax.axis_size("mdl"), sub_width)
    gain_cols = lax.dynamic_index_in_dim(
        gain_table, lax.axis_index("mdl"), 1, keepdims=False
    ).reshape(col_groups * sub_width)
    unscaled = (widened * gain_cols).astype(jnp.bfloat16)
    gate_up = gate_up_weight.reshape(2, col_groups * sub_width, gate_up_weight.shape[4])
    partial_value = jnp.einsum("rk,gkf->gfr", unscaled, gate_up, preferred_element_type=jnp.float32)
    units = partial_value.shape[1]
    mdl_count = lax.axis_size("mdl")
    quarter = units // mdl_count
    squares_high = own_squares.astype(jnp.bfloat16)
    squares_low = (own_squares - squares_high.astype(jnp.float32)).astype(jnp.bfloat16)
    squares_pair = jnp.broadcast_to(jnp.stack([squares_high, squares_low])[None], (mdl_count, 2, total_rows))
    blocks = jnp.transpose(
        partial_value.astype(jnp.bfloat16).reshape(2, mdl_count, quarter, total_rows), (1, 0, 2, 3)
    ).reshape(mdl_count, 2 * quarter, total_rows)
    payload = jnp.concatenate([blocks, squares_pair], axis=1)
    summed_payload = lax.all_to_all(payload, "mdl", 0, 0, tiled=True).astype(jnp.float32).sum(0)
    square_sum = summed_payload[2 * quarter] + summed_payload[2 * quarter + 1]
    scale = lax.rsqrt(square_sum / D + 1e-05)
    gate_part = summed_payload[:quarter] * scale[None, :]
    up_part = summed_payload[quarter : 2 * quarter] * scale[None, :]
    hidden_part = (jax.nn.silu(gate_part) * up_part).astype(jnp.bfloat16)
    hidden_copies = jnp.broadcast_to(hidden_part[None], (mdl_count,) + hidden_part.shape)
    hidden = lax.all_to_all(hidden_copies, "mdl", 0, 0, tiled=True).reshape(units, total_rows)
    columns = down_weight.reshape(down_weight.shape[0], col_groups * sub_width)
    lowered = lax.dot_general(
        columns, hidden, (((0,), (0,)), ((), ())), preferred_element_type=jnp.float32
    )
    mesh_shape = (lax.axis_size("y"), lax.axis_size("z"), lax.axis_size("c"))
    summed = scatter_sum(lowered.reshape(mesh_shape + (sub_width * total_rows // 128, 128))).reshape(sub_width, total_rows)
    layer_out = (local_wide + summed.T).astype(jnp.bfloat16)
    return (layer_out, key_value_store)


def solution(mesh):
    req_size, mdl_size = mesh.devices.shape
    chips_y = 4
    split = Mesh(
        mesh.devices.reshape(chips_y, req_size // (2 * chips_y), 2, mdl_size),
        REQ + ("mdl",),
    )
    return jax.shard_map(
        body,
        mesh=split,
        in_specs=(
            P(REQ),
            P(),
            P(REQ, "mdl"),
            P(None, REQ, "mdl"),
            P(None, REQ, "mdl"),
            P(None, (REQ + ("mdl",))),
            P("mdl", REQ),
            P(),
            P(None, None, "mdl", None, REQ),
            P(REQ, None, "mdl", None),
        ),
        out_specs=(P(None, REQ + ("mdl",)), P(None, REQ, "mdl")),
        check_vma=False,
    )
```

```python
import jax
import jax.numpy as jnp
from jax import lax
from jax.experimental import pallas as pl
from jax.experimental.pallas import tpu as pltpu
from jax.sharding import Mesh, PartitionSpec as P

D = 5120
QUERY_HEADS = 32
KEY_VALUE_HEADS = 8
HEAD_SIZE = 128


NEGATIVE_FILL = -1e30
REQ = ("y", "z", "c")


def gather_rows(part):
    count = lax.axis_size(REQ)
    flat = part.reshape(-1, 128)
    flat = lax.all_gather(flat, "c", axis=0, tiled=True)
    flat = lax.all_gather(flat, "z", axis=0, tiled=True)
    copies = jnp.broadcast_to(flat[None], (lax.axis_size("y"),) + flat.shape)
    return lax.all_to_all(copies, "y", 0, 0, tiled=True).reshape((count,) + part.shape)


def scatter_sum(parts):
    wide = None
    for position, name in ((2, "c"), (0, "y"), (1, "z")):
        moved = lax.all_to_all(parts.astype(jnp.bfloat16), name, position, position, tiled=True)
        wide = moved.astype(jnp.float32).sum(position, keepdims=True)
        parts = wide
    return wide


def mdl_sum(values, wires):
    count = lax.axis_size("mdl")
    sent = tuple(v.astype(w) for v, w in zip(values, wires))
    totals = [v.astype(jnp.float32) for v in values]
    for shift in range(1, count):
        pairs = [(i, (i + shift) % count) for i in range(count)]
        arrived = lax.ppermute(sent, "mdl", pairs)
        totals = [t + a.astype(jnp.float32) for t, a in zip(totals, arrived)]
    return totals


def mdl_scatter_sum(value, wire):
    count = lax.axis_size("mdl")
    height = value.shape[0] // count
    blocks = value.astype(wire).reshape((count, height * value.shape[1] // 128, 128))
    moved = lax.all_to_all(blocks, "mdl", 0, 0, tiled=True)
    return moved.astype(jnp.float32).sum(0).reshape(height, value.shape[1])


CHUNK_ROWS = 512


def attention_kernel(
    lengths_ref, query_ref, cache_hbm, fresh_rows, out_ref, store_hbm, keys, values, sems, write_sems
):
    rows = keys.shape[0]
    chunks = rows // CHUNK_ROWS
    copies = []
    for chunk in range(chunks):
        window = pl.ds(chunk * CHUNK_ROWS, CHUNK_ROWS)
        for which, target in ((0, keys), (1, values)):
            copy = pltpu.make_async_copy(cache_hbm.at[which, window], target.at[window], sems.at[which, chunk])
            copy.start()
            copies.append(copy)
    slot_count = lengths_ref.shape[0]
    head_dim = HEAD_SIZE
    kv_heads = keys.shape[1] // head_dim
    row_count = query_ref.shape[1] // kv_heads // head_dim * slot_count
    group_width = row_count // slot_count
    row_slot = lax.broadcasted_iota(jnp.int32, (row_count, 1), 0) // group_width
    first = jnp.zeros((row_count, 1), jnp.int32)
    end = jnp.zeros((row_count, 1), jnp.int32)
    start = jnp.int32(0)
    for slot in range(slot_count):
        length = lengths_ref[slot]
        first = jnp.where(row_slot == slot, start, first)
        end = jnp.where(row_slot == slot, start + length, end)
        start = start + length + 1
    columns = lax.broadcasted_iota(jnp.int32, (row_count, rows), 1)
    inside = (columns >= first) & (columns < end)
    pick = (lax.broadcasted_iota(jnp.int32, (row_count, slot_count), 1) == row_slot)
    for copy in copies:
        copy.wait()
    tile = 16
    within = lax.broadcasted_iota(jnp.int32, (tile, keys.shape[1]), 0)
    start = jnp.int32(0)
    for slot in range(slot_count):
        row = start + lengths_ref[slot]
        base = pl.multiple_of((row // tile) * tile, tile)
        for which, target in ((0, keys), (1, values)):
            block = target[pl.ds(base, tile), :]
            fresh_row = jnp.broadcast_to(fresh_rows[which, pl.ds(slot, 1), :], block.shape)
            target[pl.ds(base, tile), :] = jnp.where(within == row - base, fresh_row, block)
        start = row + 1
    writes = []
    for which, source in ((0, keys), (1, values)):
        write = pltpu.make_async_copy(source, store_hbm.at[which], write_sems.at[which])
        write.start()
        writes.append(write)
    score_scale = head_dim ** (-0.5)
    results = []
    wide_query = query_ref[...].astype(jnp.float32)
    for head in range(kv_heads):
        lanes = pl.ds(head * head_dim, head_dim)
        query_rows = jnp.concatenate(
            [
                wide_query[slot : slot + 1, (head * group_width + g) * head_dim : (head * group_width + g + 1) * head_dim]
                for slot in range(slot_count)
                for g in range(group_width)
            ],
            axis=0,
        ).astype(query_ref.dtype)
        scores = lax.dot_general(
            query_rows, keys[:, lanes], (((1,), (1,)), ((), ())), preferred_element_type=jnp.float32
        ) * score_scale
        fresh_scores = lax.dot_general(
            query_rows, fresh_rows[0, :, lanes], (((1,), (1,)), ((), ())), preferred_element_type=jnp.float32
        ) * score_scale
        new_score = jnp.sum(jnp.where(pick, fresh_scores, 0.0), axis=1, keepdims=True)
        scores = jnp.where(inside, scores, NEGATIVE_FILL)
        top = jnp.maximum(jnp.max(scores, axis=1, keepdims=True), new_score)
        weights = jnp.where(inside, jnp.exp(scores - top), 0.0)
        new_weight = jnp.exp(new_score - top)
        denominator = jnp.sum(weights, axis=1, keepdims=True) + new_weight
        mixed = jnp.dot(weights.astype(jnp.bfloat16), values[:, lanes], preferred_element_type=jnp.float32)
        fresh_values = jnp.dot(pick.astype(jnp.bfloat16), fresh_rows[1, :, lanes], preferred_element_type=jnp.float32)
        mixed = mixed + new_weight.astype(jnp.bfloat16).astype(jnp.float32) * fresh_values
        results.append(mixed / denominator)
    pieces = [
        results[head][slot * group_width : (slot + 1) * group_width]
        for slot in range(slot_count)
        for head in range(kv_heads)
    ]
    out_ref[...] = jnp.concatenate(pieces, axis=0).astype(out_ref.dtype)
    for write in writes:
        write.wait()


def attend_kernel(lengths, query, key_value_fresh, kv_cache):
    slot_count = lengths.shape[0]
    kv_width = kv_cache.shape[2]
    kv_heads = kv_width // HEAD_SIZE
    group_width = QUERY_HEADS // KEY_VALUE_HEADS
    rows = kv_cache.shape[1]
    out, store = pl.pallas_call(
        attention_kernel,
        out_shape=(
            jax.ShapeDtypeStruct((slot_count * kv_heads * group_width, HEAD_SIZE), jnp.bfloat16),
            jax.ShapeDtypeStruct(kv_cache.shape, kv_cache.dtype),
        ),
        in_specs=[
            pl.BlockSpec(memory_space=pltpu.SMEM),
            pl.BlockSpec(memory_space=pltpu.VMEM),
            pl.BlockSpec(memory_space=pl.ANY),
            pl.BlockSpec(memory_space=pltpu.VMEM),
        ],
        out_specs=(pl.BlockSpec(memory_space=pltpu.VMEM), pl.BlockSpec(memory_space=pl.ANY)),
        scratch_shapes=[
            pltpu.VMEM((rows, kv_width), kv_cache.dtype),
            pltpu.VMEM((rows, kv_width), kv_cache.dtype),
            pltpu.SemaphoreType.DMA((2, rows // CHUNK_ROWS)),
            pltpu.SemaphoreType.DMA((2,)),
        ],
        cost_estimate=pl.CostEstimate(
            flops=4 * kv_heads * slot_count * group_width * rows * HEAD_SIZE,
            transcendentals=kv_heads * slot_count * group_width * rows,
            bytes_accessed=2 * rows * kv_width * 2,
        ),
    )(lengths, query, kv_cache, key_value_fresh)
    return store, out.reshape(slot_count, kv_heads * group_width * HEAD_SIZE)


def slot_bounds(lengths):
    span_sizes = lengths + 1
    first_rows = jnp.cumsum(span_sizes) - span_sizes
    return (first_rows, first_rows + span_sizes)


def attend_rows(query_rows, key_value_store, row_base, first_rows, end_rows):
    block_rows = 128
    slot_count, kv_heads, group_width, head_dim = query_rows.shape
    pool_rows = key_value_store.shape[1]
    key_table = key_value_store[0].reshape(pool_rows, kv_heads, head_dim)
    value_table = key_value_store[1].reshape(pool_rows, kv_heads, head_dim)
    needed = jnp.clip(jnp.max(end_rows) - row_base, 0, pool_rows)
    block_count = (needed + block_rows - 1) // block_rows
    score_scale = head_dim ** (-0.5)

    def advance(block_index, carried):
        running_max, denominator, accumulated = carried
        offset = block_index * block_rows
        key_block = lax.dynamic_slice_in_dim(key_table, offset, block_rows, 0)
        value_block = lax.dynamic_slice_in_dim(value_table, offset, block_rows, 0)
        scores = (
            jnp.einsum("sngd,tnd->sngt", query_rows, key_block, preferred_element_type=jnp.float32)
            * score_scale
        )
        row_ids = row_base + offset + jnp.arange(block_rows, dtype=jnp.int32)
        inside = (
            (row_ids[None, :] >= first_rows[:, None]) & (row_ids[None, :] < end_rows[:, None])
        )[:, None, None, :]
        scores = jnp.where(inside, scores, NEGATIVE_FILL)
        new_max = jnp.maximum(running_max, jnp.max(scores, axis=-1))
        weights = jnp.where(inside, jnp.exp(scores - new_max[..., None]), 0.0)
        factor = jnp.exp(running_max - new_max)
        denominator = denominator * factor + jnp.sum(weights, axis=-1)
        accumulated = accumulated * factor[..., None] + jnp.einsum(
            "sngt,tnd->sngd",
            weights.astype(jnp.bfloat16),
            value_block,
            preferred_element_type=jnp.float32,
        )
        return (new_max, denominator, accumulated)

    initial = (
        jnp.full((slot_count, kv_heads, group_width), NEGATIVE_FILL, jnp.float32),
        jnp.zeros((slot_count, kv_heads, group_width), jnp.float32),
        jnp.zeros((slot_count, kv_heads, group_width, head_dim), jnp.float32),
    )
    return lax.fori_loop(0, block_count, advance, initial)


def body(
    lengths,
    assignment,
    query,
    key_value_fresh,
    kv_cache,
    hidden_in,
    out_weight,
    norm_gain,
    gate_up_weight,
    down_weight,
):
    slot_count = lengths.shape[0]
    first_rows, end_rows = slot_bounds(lengths)
    key_value_store, attended = attend_kernel(lengths, query, key_value_fresh, kv_cache)
    y_count, mdl_count = lax.axis_size("y"), lax.axis_size("mdl")
    weight_copies = jnp.broadcast_to(out_weight.T[None], (y_count,) + out_weight.T.shape)
    row_weight = lax.all_to_all(weight_copies, "y", 0, 0, tiled=True).reshape(-1, out_weight.shape[0])
    flat = attended.reshape(-1, 128)
    flat = lax.all_gather(flat, "c", axis=0, tiled=True)
    flat = lax.all_gather(flat, "z", axis=0, tiled=True)
    row_attended = flat.reshape(-1, attended.shape[1])
    row_slots = row_attended.shape[0]
    sub_width = hidden_in.shape[1]
    row_projected = lax.dot_general(
        row_weight, row_attended, (((1,), (1,)), ((), ())), preferred_element_type=jnp.float32
    )
    outgoing = row_projected.astype(jnp.bfloat16).reshape(y_count * mdl_count, sub_width, row_slots)
    arrived = lax.all_to_all(outgoing, ("y", "mdl"), 0, 0, tiled=True)
    head_sum = arrived.astype(jnp.float32).reshape(y_count, mdl_count, sub_width, row_slots).sum(1)
    head_share = jnp.transpose(head_sum, (1, 0, 2)).reshape(sub_width, y_count * row_slots).T
    total_rows = assignment.shape[0]
    selection = (
        assignment[:, None] == lax.broadcasted_iota(jnp.int32, (total_rows, total_rows), 1)
    ).astype(jnp.float32)
    placed = lax.dot_general(
        selection,
        head_share,
        (((0,), (0,)), ((), ())),
        precision=lax.Precision.HIGHEST,
        preferred_element_type=jnp.float32,
    )
    residual_wide = hidden_in.astype(jnp.float32) + placed
    residual = residual_wide.astype(jnp.bfloat16)
    local_wide = residual.astype(jnp.float32)
    col_groups = gate_up_weight.shape[1]
    sub_width = hidden_in.shape[1]
    gathered = jnp.transpose(gather_rows(residual.T), (2, 0, 1)).reshape(total_rows, col_groups * sub_width)
    widened = gathered.astype(jnp.float32)
    own_squares = jnp.sum(widened * widened, axis=1)
    gain_table = norm_gain.reshape(col_groups, lax.axis_size("mdl"), sub_width)
    gain_cols = lax.dynamic_index_in_dim(
        gain_table, lax.axis_index("mdl"), 1, keepdims=False
    ).reshape(col_groups * sub_width)
    unscaled = (widened * gain_cols).astype(jnp.bfloat16)
    gate_up = gate_up_weight.reshape(2, col_groups * sub_width, gate_up_weight.shape[4])
    partial_value = jnp.einsum("rk,gkf->gfr", unscaled, gate_up, preferred_element_type=jnp.float32)
    units = partial_value.shape[1]
    mdl_count = lax.axis_size("mdl")
    quarter = units // mdl_count
    squares_high = own_squares.astype(jnp.bfloat16)
    squares_low = (own_squares - squares_high.astype(jnp.float32)).astype(jnp.bfloat16)
    squares_pair = jnp.broadcast_to(jnp.stack([squares_high, squares_low])[None], (mdl_count, 2, total_rows))
    blocks = jnp.transpose(
        partial_value.astype(jnp.bfloat16).reshape(2, mdl_count, quarter, total_rows), (1, 0, 2, 3)
    ).reshape(mdl_count, 2 * quarter, total_rows)
    payload = jnp.concatenate([blocks, squares_pair], axis=1)
    summed_payload = lax.all_to_all(payload, "mdl", 0, 0, tiled=True).astype(jnp.float32).sum(0)
    square_sum = summed_payload[2 * quarter] + summed_payload[2 * quarter + 1]
    scale = lax.rsqrt(square_sum / D + 1e-05)
    gate_part = summed_payload[:quarter] * scale[None, :]
    up_part = summed_payload[quarter : 2 * quarter] * scale[None, :]
    hidden_part = (jax.nn.silu(gate_part) * up_part).astype(jnp.bfloat16)
    hidden_copies = jnp.broadcast_to(hidden_part[None], (mdl_count,) + hidden_part.shape)
    hidden = lax.all_to_all(hidden_copies, "mdl", 0, 0, tiled=True).reshape(units, total_rows)
    columns = down_weight.reshape(down_weight.shape[0], col_groups * sub_width)
    lowered = lax.dot_general(
        columns, hidden, (((0,), (0,)), ((), ())), preferred_element_type=jnp.float32
    )
    mesh_shape = (lax.axis_size("y"), lax.axis_size("z"), lax.axis_size("c"))
    summed = scatter_sum(lowered.reshape(mesh_shape + (sub_width * total_rows // 128, 128))).reshape(sub_width, total_rows)
    layer_out = (local_wide + summed.T).astype(jnp.bfloat16)
    return (layer_out, key_value_store)


def solution(mesh):
    req_size, mdl_size = mesh.devices.shape
    chips_y = 4
    split = Mesh(
        mesh.devices.reshape(chips_y, req_size // (2 * chips_y), 2, mdl_size),
        REQ + ("mdl",),
    )
    return jax.shard_map(
        body,
        mesh=split,
        in_specs=(
            P(REQ),
            P(),
            P(REQ, "mdl"),
            P(None, REQ, "mdl"),
            P(None, REQ, "mdl"),
            P(None, (REQ + ("mdl",))),
            P("mdl", REQ),
            P(),
            P(None, None, "mdl", None, REQ),
            P(REQ, None, "mdl", None),
        ),
        out_specs=(P(None, REQ + ("mdl",)), P(None, REQ, "mdl")),
        check_vma=False,
    )
```

```python
import jax
import jax.numpy as jnp
from jax import lax
from jax.experimental import pallas as pl
from jax.experimental.pallas import tpu as pltpu
from jax.sharding import Mesh, PartitionSpec as P

D = 5120
QUERY_HEADS = 32
KEY_VALUE_HEADS = 8
HEAD_SIZE = 128


NEGATIVE_FILL = -1e30
REQ = ("y", "z", "c")


def gather_rows(part):
    count = lax.axis_size(REQ)
    flat = part.reshape(-1, 128)
    flat = lax.all_gather(flat, "c", axis=0, tiled=True)
    flat = lax.all_gather(flat, "z", axis=0, tiled=True)
    copies = jnp.broadcast_to(flat[None], (lax.axis_size("y"),) + flat.shape)
    return lax.all_to_all(copies, "y", 0, 0, tiled=True).reshape((count,) + part.shape)


def scatter_sum(parts):
    wide = None
    for position, name in ((2, "c"), (0, "y"), (1, "z")):
        moved = lax.all_to_all(parts.astype(jnp.bfloat16), name, position, position, tiled=True)
        wide = moved.astype(jnp.float32).sum(position, keepdims=True)
        parts = wide
    return wide


def mdl_sum(values, wires):
    count = lax.axis_size("mdl")
    sent = tuple(v.astype(w) for v, w in zip(values, wires))
    totals = [v.astype(jnp.float32) for v in values]
    for shift in range(1, count):
        pairs = [(i, (i + shift) % count) for i in range(count)]
        arrived = lax.ppermute(sent, "mdl", pairs)
        totals = [t + a.astype(jnp.float32) for t, a in zip(totals, arrived)]
    return totals


def mdl_scatter_sum(value, wire):
    count = lax.axis_size("mdl")
    height = value.shape[0] // count
    blocks = value.astype(wire).reshape((count, height * value.shape[1] // 128, 128))
    moved = lax.all_to_all(blocks, "mdl", 0, 0, tiled=True)
    return moved.astype(jnp.float32).sum(0).reshape(height, value.shape[1])


CHUNK_ROWS = 1024


def attention_kernel(
    lengths_ref, query_ref, cache_hbm, fresh_rows, out_ref, store_hbm, keys, values, sems, write_sems
):
    rows = keys.shape[0]
    chunks = rows // CHUNK_ROWS
    copies = []
    for chunk in range(chunks):
        window = pl.ds(chunk * CHUNK_ROWS, CHUNK_ROWS)
        for which, target in ((0, keys), (1, values)):
            copy = pltpu.make_async_copy(cache_hbm.at[which, window], target.at[window], sems.at[which, chunk])
            copy.start()
            copies.append(copy)
    slot_count = lengths_ref.shape[0]
    head_dim = HEAD_SIZE
    kv_heads = keys.shape[1] // head_dim
    row_count = query_ref.shape[1] // kv_heads // head_dim * slot_count
    group_width = row_count // slot_count
    row_slot = lax.broadcasted_iota(jnp.int32, (row_count, 1), 0) // group_width
    first = jnp.zeros((row_count, 1), jnp.int32)
    end = jnp.zeros((row_count, 1), jnp.int32)
    start = jnp.int32(0)
    for slot in range(slot_count):
        length = lengths_ref[slot]
        first = jnp.where(row_slot == slot, start, first)
        end = jnp.where(row_slot == slot, start + length, end)
        start = start + length + 1
    columns = lax.broadcasted_iota(jnp.int32, (row_count, rows), 1)
    inside = (columns >= first) & (columns < end)
    pick = (lax.broadcasted_iota(jnp.int32, (row_count, slot_count), 1) == row_slot)
    for copy in copies:
        copy.wait()
    tile = 16
    within = lax.broadcasted_iota(jnp.int32, (tile, keys.shape[1]), 0)
    start = jnp.int32(0)
    for slot in range(slot_count):
        row = start + lengths_ref[slot]
        base = pl.multiple_of((row // tile) * tile, tile)
        for which, target in ((0, keys), (1, values)):
            block = target[pl.ds(base, tile), :]
            fresh_row = jnp.broadcast_to(fresh_rows[which, pl.ds(slot, 1), :], block.shape)
            target[pl.ds(base, tile), :] = jnp.where(within == row - base, fresh_row, block)
        start = row + 1
    writes = []
    for which, source in ((0, keys), (1, values)):
        write = pltpu.make_async_copy(source, store_hbm.at[which], write_sems.at[which])
        write.start()
        writes.append(write)
    score_scale = head_dim ** (-0.5)
    results = []
    wide_query = query_ref[...].astype(jnp.float32)
    for head in range(kv_heads):
        lanes = pl.ds(head * head_dim, head_dim)
        query_rows = jnp.concatenate(
            [
                wide_query[slot : slot + 1, (head * group_width + g) * head_dim : (head * group_width + g + 1) * head_dim]
                for slot in range(slot_count)
                for g in range(group_width)
            ],
            axis=0,
        ).astype(query_ref.dtype)
        scores = lax.dot_general(
            query_rows, keys[:, lanes], (((1,), (1,)), ((), ())), preferred_element_type=jnp.float32
        ) * score_scale
        fresh_scores = lax.dot_general(
            query_rows, fresh_rows[0, :, lanes], (((1,), (1,)), ((), ())), preferred_element_type=jnp.float32
        ) * score_scale
        new_score = jnp.sum(jnp.where(pick, fresh_scores, 0.0), axis=1, keepdims=True)
        scores = jnp.where(inside, scores, NEGATIVE_FILL)
        top = jnp.maximum(jnp.max(scores, axis=1, keepdims=True), new_score)
        weights = jnp.where(inside, jnp.exp(scores - top), 0.0)
        new_weight = jnp.exp(new_score - top)
        denominator = jnp.sum(weights, axis=1, keepdims=True) + new_weight
        mixed = jnp.dot(weights.astype(jnp.bfloat16), values[:, lanes], preferred_element_type=jnp.float32)
        fresh_values = jnp.dot(pick.astype(jnp.bfloat16), fresh_rows[1, :, lanes], preferred_element_type=jnp.float32)
        mixed = mixed + new_weight.astype(jnp.bfloat16).astype(jnp.float32) * fresh_values
        results.append(mixed / denominator)
    pieces = [
        results[head][slot * group_width : (slot + 1) * group_width]
        for slot in range(slot_count)
        for head in range(kv_heads)
    ]
    out_ref[...] = jnp.concatenate(pieces, axis=0).astype(out_ref.dtype)
    for write in writes:
        write.wait()


def attend_kernel(lengths, query, key_value_fresh, kv_cache):
    slot_count = lengths.shape[0]
    kv_width = kv_cache.shape[2]
    kv_heads = kv_width // HEAD_SIZE
    group_width = QUERY_HEADS // KEY_VALUE_HEADS
    rows = kv_cache.shape[1]
    out, store = pl.pallas_call(
        attention_kernel,
        out_shape=(
            jax.ShapeDtypeStruct((slot_count * kv_heads * group_width, HEAD_SIZE), jnp.bfloat16),
            jax.ShapeDtypeStruct(kv_cache.shape, kv_cache.dtype),
        ),
        in_specs=[
            pl.BlockSpec(memory_space=pltpu.SMEM),
            pl.BlockSpec(memory_space=pltpu.VMEM),
            pl.BlockSpec(memory_space=pl.ANY),
            pl.BlockSpec(memory_space=pltpu.VMEM),
        ],
        out_specs=(pl.BlockSpec(memory_space=pltpu.VMEM), pl.BlockSpec(memory_space=pl.ANY)),
        scratch_shapes=[
            pltpu.VMEM((rows, kv_width), kv_cache.dtype),
            pltpu.VMEM((rows, kv_width), kv_cache.dtype),
            pltpu.SemaphoreType.DMA((2, rows // CHUNK_ROWS)),
            pltpu.SemaphoreType.DMA((2,)),
        ],
        cost_estimate=pl.CostEstimate(
            flops=4 * kv_heads * slot_count * group_width * rows * HEAD_SIZE,
            transcendentals=kv_heads * slot_count * group_width * rows,
            bytes_accessed=2 * rows * kv_width * 2,
        ),
    )(lengths, query, kv_cache, key_value_fresh)
    return store, out.reshape(slot_count, kv_heads * group_width * HEAD_SIZE)


def slot_bounds(lengths):
    span_sizes = lengths + 1
    first_rows = jnp.cumsum(span_sizes) - span_sizes
    return (first_rows, first_rows + span_sizes)


def attend_rows(query_rows, key_value_store, row_base, first_rows, end_rows):
    block_rows = 128
    slot_count, kv_heads, group_width, head_dim = query_rows.shape
    pool_rows = key_value_store.shape[1]
    key_table = key_value_store[0].reshape(pool_rows, kv_heads, head_dim)
    value_table = key_value_store[1].reshape(pool_rows, kv_heads, head_dim)
    needed = jnp.clip(jnp.max(end_rows) - row_base, 0, pool_rows)
    block_count = (needed + block_rows - 1) // block_rows
    score_scale = head_dim ** (-0.5)

    def advance(block_index, carried):
        running_max, denominator, accumulated = carried
        offset = block_index * block_rows
        key_block = lax.dynamic_slice_in_dim(key_table, offset, block_rows, 0)
        value_block = lax.dynamic_slice_in_dim(value_table, offset, block_rows, 0)
        scores = (
            jnp.einsum("sngd,tnd->sngt", query_rows, key_block, preferred_element_type=jnp.float32)
            * score_scale
        )
        row_ids = row_base + offset + jnp.arange(block_rows, dtype=jnp.int32)
        inside = (
            (row_ids[None, :] >= first_rows[:, None]) & (row_ids[None, :] < end_rows[:, None])
        )[:, None, None, :]
        scores = jnp.where(inside, scores, NEGATIVE_FILL)
        new_max = jnp.maximum(running_max, jnp.max(scores, axis=-1))
        weights = jnp.where(inside, jnp.exp(scores - new_max[..., None]), 0.0)
        factor = jnp.exp(running_max - new_max)
        denominator = denominator * factor + jnp.sum(weights, axis=-1)
        accumulated = accumulated * factor[..., None] + jnp.einsum(
            "sngt,tnd->sngd",
            weights.astype(jnp.bfloat16),
            value_block,
            preferred_element_type=jnp.float32,
        )
        return (new_max, denominator, accumulated)

    initial = (
        jnp.full((slot_count, kv_heads, group_width), NEGATIVE_FILL, jnp.float32),
        jnp.zeros((slot_count, kv_heads, group_width), jnp.float32),
        jnp.zeros((slot_count, kv_heads, group_width, head_dim), jnp.float32),
    )
    return lax.fori_loop(0, block_count, advance, initial)


def body(
    lengths,
    assignment,
    query,
    key_value_fresh,
    kv_cache,
    hidden_in,
    out_weight,
    norm_gain,
    gate_up_weight,
    down_weight,
):
    slot_count = lengths.shape[0]
    first_rows, end_rows = slot_bounds(lengths)
    key_value_store, attended = attend_kernel(lengths, query, key_value_fresh, kv_cache)
    y_count, mdl_count = lax.axis_size("y"), lax.axis_size("mdl")
    weight_copies = jnp.broadcast_to(out_weight.T[None], (y_count,) + out_weight.T.shape)
    row_weight = lax.all_to_all(weight_copies, "y", 0, 0, tiled=True).reshape(-1, out_weight.shape[0])
    flat = attended.reshape(-1, 128)
    flat = lax.all_gather(flat, "c", axis=0, tiled=True)
    flat = lax.all_gather(flat, "z", axis=0, tiled=True)
    row_attended = flat.reshape(-1, attended.shape[1])
    row_slots = row_attended.shape[0]
    sub_width = hidden_in.shape[1]
    row_projected = lax.dot_general(
        row_weight, row_attended, (((1,), (1,)), ((), ())), preferred_element_type=jnp.float32
    )
    outgoing = row_projected.astype(jnp.bfloat16).reshape(y_count * mdl_count, sub_width, row_slots)
    arrived = lax.all_to_all(outgoing, ("y", "mdl"), 0, 0, tiled=True)
    head_sum = arrived.astype(jnp.float32).reshape(y_count, mdl_count, sub_width, row_slots).sum(1)
    head_share = jnp.transpose(head_sum, (1, 0, 2)).reshape(sub_width, y_count * row_slots).T
    total_rows = assignment.shape[0]
    selection = (
        assignment[:, None] == lax.broadcasted_iota(jnp.int32, (total_rows, total_rows), 1)
    ).astype(jnp.float32)
    placed = lax.dot_general(
        selection,
        head_share,
        (((0,), (0,)), ((), ())),
        precision=lax.Precision.HIGHEST,
        preferred_element_type=jnp.float32,
    )
    residual_wide = hidden_in.astype(jnp.float32) + placed
    residual = residual_wide.astype(jnp.bfloat16)
    local_wide = residual.astype(jnp.float32)
    col_groups = gate_up_weight.shape[1]
    sub_width = hidden_in.shape[1]
    gathered = jnp.transpose(gather_rows(residual.T), (2, 0, 1)).reshape(total_rows, col_groups * sub_width)
    widened = gathered.astype(jnp.float32)
    own_squares = jnp.sum(widened * widened, axis=1)
    gain_table = norm_gain.reshape(col_groups, lax.axis_size("mdl"), sub_width)
    gain_cols = lax.dynamic_index_in_dim(
        gain_table, lax.axis_index("mdl"), 1, keepdims=False
    ).reshape(col_groups * sub_width)
    unscaled = (widened * gain_cols).astype(jnp.bfloat16)
    gate_up = gate_up_weight.reshape(2, col_groups * sub_width, gate_up_weight.shape[4])
    partial_value = jnp.einsum("rk,gkf->gfr", unscaled, gate_up, preferred_element_type=jnp.float32)
    units = partial_value.shape[1]
    mdl_count = lax.axis_size("mdl")
    quarter = units // mdl_count
    squares_high = own_squares.astype(jnp.bfloat16)
    squares_low = (own_squares - squares_high.astype(jnp.float32)).astype(jnp.bfloat16)
    squares_pair = jnp.broadcast_to(jnp.stack([squares_high, squares_low])[None], (mdl_count, 2, total_rows))
    blocks = jnp.transpose(
        partial_value.astype(jnp.bfloat16).reshape(2, mdl_count, quarter, total_rows), (1, 0, 2, 3)
    ).reshape(mdl_count, 2 * quarter, total_rows)
    payload = jnp.concatenate([blocks, squares_pair], axis=1)
    summed_payload = lax.all_to_all(payload, "mdl", 0, 0, tiled=True).astype(jnp.float32).sum(0)
    square_sum = summed_payload[2 * quarter] + summed_payload[2 * quarter + 1]
    scale = lax.rsqrt(square_sum / D + 1e-05)
    gate_part = summed_payload[:quarter] * scale[None, :]
    up_part = summed_payload[quarter : 2 * quarter] * scale[None, :]
    hidden_part = (jax.nn.silu(gate_part) * up_part).astype(jnp.bfloat16)
    hidden_copies = jnp.broadcast_to(hidden_part[None], (mdl_count,) + hidden_part.shape)
    hidden = lax.all_to_all(hidden_copies, "mdl", 0, 0, tiled=True).reshape(units, total_rows)
    columns = down_weight.reshape(down_weight.shape[0], col_groups * sub_width)
    lowered = lax.dot_general(
        columns, hidden, (((0,), (0,)), ((), ())), preferred_element_type=jnp.float32
    )
    mesh_shape = (lax.axis_size("y"), lax.axis_size("z"), lax.axis_size("c"))
    summed = scatter_sum(lowered.reshape(mesh_shape + (sub_width * total_rows // 128, 128))).reshape(sub_width, total_rows)
    layer_out = (local_wide + summed.T).astype(jnp.bfloat16)
    return (layer_out, key_value_store)


def solution(mesh):
    req_size, mdl_size = mesh.devices.shape
    chips_y = 4
    split = Mesh(
        mesh.devices.reshape(chips_y, req_size // (2 * chips_y), 2, mdl_size),
        REQ + ("mdl",),
    )
    return jax.shard_map(
        body,
        mesh=split,
        in_specs=(
            P(REQ),
            P(),
            P(REQ, "mdl"),
            P(None, REQ, "mdl"),
            P(None, REQ, "mdl"),
            P(None, (REQ + ("mdl",))),
            P("mdl", REQ),
            P(),
            P(None, None, "mdl", None, REQ),
            P(REQ, None, "mdl", None),
        ),
        out_specs=(P(None, REQ + ("mdl",)), P(None, REQ, "mdl")),
        check_vma=False,
    )
```
